128 devices in a mesh: section: 2 (over core), seq: 4 (over z), shard: 16 (over x, y).
Axes of the slice: x: 4, y: 4, z: 4, core: 2. Of those that a mesh axis runs over, the one named last changes fastest.
Arguments:
- ends: bfloat16 [2, 16, 4, 256, 768], P('section', 'shard', None, 'seq'), may hold values from -6 to 6
- w_qkv: bfloat16 [2, 768, 2304], P('section', ('seq', 'shard')), may hold values from -0.21875 to 0.21875
- w_out: bfloat16 [2, 768, 768], P('section', ('seq', 'shard')), may hold values from -1.25 to 1.25
- w_up: bfloat16 [2, 768, 3072], P('section', ('seq', 'shard')), may hold values from -0.21875 to 0.21875
- w_down: bfloat16 [2, 3072, 768], P('section', ('seq', 'shard')), may hold values from -0.109375 to 0.109375
- norm_gains: bfloat16 [2, 2, 768], P('section', None, ('seq', 'shard')), may hold values from 0.25 to 1.75
- biases: bfloat16 [2, 6, 768], P('section', None, ('seq', 'shard')), may hold values from -3 to 3
- up_bias: bfloat16 [2, 3072], P('section', ('seq', 'shard')), may hold values from -3 to 3
Outputs:
- boundary: bfloat16 [2, 16, 4, 256, 768], P('section', 'shard', None, 'seq')
- grad_qkv: float32 [2, 768, 2304], P('section', ('seq', 'shard'))
- grad_out: float32 [2, 768, 768], P('section', ('seq', 'shard'))
- grad_up: float32 [2, 768, 3072], P('section', ('seq', 'shard'))
- grad_down: float32 [2, 3072, 768], P('section', ('seq', 'shard'))
- grad_gains: float32 [2, 2, 768], P('section', None, ('seq', 'shard'))
- grad_biases: float32 [2, 6, 768], P('section', None, ('seq', 'shard'))
- grad_up_bias: float32 [2, 3072], P('section', ('seq', 'shard'))
The draws below stay inside these ranges and needn't reach their ends.
All inputs are finite; a program needn't handle non-finite values.
Results may differ from the reference program's by a relative error of at most 0.015.
Values may be sent and summed in bfloat16 or wider, within the bound.
A program may use at most 320 MiB of HBM per device.

```python
import jax
import jax.numpy as jnp
from jax import lax

D = 768
HEADS = 12
HEAD = 64
FF = 3072
GROUP = 256
GROUPS = 4
SEQS = 16
N_SECTION = 2


def levels(key, shape, cuts, least, top_value):
    def one(axis_at, parts):
        steps = jax.random.uniform(jax.random.fold_in(jax.random.fold_in(key, 6), axis_at), (parts,), jnp.float32, least / len(cuts), top_value / len(cuts))
        return jnp.repeat(jnp.exp(steps), shape[axis_at] // parts).reshape((-1,) + (1,) * (len(shape) - axis_at - 1))

    loudness = one(*cuts[0])
    for cut in cuts[1:]:
        loudness = loudness * one(*cut)
    return loudness


def noise(stream_key, shape, deviation, most, cuts=(), kind=jnp.bfloat16):
    factor_of = levels(stream_key, shape, cuts, -0.22, 0.18) if cuts else 1.0
    array = jax.random.normal(stream_key, shape, jnp.float32) * deviation * factor_of
    return jnp.minimum(jnp.maximum(array, -most), most).astype(kind)


def setup_inputs(seed: int = 0) -> dict:
    key_list = jax.random.split(jax.random.key(seed), 9)
    ends = noise(key_list[0], (N_SECTION, SEQS, GROUPS, GROUP, D), 1.0, 6.0, ((0, 2), (1, 16), (3, 4)))
    w_qkv = noise(key_list[1], (N_SECTION, D, 3 * D), D ** -0.5, 0.21875, ((0, 2), (1, 64)))
    w_out = noise(key_list[2], (N_SECTION, D, D), (D // 32) ** -0.5, 1.25, ((0, 2), (1, 64)))
    w_up = noise(key_list[3], (N_SECTION, D, FF), D ** -0.5, 0.21875, ((0, 2), (1, 64)))
    w_down = noise(key_list[4], (N_SECTION, FF, D), FF ** -0.5, 0.109375, ((0, 2), (1, 64)))
    norm_gains = jnp.clip(1.0 + 0.15 * jax.random.normal(key_list[5], (N_SECTION, 2, D), jnp.float32), 0.25, 1.75).astype(jnp.bfloat16)
    biases = noise(key_list[6], (N_SECTION, 6, D), 0.5, 3.0, ((0, 2), (2, 64)))
    up_bias = noise(key_list[7], (N_SECTION, FF), 0.5, 3.0, ((0, 2), (1, 64)))
    return {"ends": ends, "w_qkv": w_qkv, "w_out": w_out, "w_up": w_up, "w_down": w_down, "norm_gains": norm_gains, "biases": biases, "up_bias": up_bias}


@jax.custom_vjp
def low(v):
    return lax.optimization_barrier(v.astype(jnp.bfloat16)).astype(jnp.float32)

@jax.custom_vjp
def low_back(v):
    return v

def low_keep(v):
    return (low(v), None)

def low_pass(kept, grad):
    return (grad,)

def back_keep(v):
    return (v, None)

def back_low(kept, grad):
    return (low(grad),)
low.defvjp(low_keep, low_pass)
low_back.defvjp(back_keep, back_low)
EPSILON = 1e-05
MASKED = -1e+30
HIGHEST = lax.Precision.HIGHEST

def layer_norm(values, gain, shift):
    centre = lax.optimization_barrier(jnp.mean(values, axis=-1, keepdims=True))
    centered = values - centre
    spread = lax.optimization_barrier(jnp.mean(centered * centered, axis=-1, keepdims=True))
    return centered * lax.rsqrt(spread + EPSILON) * gain + shift

def attention(queries, key_heads, value_heads):
    length = queries.shape[0]
    block_rows = min(length, 512)
    scaling = HEAD ** (-0.5)
    blocked = queries.reshape(length // block_rows, block_rows, HEADS, HEAD)
    starts = jnp.arange(length // block_rows, dtype=jnp.int32) * block_rows

    def one_block(packed):
        block_queries, first_row = packed
        product = jnp.einsum('qhd,khd->hqk', block_queries, key_heads, precision=HIGHEST)
        scores = low_back(product * scaling)
        row_pos = first_row + lax.broadcasted_iota(jnp.int32, (block_rows, length), 0)
        col_pos = lax.broadcasted_iota(jnp.int32, (block_rows, length), 1)
        scores = jnp.where((col_pos <= row_pos)[None], scores, MASKED)
        chances = low(jax.nn.softmax(scores, axis=-1))
        return jnp.einsum('hqk,khd->qhd', chances, value_heads, precision=HIGHEST)
    mixed = lax.map(jax.checkpoint(one_block), (blocked, starts))
    return mixed.reshape(length, HEADS * HEAD)

def block(hidden, w_qkv, w_out, w_up, w_down, gains, shifts, up_bias):
    normed = low(layer_norm(hidden, gains[0], shifts[0]))
    qkv_bias = jnp.concatenate([shifts[2], jnp.zeros_like(shifts[2]), shifts[3]])
    projected = low(low_back(jnp.dot(normed, w_qkv, precision=HIGHEST) + qkv_bias))
    length = hidden.shape[0]
    split = projected.reshape(length, 3, HEADS, HEAD)
    mixed = low(low_back(attention(split[:, 0], split[:, 1], split[:, 2])))
    middle = hidden + low_back(jnp.dot(mixed, w_out, precision=HIGHEST) + shifts[4])
    normed_two = low(layer_norm(middle, gains[1], shifts[1]))
    raised = low_back(jnp.dot(normed_two, w_up, precision=HIGHEST) + up_bias)
    active = low(jax.nn.gelu(raised, approximate=True))
    return middle + low_back(jnp.dot(active, w_down, precision=HIGHEST) + shifts[5])

def network(hidden, params):
    for layer_index in range(2):
        layer = tuple((item[layer_index] for item in params))
        hidden = block(hidden, *layer)
        if layer_index == 0:
            hidden = low(low_back(hidden))
    return hidden

def reference(ends, w_qkv, w_out, w_up, w_down, norm_gains, biases, up_bias):
    params = tuple((item.astype(jnp.float32) for item in (w_qkv, w_out, w_up, w_down, norm_gains, biases, up_bias)))
    seq_count = ends.shape[1]
    width = ends.shape[-1]
    length = GROUPS * GROUP
    inputs = ends[0].astype(jnp.float32).reshape(seq_count, length, width)
    cotangent = ends[1].astype(jnp.float32).reshape(seq_count, length, width)

    def one_sequence(totals, packed):
        result, pullback = jax.vjp(network, packed[0], params)
        grad_in, grad_params = pullback(packed[1])
        totals = tuple((total + addend for total, addend in zip(totals, grad_params)))
        return (totals, (result, grad_in))
    zeros = tuple((jnp.zeros(item.shape, jnp.float32) for item in params))
    grads, (results, grad_inputs) = lax.scan(one_sequence, zeros, (inputs, cotangent))
    boundary = jnp.stack([grad_inputs, results]).reshape(2, seq_count, GROUPS, GROUP, width).astype(jnp.bfloat16)
    return (boundary, grads[0], grads[1], grads[2], grads[3], grads[4], grads[5], grads[6])
```

```python
import functools

import jax
import jax.numpy as jnp
from jax import lax
from jax.experimental import pallas as pl
from jax.experimental.pallas import tpu as pltpu
from jax.sharding import PartitionSpec as P

HEAD = 64
FF = 3072
D = 768
GROUPS = 4
ROWS = 64
TOK = GROUPS * ROWS
SEQ_LEN = 1024
HL = 192
EPSILON = 1e-05
MASKED = -1e30
BF = jnp.bfloat16
F32 = jnp.float32
MESH = pl.DeviceIdType.MESH
HBM = pltpu.HBM


def sds(shape, dtype):
    return jax.ShapeDtypeStruct(shape, dtype)


def coords():
    shard = lax.axis_index("shard")
    return {"x": shard // 4, "y": lax.rem(shard, 4), "z": lax.axis_index("seq")}


def peer(c, axis, by):
    moved = dict(c)
    moved[axis] = lax.rem(c[axis] + by, 4)
    return {"section": lax.axis_index("section"), "seq": moved["z"], "shard": moved["x"] * 4 + moved["y"]}


def meet(c, axes, steps):
    barrier = pltpu.get_barrier_semaphore()
    for axis in axes:
        for by in steps:
            pl.semaphore_signal(barrier, inc=1, device_id=peer(c, axis, by), device_id_type=MESH)
    pl.semaphore_wait(barrier, len(axes) * len(steps))


class Copies:
    def __init__(self, send, recv):
        self.send, self.recv, self.used, self.sent = send, recv, 0, []

    def remote(self, src, dst, to):
        copy = pltpu.make_async_remote_copy(
            src_ref=src,
            dst_ref=dst,
            send_sem=self.send.at[self.used],
            recv_sem=self.recv.at[self.used],
            device_id=to,
            device_id_type=MESH,
        )
        self.used += 1
        copy.start()
        self.sent.append(copy)
        return copy

    def local(self, src, dst):
        copy = pltpu.make_async_copy(src, dst, self.send.at[self.used])
        self.used += 1
        copy.start()
        return copy

    def drain(self):
        for copy in self.sent:
            copy.wait_send()


class Gather:
    def __init__(self, copies, c, axis, own, dst, half):
        self.copies, self.c, self.axis, self.own, self.dst, self.half = copies, c, axis, own, dst, half

    def first(self):
        a = self.c[self.axis]
        self.right, self.left = peer(self.c, self.axis, 1), peer(self.c, self.axis, 3)
        self.go_right = self.copies.remote(self.own, self.dst(a), self.right)
        self.go_left = self.copies.remote(self.own, self.dst(a), self.left)

    def second(self):
        a = self.c[self.axis]
        before, after = lax.rem(a + 3, 4), lax.rem(a + 1, 4)
        self.go_right.wait_recv()
        self.on_right = self.copies.remote(self.half(before, 0), self.half(before, 0), self.right)
        self.go_left.wait_recv()
        self.on_left = self.copies.remote(self.half(after, 1), self.half(after, 1), self.left)

    def third(self):
        self.on_right.wait_recv()
        self.on_left.wait_recv()


def run_gathers(gathers):
    for g in gathers:
        g.first()
    for g in gathers:
        g.second()


def comm_call(body, live, axes, steps, count, ins, out_shapes, collective_id, aliases=None):
    n_in, n_out = len(ins), len(out_shapes)

    def kernel(*refs):
        in_refs, out_refs = refs[:n_in], refs[n_in : n_in + n_out]
        send, recv = refs[n_in + n_out :]

        def act():
            c = coords()
            meet(c, axes, steps)
            body(Copies(send, recv), c, in_refs, out_refs)

        if live is None:
            act()
        else:
            pl.when(lax.axis_index("section") == live)(act)

    return pl.pallas_call(
        kernel,
        out_shape=tuple(out_shapes),
        in_specs=[pl.BlockSpec(memory_space=HBM)] * n_in,
        out_specs=tuple([pl.BlockSpec(memory_space=HBM)] * n_out),
        scratch_shapes=[pltpu.SemaphoreType.DMA((count,)), pltpu.SemaphoreType.DMA((count,))],
        input_output_aliases=aliases or {},
        compiler_params=pltpu.CompilerParams(collective_id=collective_id, has_side_effects=True),
    )(*ins)


def gather_first(qkv, out, up, down, small):
    def body(copies, c, ins, outs):
        y, x = c["y"], c["x"]
        q_in, o_in, u_in, d_in, s_in = ins
        q_y, o_y, u_y, d_x, s_x = outs
        gathers = [
            Gather(copies, c, "y", u_in, lambda i: u_y.at[i], lambda i, h: u_y.at[i, :, pl.ds(1536 * h, 1536)]),
            Gather(copies, c, "y", q_in, lambda i: q_y.at[i], lambda i, h: q_y.at[i, pl.ds(2 * h, 2)]),
            Gather(copies, c, "y", o_in, lambda i: o_y.at[i], lambda i, h: o_y.at[i, :, pl.ds(384 * h, 384)]),
            Gather(copies, c, "x", d_in, lambda i: d_x.at[i], lambda i, h: d_x.at[i, :, pl.ds(384 * h, 384)]),
            Gather(copies, c, "x", s_in, lambda i: s_x.at[i], lambda i, h: s_x.at[i, h]),
        ]
        own = [
            copies.local(u_in, u_y.at[y]),
            copies.local(q_in, q_y.at[y]),
            copies.local(o_in, o_y.at[y]),
            copies.local(d_in, d_x.at[x]),
            copies.local(s_in, s_x.at[x]),
        ]
        run_gathers(gathers)
        for g in gathers:
            g.third()
        for copy in own:
            copy.wait()
        copies.drain()

    shapes = (
        sds((4, 4, 12, 576), BF),
        sds((4, 12, D), BF),
        sds((4, 12, FF), BF),
        sds((4, 48, D), BF),
        sds((4, 2, 8, 128), F32),
    )
    return comm_call(body, None, ("x", "y"), (1, 3), 25, (qkv, out, up, down, small), shapes, 0)


def gather_rest(live, qkv, out, up, down, small, previous, collective_id):
    def body(copies, c, ins, outs):
        x, y, z = c["x"], c["y"], c["z"]
        q_in, o_in, u_in, d_in, s_in = ins[:5]
        q, o, u, d, s = outs
        one = [
            Gather(copies, c, "z", q_in, lambda i: q.at[:, i, x], lambda i, h: q.at[pl.ds(2 * h, 2), i, x]),
            Gather(copies, c, "z", o_in, lambda i: o.at[i, x], lambda i, h: o.at[i, x, :, pl.ds(384 * h, 384)]),
            Gather(copies, c, "x", u_in, lambda i: u.at[z, i], lambda i, h: u.at[z, i, :, pl.ds(1536 * h, 1536)]),
            Gather(copies, c, "z", d_in, lambda i: d.at[i, :, y], lambda i, h: d.at[i, pl.ds(2 * h, 2), y]),
            Gather(copies, c, "z", s_in, lambda i: s.at[i, :, y], lambda i, h: s.at[i, pl.ds(2 * h, 2), y]),
        ]
        own = [
            copies.local(q_in, q.at[:, z, x]),
            copies.local(o_in, o.at[z, x]),
            copies.local(u_in, u.at[z, x]),
            copies.local(d_in, d.at[z, :, y]),
            copies.local(s_in, s.at[z, :, y]),
        ]
        run_gathers(one)
        two = [
            Gather(copies, c, "x", q.at[:, :, x], lambda i: q.at[:, :, i], lambda i, h: q.at[pl.ds(2 * h, 2), :, i]),
            Gather(copies, c, "x", o.at[:, x], lambda i: o.at[:, i], lambda i, h: o.at[pl.ds(2 * h, 2), i]),
            Gather(copies, c, "z", u.at[z], lambda i: u.at[i], lambda i, h: u.at[i, pl.ds(2 * h, 2)]),
            Gather(copies, c, "y", d.at[:, :, y], lambda i: d.at[:, :, i], lambda i, h: d.at[pl.ds(2 * h, 2), :, i]),
            Gather(copies, c, "y", s.at[:, :, y], lambda i: s.at[:, :, i], lambda i, h: s.at[pl.ds(2 * h, 2), :, i]),
        ]
        for k in range(5):
            one[k].third()
            own[k].wait()
            two[k].first()
        for g in two:
            g.second()
        for g in two:
            g.third()
        copies.drain()

    shapes = (
        sds((4, 4, 4, 48, 576), BF),
        sds((4, 4, 48, D), BF),
        sds((4, 4, 48, FF), BF),
        sds((4, 4, 4, 48, D), BF),
        sds((4, 4, 4, 2, 8, 128), F32),
    )
    ins = (qkv, out, up, down, small)
    aliases = None
    if previous is not None:
        ins = ins + tuple(previous)
        aliases = {5 + i: i for i in range(5)}
    return comm_call(body, live, ("x", "y", "z"), (1, 3), 45, ins, shapes, collective_id, aliases)


def to_heads(live, array, previous, collective_id):
    width = array.shape[-1]

    def body(copies, c, ins, outs):
        z = c["z"]
        moves = []
        for by in (2, 1, 3):
            to = peer(c, "z", by)
            moves.append(copies.remote(ins[0].at[to["seq"]], outs[0].at[:, z], to))
        own = copies.local(ins[0].at[z], outs[0].at[:, z])
        for move in moves:
            move.wait_recv()
        own.wait()
        copies.drain()

    ins, aliases = (array,), None
    if previous is not None:
        ins, aliases = (array, previous), {1: 0}
    return comm_call(
        body, live, ("z",), (1, 2, 3), 4, ins, (sds((4, 4, ROWS, width), BF),), collective_id, aliases
    )[0]


def to_tokens(live, array, previous, collective_id):
    width = array.shape[-1]

    def body(copies, c, ins, outs):
        z = c["z"]
        moves = []
        for by in (2, 1, 3):
            to = peer(c, "z", by)
            moves.append(copies.remote(ins[0].at[:, to["seq"]], outs[0].at[z], to))
        own = copies.local(ins[0].at[:, z], outs[0].at[z])
        for move in moves:
            move.wait_recv()
        own.wait()
        copies.drain()

    ins, aliases = (array,), None
    if previous is not None:
        ins, aliases = (array, previous), {1: 0}
    return comm_call(
        body, live, ("z",), (1, 2, 3), 4, ins, (sds((4, 4, ROWS, width), BF),), collective_id, aliases
    )[0]


def exchange(live, parts, collective_id):
    shapes = []
    for array, axis, dim in parts:
        shapes.append(sds((4,) + array.shape[:dim] + array.shape[dim + 1 :], array.dtype))
    axes = tuple(sorted({axis for _, axis, _ in parts}))

    def body(copies, c, ins, outs):
        moves, own = [], []
        for by in (2, 1, 3):
            for ref, out, (_, axis, dim) in zip(ins, outs, parts):
                to = peer(c, axis, by)
                there = lax.rem(c[axis] + by, 4)
                src = ref.at[(slice(None),) * dim + (there,)]
                moves.append(copies.remote(src, out.at[by], to))
        for ref, out, (_, axis, dim) in zip(ins, outs, parts):
            own.append(copies.local(ref.at[(slice(None),) * dim + (c[axis],)], out.at[0]))
        for move in moves:
            move.wait_recv()
        for copy in own:
            copy.wait()
        copies.drain()

    return comm_call(
        body, live, axes, (1, 2, 3), 4 * len(parts), tuple(p[0] for p in parts), shapes, collective_id
    )


def added(terms, dtype):
    return jnp.sum(terms.astype(F32), axis=0).astype(dtype)


def reduce_grads(live, qkv, out, up, down, small, base_id):
    q, o, u, d, s = exchange(
        live,
        ((qkv, "x", 2), (out, "x", 1), (up, "z", 0), (down, "y", 2), (small, "y", 2)),
        base_id,
    )
    q, o, u, d, s = added(q, BF), added(o, BF), added(u, BF), added(d, BF), added(s, F32)
    q, o, u, d, s = exchange(
        live, ((q, "z", 1), (o, "z", 0), (u, "x", 0), (d, "z", 0), (s, "z", 0)), base_id + 1
    )
    q, o, u, d, s = added(q, BF), added(o, BF), added(u, BF), added(d, BF), added(s, F32)
    q, o, u = q.reshape(4, 4, 12, 576), o.reshape(4, 12, D), u.reshape(4, 12, FF)
    return exchange(
        live, ((q, "y", 1), (o, "y", 0), (u, "y", 0), (d, "x", 0), (s, "x", 0)), base_id + 2
    )


BIG = pltpu.CompilerParams(vmem_limit_bytes=56 * 1024 * 1024)


def dot(a, b):
    return jnp.dot(a, b, preferred_element_type=F32)


def dot_nt(a, b):
    return lax.dot_general(a, b, (((1,), (1,)), ((), ())), preferred_element_type=F32)


def dot_tn(a, b):
    return lax.dot_general(a, b, (((0,), (0,)), ((), ())), preferred_element_type=F32)


def normalize(values):
    centered = values - jnp.mean(values, axis=-1, keepdims=True)
    spread = jnp.mean(centered * centered, axis=-1, keepdims=True)
    inverse = lax.rsqrt(spread + EPSILON)
    return centered * inverse, inverse


def norm_back(e, n, inverse):
    return inverse * (
        e - jnp.mean(e, axis=-1, keepdims=True) - n * jnp.mean(e * n, axis=-1, keepdims=True)
    )


def gelu_parts(u):
    inner = 0.7978845608 * (u + 0.044715 * (u * u * u))
    t = jnp.tanh(inner)
    return t


def whole(shape):
    zeros = (0,) * len(shape)
    return pl.BlockSpec(shape, lambda j: zeros)


def project_kernel(x_ref, vec_ref, bias_ref, w_ref, out_ref, n_ref):
    @pl.when(pl.program_id(0) == 0)
    def _():
        n, _ = normalize(x_ref[...].astype(F32))
        n_ref[...] = (n * vec_ref[0:1, :] + vec_ref[2:3, :]).astype(BF)

    out_ref[0] = (dot(n_ref[...], w_ref[0]) + bias_ref[0]).astype(BF)


def project(x, vec, bias, w):
    return pl.pallas_call(
        project_kernel,
        grid=(4,),
        out_shape=sds((4, TOK, 576), BF),
        in_specs=[
            whole((TOK, D)),
            whole((16, D)),
            pl.BlockSpec((1, 1, 576), lambda j: (j, 0, 0)),
            pl.BlockSpec((1, D, 576), lambda j: (j, 0, 0)),
        ],
        out_specs=pl.BlockSpec((1, TOK, 576), lambda j: (j, 0, 0)),
        scratch_shapes=[pltpu.VMEM((TOK, D), BF)],
        compiler_params=BIG,
    )(x, vec, bias, w)


BLOCK = 256


def masked(scores, block):
    rows = block * BLOCK + lax.broadcasted_iota(jnp.int32, scores.shape, 0)
    cols = lax.broadcasted_iota(jnp.int32, scores.shape, 1)
    return jnp.where(cols <= rows, scores, MASKED)


def attend_kernel(h_ref, o_ref, lse_ref):
    for head in range(3):
        q_at, k_at, v_at = HEAD * head, HL + HEAD * head, 2 * HL + HEAD * head
        for block in range(SEQ_LEN // BLOCK):
            rows, keys = pl.ds(block * BLOCK, BLOCK), (block + 1) * BLOCK
            q = h_ref[rows, q_at : q_at + HEAD] * jnp.asarray(0.125, BF)
            scores = masked(dot_nt(q, h_ref[0:keys, k_at : k_at + HEAD]), block)
            top = jnp.max(scores, axis=-1, keepdims=True)
            e = jnp.exp(scores - top)
            total = jnp.sum(e, axis=-1, keepdims=True)
            mixed = dot(e.astype(BF), h_ref[0:keys, v_at : v_at + HEAD])
            o_ref[rows, q_at : q_at + HEAD] = (mixed / total).astype(BF)
            lse_ref[rows, head : head + 1] = top + jnp.log(total)


def attend(heads):
    return pl.pallas_call(
        attend_kernel,
        out_shape=(sds((SEQ_LEN, HL), BF), sds((SEQ_LEN, 128), F32)),
        compiler_params=BIG,
    )(heads)


def attend_back_kernel(h_ref, lse_ref, g_ref, out_ref, dk_ref, dv_ref):
    for head in range(3):
        q_at, k_at, v_at = HEAD * head, HL + HEAD * head, 2 * HL + HEAD * head
        for block in reversed(range(SEQ_LEN // BLOCK)):
            rows, keys = pl.ds(block * BLOCK, BLOCK), (block + 1) * BLOCK
            q = h_ref[rows, q_at : q_at + HEAD] * jnp.asarray(0.125, BF)
            k = h_ref[0:keys, k_at : k_at + HEAD]
            g = g_ref[rows, q_at : q_at + HEAD]
            scores = masked(dot_nt(q, k), block)
            p = jnp.exp(scores - lse_ref[rows, head : head + 1])
            dp = dot_nt(g, h_ref[0:keys, v_at : v_at + HEAD])
            centre = jnp.sum(p * dp, axis=-1, keepdims=True)
            ds = (p * (dp - centre)).astype(BF)
            out_ref[rows, q_at : q_at + HEAD] = (dot(ds, k) * 0.125).astype(BF)
            dk = dot_tn(ds, q)
            dv = dot_tn(p.astype(BF), g)
            if block == SEQ_LEN // BLOCK - 1:
                dk_ref[...] = dk
                dv_ref[...] = dv
            else:
                dk_ref[0:keys, :] += dk
                dv_ref[0:keys, :] += dv
        out_ref[:, k_at : k_at + HEAD] = dk_ref[...].astype(BF)
        out_ref[:, v_at : v_at + HEAD] = dv_ref[...].astype(BF)


def attend_back(heads, lse, grads):
    return pl.pallas_call(
        attend_back_kernel,
        out_shape=sds((SEQ_LEN, 576), BF),
        scratch_shapes=[pltpu.VMEM((SEQ_LEN, HEAD), F32), pltpu.VMEM((SEQ_LEN, HEAD), F32)],
        compiler_params=BIG,
    )(heads, lse, grads)


def mlp_kernel(x_ref, m_ref, vec_ref, ub_ref, wo_ref, wu_ref, wd_ref, res_ref, mid_ref, raised_ref, n_ref, acc_ref):
    step = pl.program_id(0)

    @pl.when(step == 0)
    def _():
        branch = dot(m_ref[0], wo_ref[0])
        for p in range(1, 4):
            branch += dot(m_ref[p], wo_ref[p])
        middle = x_ref[...].astype(F32) + (branch + vec_ref[6:7, :])
        mid_ref[...] = middle
        n, _ = normalize(middle)
        n_ref[...] = (n * vec_ref[1:2, :] + vec_ref[3:4, :]).astype(BF)
        acc_ref[...] = middle + vec_ref[7:8, :]

    raised = dot(n_ref[...], wu_ref[...]) + ub_ref[0]
    raised_ref[...] = raised
    active = (0.5 * raised * (1.0 + gelu_parts(raised))).astype(BF)
    acc_ref[...] += dot(active, wd_ref[...])

    @pl.when(step == 3)
    def _():
        res_ref[...] = acc_ref[...].astype(BF)


def mlp(x, mixed, vec, ub, wo, wu, wd):
    return pl.pallas_call(
        mlp_kernel,
        grid=(4,),
        out_shape=(sds((TOK, D), BF), sds((TOK, D), F32), sds((TOK, FF), F32)),
        in_specs=[
            whole((TOK, D)),
            whole((4, TOK, HL)),
            whole((16, D)),
            pl.BlockSpec((1, 1, D), lambda j: (j, 0, 0)),
            whole((4, HL, D)),
            pl.BlockSpec((D, D), lambda j: (0, j)),
            pl.BlockSpec((D, D), lambda j: (j, 0)),
        ],
        out_specs=(whole((TOK, D)), whole((TOK, D)), pl.BlockSpec((TOK, D), lambda j: (0, j))),
        scratch_shapes=[pltpu.VMEM((TOK, D), BF), pltpu.VMEM((TOK, D), F32)],
        compiler_params=BIG,
    )(x, mixed, vec, ub, wo, wu, wd)


def mlp_back_kernel(
    g_ref, raised_ref, mid_ref, m_ref, vec_ref, wo_ref, wu_ref, wd_ref,
    gd_ref, gu_ref, go_ref, gm_ref, gmid_ref, sums_ref, gub_ref, n_ref, acc_ref,
):
    step = pl.program_id(0)

    @pl.when(step == 0)
    def _():
        n, _ = normalize(mid_ref[...])
        n_ref[...] = (n * vec_ref[1:2, :] + vec_ref[3:4, :]).astype(BF)
        acc_ref[...] = jnp.zeros_like(acc_ref)

    g = g_ref[...]
    u = raised_ref[...]
    t = gelu_parts(u)
    active = (0.5 * u * (1.0 + t)).astype(BF)
    gd_ref[...] = dot_tn(active, g).astype(BF)
    slope = 0.5 * (1.0 + t) + 0.5 * u * (1.0 - t * t) * (
        0.7978845608 * (1.0 + 3.0 * 0.044715 * (u * u))
    )
    grad_raised = (dot_nt(g, wd_ref[...]) * slope).astype(BF)
    gub_ref[0] = jnp.sum(grad_raised.astype(F32), axis=0, keepdims=True)
    gu_ref[...] = dot_tn(n_ref[...], grad_raised).astype(BF)
    acc_ref[...] += dot_nt(grad_raised, wu_ref[...])

    @pl.when(step == 3)
    def _():
        n, inverse = normalize(mid_ref[...])
        back = acc_ref[...]
        g32 = g.astype(F32)
        grad_middle = g32 + norm_back(back * vec_ref[1:2, :], n, inverse)
        gmid_ref[...] = grad_middle
        branch = grad_middle.astype(BF)
        sums_ref[...] = jnp.zeros_like(sums_ref)
        sums_ref[0:1, :] = jnp.sum(back * n, axis=0, keepdims=True)
        sums_ref[1:2, :] = jnp.sum(back, axis=0, keepdims=True)
        sums_ref[2:3, :] = jnp.sum(branch.astype(F32), axis=0, keepdims=True)
        sums_ref[3:4, :] = jnp.sum(g32, axis=0, keepdims=True)
        for p in range(4):
            go_ref[p] = dot_tn(m_ref[p], branch).astype(BF)
            gm_ref[p] = dot_nt(branch, wo_ref[p]).astype(BF)


def mlp_back(g, raised, middle, mixed, vec, wo, wu, wd):
    return pl.pallas_call(
        mlp_back_kernel,
        grid=(4,),
        out_shape=(
            sds((FF, D), BF),
            sds((D, FF), BF),
            sds((4, HL, D), BF),
            sds((4, TOK, HL), BF),
            sds((TOK, D), F32),
            sds((8, D), F32),
            sds((4, 1, D), F32),
        ),
        in_specs=[
            whole((TOK, D)),
            pl.BlockSpec((TOK, D), lambda j: (0, j)),
            whole((TOK, D)),
            whole((4, TOK, HL)),
            whole((16, D)),
            whole((4, HL, D)),
            pl.BlockSpec((D, D), lambda j: (0, j)),
            pl.BlockSpec((D, D), lambda j: (j, 0)),
        ],
        out_specs=(
            pl.BlockSpec((D, D), lambda j: (j, 0)),
            pl.BlockSpec((D, D), lambda j: (0, j)),
            whole((4, HL, D)),
            whole((4, TOK, HL)),
            whole((TOK, D)),
            whole((8, D)),
            pl.BlockSpec((1, 1, D), lambda j: (j, 0, 0)),
        ),
        scratch_shapes=[pltpu.VMEM((TOK, D), BF), pltpu.VMEM((TOK, D), F32)],
        compiler_params=BIG,
    )(g, raised, middle, mixed, vec, wo, wu, wd)


def project_back_kernel(x_ref, gp_ref, gmid_ref, vec_ref, w_ref, gw_ref, gx_ref, sums_ref, gb_ref, n_ref, acc_ref):
    step = pl.program_id(0)

    @pl.when(step == 0)
    def _():
        n, _ = normalize(x_ref[...].astype(F32))
        n_ref[...] = (n * vec_ref[0:1, :] + vec_ref[2:3, :]).astype(BF)
        acc_ref[...] = jnp.zeros_like(acc_ref)

    gp = gp_ref[0]
    gw_ref[0] = dot_tn(n_ref[...], gp).astype(BF)
    gb_ref[0] = jnp.sum(gp.astype(F32), axis=0, keepdims=True)
    acc_ref[...] += dot_nt(gp, w_ref[0])

    @pl.when(step == 3)
    def _():
        n, inverse = normalize(x_ref[...].astype(F32))
        back = acc_ref[...]
        gx_ref[...] = (gmid_ref[...] + norm_back(back * vec_ref[0:1, :], n, inverse)).astype(BF)
        sums_ref[...] = jnp.zeros_like(sums_ref)
        sums_ref[0:1, :] = jnp.sum(back * n, axis=0, keepdims=True)
        sums_ref[1:2, :] = jnp.sum(back, axis=0, keepdims=True)


def project_back(x, gp, gmid, vec, w):
    return pl.pallas_call(
        project_back_kernel,
        grid=(4,),
        out_shape=(sds((4, D, 576), BF), sds((TOK, D), BF), sds((8, D), F32), sds((4, 1, 576), F32)),
        in_specs=[
            whole((TOK, D)),
            pl.BlockSpec((1, TOK, 576), lambda j: (j, 0, 0)),
            whole((TOK, D)),
            whole((16, D)),
            pl.BlockSpec((1, D, 576), lambda j: (j, 0, 0)),
        ],
        out_specs=(
            pl.BlockSpec((1, D, 576), lambda j: (j, 0, 0)),
            whole((TOK, D)),
            whole((8, D)),
            pl.BlockSpec((1, 1, 576), lambda j: (j, 0, 0)),
        ),
        scratch_shapes=[pltpu.VMEM((TOK, D), BF), pltpu.VMEM((TOK, D), F32)],
        compiler_params=BIG,
    )(x, gp, gmid, vec, w)


def unpack_small(small):
    flat = small.reshape(64, 2048)
    rows = flat[:, :96].reshape(64, 8, 12).transpose(1, 0, 2).reshape(8, D)
    up = flat[:, 96:144].reshape(4, 1, D)
    vec = jnp.concatenate([rows, jnp.zeros((8, D), F32)])
    bias = jnp.concatenate([rows[4].reshape(4, HL), jnp.zeros((4, HL), F32), rows[5].reshape(4, HL)], axis=1)
    return vec, bias.reshape(4, 1, 576), up


def open_weights(raw):
    qkv, out, up, down, small = raw
    vec, bias, ub = unpack_small(small)
    return (
        qkv.reshape(4, D, 576),
        out.reshape(4, HL, D),
        up.reshape(D, FF),
        down.reshape(FF, D),
        vec,
        bias,
        ub,
    )


def forward(live, x, weights, previous, base_id):
    qkv, wo, wu, wd, vec, bias, ub = weights
    projected = project(x, vec, bias, qkv)
    heads4 = to_heads(live, projected.reshape(4, 4, ROWS, 576), previous[0], base_id)
    heads = heads4.reshape(SEQ_LEN, 576)
    mixed_heads, lse = attend(heads)
    mixed4 = to_tokens(live, mixed_heads.reshape(4, 4, ROWS, HL), previous[1], base_id + 1)
    mixed = mixed4.reshape(4, TOK, HL)
    result, middle, raised = mlp(x, mixed, vec, ub, wo, wu, wd)
    return result, (heads, lse, mixed, middle, raised), (heads4, mixed4)


def backward(live, g, x, weights, saved, previous, base_id):
    qkv, wo, wu, wd, vec, bias, ub = weights
    heads, lse, mixed, middle, raised = saved
    g_down, g_up, g_out, g_mixed, g_middle, sums_two, g_ub = mlp_back(
        g, raised, middle, mixed, vec, wo, wu, wd
    )
    g_heads4 = to_heads(live, g_mixed.reshape(4, 4, ROWS, HL), previous[0], base_id)
    g_split = attend_back(heads, lse, g_heads4.reshape(SEQ_LEN, HL))
    g_proj4 = to_tokens(live, g_split.reshape(4, 4, ROWS, 576), previous[1], base_id + 1)
    g_qkv, g_x, sums_one, g_bias = project_back(x, g_proj4.reshape(4, TOK, 576), g_middle, vec, qkv)
    rows = jnp.concatenate(
        [
            sums_one[0:1],
            sums_two[0:1],
            sums_one[1:2],
            sums_two[1:2],
            g_bias[:, 0, :HL].reshape(1, D),
            g_bias[:, 0, 2 * HL :].reshape(1, D),
            sums_two[2:4],
        ]
    )
    small = jnp.concatenate(
        [
            rows.reshape(8, 64, 12).transpose(1, 0, 2).reshape(64, 96),
            g_ub.reshape(64, 48),
            jnp.zeros((64, 1024 - 144), F32),
        ],
        axis=1,
    )
    grads = (
        g_qkv.reshape(4, 4, 4, 48, 576),
        g_out.reshape(4, 4, 48, D),
        g_up.reshape(4, 4, 48, FF),
        g_down.reshape(4, 4, 4, 48, D),
        small.reshape(4, 4, 4, 8, 128),
    )
    return g_x, grads, (g_heads4, g_proj4)


def per_device(ends, w_qkv, w_out, w_up, w_down, norm_gains, biases, up_bias):
    section = lax.axis_index("section")
    own = ends.reshape(TOK, D)
    qkv = w_qkv[0].reshape(12, 3, 4, HL).transpose(2, 0, 1, 3).reshape(4, 12, 576)
    small = jnp.concatenate(
        [norm_gains.reshape(-1), biases.reshape(-1), up_bias.reshape(-1), jnp.zeros((2048 - 144,), BF)]
    ).astype(F32)
    q_y, o_y, u_y, d_x, s_x = gather_first(qkv, w_out[0], w_up[0], w_down[0], small.reshape(2, 8, 128))
    first = (
        q_y.transpose(1, 0, 2, 3).reshape(4, 48, 576),
        o_y.reshape(48, D),
        u_y.reshape(48, FF),
        d_x,
        s_x,
    )
    raw = gather_rest(0, *first, None, 1)
    result, _, kept = forward(0, own, open_weights(raw), (None, None), 3)
    arriving = lax.ppermute(result, "section", [(0, 1)])
    raw, arriving = lax.optimization_barrier((raw, arriving))
    raw = gather_rest(1, *first, raw, 2)
    weights = open_weights(raw)
    x = jnp.where(section == 0, own, arriving)
    result, saved, _ = forward(1, x, weights, kept, 5)

    g_x, grads, _ = backward(1, own, x, weights, saved, (None, None), 7)
    arriving = lax.ppermute(g_x, "section", [(1, 0)])
    grads, arriving = lax.optimization_barrier((grads, arriving))
    total_one = reduce_grads(1, *grads, 11)
    total_one, arriving = lax.optimization_barrier((total_one, arriving))
    g = jnp.where(section == 1, own, arriving)
    g_x, grads, _ = backward(0, g, x, weights, saved, (None, None), 9)
    total_zero = reduce_grads(0, *grads, 14)
    q, o, u, d, s = (
        added(jnp.where(section == 0, zero, one), F32) for zero, one in zip(total_zero, total_one)
    )
    flat = s.reshape(1024)
    boundary = jnp.where(section == 0, g_x, result)
    return (
        boundary.reshape(1, 1, GROUPS, ROWS, D),
        q.reshape(4, 12, 3, HL).transpose(1, 2, 0, 3).reshape(1, 12, 3 * D),
        o[None],
        u[None],
        d[None],
        flat[:24].reshape(1, 2, 12),
        flat[24:96].reshape(1, 6, 12),
        flat[96:144].reshape(1, 48),
    )


def solution(mesh):
    rows = P("section", ("seq", "shard"), None)
    columns = P("section", None, ("seq", "shard"))
    ends = P("section", "shard", None, "seq", None)
    hidden = P("section", ("seq", "shard"))
    placed = (ends, rows, rows, rows, rows, columns, columns, hidden)
    return jax.shard_map(per_device, mesh=mesh, in_specs=placed, out_specs=placed, check_vma=False)
```

```python
import functools

import jax
import jax.numpy as jnp
from jax import lax
from jax.experimental import pallas as pl
from jax.experimental.pallas import tpu as pltpu
from jax.sharding import PartitionSpec as P

HEAD = 64
FF = 3072
D = 768
GROUPS = 4
ROWS = 64
TOK = GROUPS * ROWS
SEQ_LEN = 1024
HL = 192
EPSILON = 1e-05
MASKED = -1e30
BF = jnp.bfloat16
F32 = jnp.float32
MESH = pl.DeviceIdType.MESH
HBM = pltpu.HBM


def sds(shape, dtype):
    return jax.ShapeDtypeStruct(shape, dtype)


def coords():
    shard = lax.axis_index("shard")
    return {"x": shard // 4, "y": lax.rem(shard, 4), "z": lax.axis_index("seq")}


def peer(c, axis, by):
    moved = dict(c)
    moved[axis] = lax.rem(c[axis] + by, 4)
    return {"section": lax.axis_index("section"), "seq": moved["z"], "shard": moved["x"] * 4 + moved["y"]}


def meet(c, axes, steps):
    barrier = pltpu.get_barrier_semaphore()
    for axis in axes:
        for by in steps:
            pl.semaphore_signal(barrier, inc=1, device_id=peer(c, axis, by), device_id_type=MESH)
    pl.semaphore_wait(barrier, len(axes) * len(steps))


class Copies:
    def __init__(self, send, recv):
        self.send, self.recv, self.used, self.sent = send, recv, 0, []

    def remote(self, src, dst, to):
        copy = pltpu.make_async_remote_copy(
            src_ref=src,
            dst_ref=dst,
            send_sem=self.send.at[self.used],
            recv_sem=self.recv.at[self.used],
            device_id=to,
            device_id_type=MESH,
        )
        self.used += 1
        copy.start()
        self.sent.append(copy)
        return copy

    def local(self, src, dst):
        copy = pltpu.make_async_copy(src, dst, self.send.at[self.used])
        self.used += 1
        copy.start()
        return copy

    def drain(self):
        for copy in self.sent:
            copy.wait_send()


class Gather:
    def __init__(self, copies, c, axis, own, dst, half):
        self.copies, self.c, self.axis, self.own, self.dst, self.half = copies, c, axis, own, dst, half

    def first(self):
        a = self.c[self.axis]
        self.right, self.left = peer(self.c, self.axis, 1), peer(self.c, self.axis, 3)
        self.go_right = self.copies.remote(self.own, self.dst(a), self.right)
        self.go_left = self.copies.remote(self.own, self.dst(a), self.left)

    def second(self):
        a = self.c[self.axis]
        before, after = lax.rem(a + 3, 4), lax.rem(a + 1, 4)
        self.go_right.wait_recv()
        self.on_right = self.copies.remote(self.half(before, 0), self.half(before, 0), self.right)
        self.go_left.wait_recv()
        self.on_left = self.copies.remote(self.half(after, 1), self.half(after, 1), self.left)

    def third(self):
        self.on_right.wait_recv()
        self.on_left.wait_recv()


def run_gathers(gathers):
    for g in gathers:
        g.first()
    for g in gathers:
        g.second()


def comm_call(body, live, axes, steps, count, ins, out_shapes, collective_id, aliases=None, in_vmem=0):
    n_in, n_out = len(ins), len(out_shapes)

    def kernel(*refs):
        in_refs, out_refs = refs[:n_in], refs[n_in : n_in + n_out]
        send, recv = refs[n_in + n_out :]

        def act():
            c = coords()
            meet(c, axes, steps)
            body(Copies(send, recv), c, in_refs, out_refs)

        if live is None:
            act()
        else:
            pl.when(lax.axis_index("section") == live)(act)

    return pl.pallas_call(
        kernel,
        out_shape=tuple(out_shapes),
        in_specs=[pl.BlockSpec(memory_space=pltpu.VMEM if i < in_vmem else HBM) for i in range(n_in)],
        out_specs=tuple([pl.BlockSpec(memory_space=HBM)] * n_out),
        scratch_shapes=[pltpu.SemaphoreType.DMA((count,)), pltpu.SemaphoreType.DMA((count,))],
        input_output_aliases=aliases or {},
        compiler_params=pltpu.CompilerParams(
            collective_id=collective_id, has_side_effects=True, vmem_limit_bytes=24 * 1024 * 1024
        ),
    )(*ins)


def gather_first(qkv, out, up, down, small):
    def body(copies, c, ins, outs):
        y, x = c["y"], c["x"]
        q_in, o_in, u_in, d_in, s_in = ins
        q_y, o_y, u_y, d_x, s_x = outs
        gathers = [
            Gather(copies, c, "y", u_in, lambda i: u_y.at[i], lambda i, h: u_y.at[i, :, pl.ds(1536 * h, 1536)]),
            Gather(copies, c, "y", q_in, lambda i: q_y.at[i], lambda i, h: q_y.at[i, pl.ds(2 * h, 2)]),
            Gather(copies, c, "y", o_in, lambda i: o_y.at[i], lambda i, h: o_y.at[i, :, pl.ds(384 * h, 384)]),
            Gather(copies, c, "x", d_in, lambda i: d_x.at[i], lambda i, h: d_x.at[i, :, pl.ds(384 * h, 384)]),
            Gather(copies, c, "x", s_in, lambda i: s_x.at[i], lambda i, h: s_x.at[i, h]),
        ]
        own = [
            copies.local(u_in, u_y.at[y]),
            copies.local(q_in, q_y.at[y]),
            copies.local(o_in, o_y.at[y]),
            copies.local(d_in, d_x.at[x]),
            copies.local(s_in, s_x.at[x]),
        ]
        run_gathers(gathers)
        for g in gathers:
            g.third()
        for copy in own:
            copy.wait()
        copies.drain()

    shapes = (
        sds((4, 4, 12, 576), BF),
        sds((4, 12, D), BF),
        sds((4, 12, FF), BF),
        sds((4, 48, D), BF),
        sds((4, 2, 8, 128), F32),
    )
    return comm_call(body, None, ("x", "y"), (1, 3), 25, (qkv, out, up, down, small), shapes, 0, None, 5)


def gather_rest(live, qkv, out, up, down, small, previous, token, collective_id):
    def body(copies, c, ins, outs):
        x, y, z = c["x"], c["y"], c["z"]
        q_in, o_in, u_in, d_in, s_in = ins[:5]
        q, o, u, d, s = outs
        one = [
            Gather(copies, c, "z", q_in, lambda i: q.at[:, i, x], lambda i, h: q.at[pl.ds(2 * h, 2), i, x]),
            Gather(copies, c, "z", o_in, lambda i: o.at[i, x], lambda i, h: o.at[i, x, :, pl.ds(384 * h, 384)]),
            Gather(copies, c, "x", u_in, lambda i: u.at[z, i], lambda i, h: u.at[z, i, :, pl.ds(1536 * h, 1536)]),
            Gather(copies, c, "z", d_in, lambda i: d.at[i, :, y], lambda i, h: d.at[i, pl.ds(2 * h, 2), y]),
            Gather(copies, c, "z", s_in, lambda i: s.at[i, :, y], lambda i, h: s.at[i, pl.ds(2 * h, 2), y]),
        ]
        own = [
            copies.local(q_in, q.at[:, z, x]),
            copies.local(o_in, o.at[z, x]),
            copies.local(u_in, u.at[z, x]),
            copies.local(d_in, d.at[z, :, y]),
            copies.local(s_in, s.at[z, :, y]),
        ]
        run_gathers(one)
        two = [
            Gather(copies, c, "x", q.at[:, :, x], lambda i: q.at[:, :, i], lambda i, h: q.at[pl.ds(2 * h, 2), :, i]),
            Gather(copies, c, "x", o.at[:, x], lambda i: o.at[:, i], lambda i, h: o.at[pl.ds(2 * h, 2), i]),
            Gather(copies, c, "z", u.at[z], lambda i: u.at[i], lambda i, h: u.at[i, pl.ds(2 * h, 2)]),
            Gather(copies, c, "y", d.at[:, :, y], lambda i: d.at[:, :, i], lambda i, h: d.at[pl.ds(2 * h, 2), :, i]),
            Gather(copies, c, "y", s.at[:, :, y], lambda i: s.at[:, :, i], lambda i, h: s.at[pl.ds(2 * h, 2), :, i]),
        ]
        for k in range(5):
            one[k].third()
            own[k].wait()
            two[k].first()
        for g in two:
            g.second()
        for g in two:
            g.third()
        copies.drain()

    shapes = (
        sds((4, 4, 4, 48, 576), BF),
        sds((4, 4, 48, D), BF),
        sds((4, 4, 48, FF), BF),
        sds((4, 4, 4, 48, D), BF),
        sds((4, 4, 4, 2, 8, 128), F32),
    )
    ins = (qkv, out, up, down, small)
    aliases = None
    if previous is not None:
        ins = ins + tuple(previous) + (token,)
        aliases = {5 + i: i for i in range(5)}
    return comm_call(body, live, ("x", "y", "z"), (1, 3), 45, ins, shapes, collective_id, aliases, 5)


def to_heads(live, array, previous, collective_id):
    width = array.shape[-1]

    def body(copies, c, ins, outs):
        z = c["z"]
        moves = []
        for by in (2, 1, 3):
            to = peer(c, "z", by)
            moves.append(copies.remote(ins[0].at[to["seq"]], outs[0].at[:, z], to))
        own = copies.local(ins[0].at[z], outs[0].at[:, z])
        for move in moves:
            move.wait_recv()
        own.wait()
        copies.drain()

    ins, aliases = (array,), None
    if previous is not None:
        ins, aliases = (array, previous), {1: 0}
    return comm_call(
        body, live, ("z",), (1, 2, 3), 4, ins, (sds((4, 4, ROWS, width), BF),), collective_id, aliases, 1
    )[0]


def to_tokens(live, array, previous, collective_id):
    width = array.shape[-1]

    def body(copies, c, ins, outs):
        z = c["z"]
        moves = []
        for by in (2, 1, 3):
            to = peer(c, "z", by)
            moves.append(copies.remote(ins[0].at[:, to["seq"]], outs[0].at[z], to))
        own = copies.local(ins[0].at[:, z], outs[0].at[z])
        for move in moves:
            move.wait_recv()
        own.wait()
        copies.drain()

    ins, aliases = (array,), None
    if previous is not None:
        ins, aliases = (array, previous), {1: 0}
    return comm_call(
        body, live, ("z",), (1, 2, 3), 4, ins, (sds((4, 4, ROWS, width), BF),), collective_id, aliases, 1
    )[0]


def reduce_kernel(live, q_in, o_in, u_in, d_in, s_in, q, o, u, d, s, *scratch):
    q1, o1, u1, d1, s1, q2, o2, u2, d2, s2, tmp, qs, os, us, q3, o3, u3, d3, s3, send, recv = scratch

    def act():
        c = coords()
        x, y, z = c["x"], c["y"], c["z"]
        copies = Copies(send, recv)
        own = [
            copies.local(d_in.at[:, :, y], d1.at[0]),
            copies.local(u_in.at[z], u1.at[0]),
            copies.local(q_in.at[:, :, x], q1.at[0]),
            copies.local(o_in.at[:, x], o1.at[0]),
            copies.local(s_in.at[:, :, y], s1.at[0]),
        ]
        meet(c, ("x", "y", "z"), (1, 2, 3))

        def spread(axis, source, target):
            moves = []
            for by in (2, 1, 3):
                there = lax.rem(c[axis] + by, 4)
                moves.append(copies.remote(source(there), target.at[by], peer(c, axis, by)))
            return moves

        one = [
            spread("y", lambda i: d_in.at[:, :, i], d1),
            spread("z", lambda i: u_in.at[i], u1),
            spread("x", lambda i: q_in.at[:, :, i], q1),
            spread("x", lambda i: o_in.at[:, i], o1),
            spread("y", lambda i: s_in.at[:, :, i], s1),
        ]

        def arrived(moves):
            for move in moves:
                move.wait_recv()

        def add(ref, at):
            total = ref[(0,) + at].astype(F32)
            for k in range(1, 4):
                total += ref[(k,) + at].astype(F32)
            return total

        def add_all(ref, kind):
            @pl.loop(0, 16)
            def _(i):
                at = (i // 4, lax.rem(i, 4))
                ref[(0,) + at] = add(ref, at).astype(kind)

        arrived(one[0])
        own[0].wait()
        add_all(d1, BF)
        two_d = spread("z", lambda i: d1.at[0, i], d2)
        arrived(one[1])
        own[1].wait()

        @pl.loop(0, 4)
        def _(i):
            for k in range(4):
                at = (i, slice(None), pl.ds(D * k, D))
                u1[(0,) + at] = add(u1, at).astype(BF)

        two_u = spread("x", lambda i: u1.at[0, i], u2)
        arrived(one[2])
        own[2].wait()
        add_all(q1, BF)
        two_q = spread("z", lambda i: q1.at[0, :, i], q2)
        arrived(one[3])
        own[3].wait()

        @pl.loop(0, 4)
        def _(i):
            o1[0, i] = add(o1, (i,)).astype(BF)

        two_o = spread("z", lambda i: o1.at[0, i], o2)
        arrived(one[4])
        own[4].wait()
        add_all(s1, F32)
        two_s = spread("z", lambda i: s1.at[0, i], s2)

        def more(mine, ref, at):
            total = mine.astype(F32)
            for k in range(1, 4):
                total += ref[(k,) + at].astype(F32)
            return total

        arrived(two_d)

        @pl.loop(0, 4)
        def _(i):
            d2[0, i] = more(d1[0, z, i], d2, (i,)).astype(BF)

        three_d = spread("x", lambda i: d2.at[0, i], d3)
        arrived(two_u)
        for k in range(4):
            at = (slice(None), pl.ds(D * k, D))
            tmp[...] = more(u1[(0, x) + at], u2, at)
            for i in range(4):
                us[i, :, D * k : D * k + D] = tmp[12 * i : 12 * i + 12, :].astype(BF)
        three_u = spread("y", lambda i: us.at[i], u3)
        arrived(two_q)
        for p in range(4):
            tmp[:, 0:576] = more(q1[0, p, z], q2, (p,))
            for i in range(4):
                qs[i, p] = tmp[12 * i : 12 * i + 12, 0:576].astype(BF)
        three_q = spread("y", lambda i: qs.at[i], q3)
        arrived(two_o)
        tmp[...] = more(o1[0, z], o2, ())
        for i in range(4):
            os[i] = tmp[12 * i : 12 * i + 12, :].astype(BF)
        three_o = spread("y", lambda i: os.at[i], o3)
        arrived(two_s)

        @pl.loop(0, 4)
        def _(i):
            s2[0, i] = more(s1[0, z, i], s2, (i,))

        three_s = spread("x", lambda i: s2.at[0, i], s3)
        arrived(three_d)
        d[...] = more(d2[0, x], d3, ())
        arrived(three_u)
        u[...] = more(us[y], u3, ())
        arrived(three_q)
        q[...] = more(qs[y], q3, ())
        arrived(three_o)
        o[...] = more(os[y], o3, ())
        arrived(three_s)
        s[...] = more(s2[0, x], s3, ())
        copies.drain()

    pl.when(lax.axis_index("section") == live)(act)


def reduce_grads(live, qkv, out, up, down, small, collective_id):
    vmem = pltpu.VMEM
    count = 5 + 3 * 15
    return pl.pallas_call(
        functools.partial(reduce_kernel, live),
        out_shape=(
            sds((4, 12, 576), F32),
            sds((12, D), F32),
            sds((12, FF), F32),
            sds((48, D), F32),
            sds((8, 128), F32),
        ),
        in_specs=[pl.BlockSpec(memory_space=HBM)] * 5,
        out_specs=tuple([pl.BlockSpec(memory_space=vmem)] * 5),
        scratch_shapes=[
            vmem((4, 4, 4, 48, 576), BF),
            vmem((4, 4, 48, D), BF),
            vmem((4, 4, 48, FF), BF),
            vmem((4, 4, 4, 48, D), BF),
            vmem((4, 4, 4, 8, 128), F32),
            vmem((4, 4, 48, 576), BF),
            vmem((4, 48, D), BF),
            vmem((4, 48, FF), BF),
            vmem((4, 4, 48, D), BF),
            vmem((4, 4, 8, 128), F32),
            vmem((48, D), F32),
            vmem((4, 4, 12, 576), BF),
            vmem((4, 12, D), BF),
            vmem((4, 12, FF), BF),
            vmem((4, 4, 12, 576), BF),
            vmem((4, 12, D), BF),
            vmem((4, 12, FF), BF),
            vmem((4, 48, D), BF),
            vmem((4, 8, 128), F32),
            pltpu.SemaphoreType.DMA((count,)),
            pltpu.SemaphoreType.DMA((count,)),
        ],
        compiler_params=pltpu.CompilerParams(
            collective_id=collective_id, has_side_effects=True, vmem_limit_bytes=48 * 1024 * 1024
        ),
    )(qkv, out, up, down, small)


BIG = pltpu.CompilerParams(vmem_limit_bytes=56 * 1024 * 1024)


def dot(a, b):
    return jnp.dot(a, b, preferred_element_type=F32)


def dot_nt(a, b):
    return lax.dot_general(a, b, (((1,), (1,)), ((), ())), preferred_element_type=F32)


def dot_tn(a, b):
    return lax.dot_general(a, b, (((0,), (0,)), ((), ())), preferred_element_type=F32)


def normalize(values):
    centered = values - jnp.mean(values, axis=-1, keepdims=True)
    spread = jnp.mean(centered * centered, axis=-1, keepdims=True)
    inverse = lax.rsqrt(spread + EPSILON)
    return centered * inverse, inverse


def norm_back(e, n, inverse):
    return inverse * (
        e - jnp.mean(e, axis=-1, keepdims=True) - n * jnp.mean(e * n, axis=-1, keepdims=True)
    )


def gelu_parts(u):
    inner = 0.7978845608 * (u + 0.044715 * (u * u * u))
    t = jnp.tanh(inner)
    return t


def whole(shape):
    zeros = (0,) * len(shape)
    return pl.BlockSpec(shape, lambda j: zeros)


def project_kernel(x_ref, vec_ref, bias_ref, w_ref, out_ref, n_ref):
    @pl.when(pl.program_id(0) == 0)
    def _():
        n, _ = normalize(x_ref[...].astype(F32))
        n_ref[...] = (n * vec_ref[0:1, :] + vec_ref[2:3, :]).astype(BF)

    out_ref[0] = (dot(n_ref[...], w_ref[0]) + bias_ref[0]).astype(BF)


def project(x, vec, bias, w):
    return pl.pallas_call(
        project_kernel,
        grid=(4,),
        out_shape=sds((4, TOK, 576), BF),
        in_specs=[
            whole((TOK, D)),
            whole((16, D)),
            pl.BlockSpec((1, 1, 576), lambda j: (j, 0, 0)),
            pl.BlockSpec((1, D, 576), lambda j: (j, 0, 0)),
        ],
        out_specs=pl.BlockSpec((1, TOK, 576), lambda j: (j, 0, 0)),
        scratch_shapes=[pltpu.VMEM((TOK, D), BF)],
        compiler_params=BIG,
    )(x, vec, bias, w)


BLOCK = 256


def masked(scores, block):
    rows = block * BLOCK + lax.broadcasted_iota(jnp.int32, scores.shape, 0)
    cols = lax.broadcasted_iota(jnp.int32, scores.shape, 1)
    return jnp.where(cols <= rows, scores, MASKED)


def attend_kernel(h_ref, o_ref, lse_ref):
    for head in range(3):
        q_at, k_at, v_at = HEAD * head, HL + HEAD * head, 2 * HL + HEAD * head
        for block in range(SEQ_LEN // BLOCK):
            rows, keys = pl.ds(block * BLOCK, BLOCK), (block + 1) * BLOCK
            q = h_ref[rows, q_at : q_at + HEAD] * jnp.asarray(0.125, BF)
            scores = masked(dot_nt(q, h_ref[0:keys, k_at : k_at + HEAD]), block)
            top = jnp.max(scores, axis=-1, keepdims=True)
            e = jnp.exp(scores - top)
            total = jnp.sum(e, axis=-1, keepdims=True)
            mixed = dot(e.astype(BF), h_ref[0:keys, v_at : v_at + HEAD])
            o_ref[rows, q_at : q_at + HEAD] = (mixed / total).astype(BF)
            lse_ref[rows, head : head + 1] = top + jnp.log(total)


def attend(heads):
    return pl.pallas_call(
        attend_kernel,
        out_shape=(sds((SEQ_LEN, HL), BF), sds((SEQ_LEN, 128), F32)),
        compiler_params=BIG,
    )(heads)


def attend_back_kernel(h_ref, lse_ref, g_ref, out_ref, dk_ref, dv_ref):
    for head in range(3):
        q_at, k_at, v_at = HEAD * head, HL + HEAD * head, 2 * HL + HEAD * head
        for block in reversed(range(SEQ_LEN // BLOCK)):
            rows, keys = pl.ds(block * BLOCK, BLOCK), (block + 1) * BLOCK
            q = h_ref[rows, q_at : q_at + HEAD] * jnp.asarray(0.125, BF)
            k = h_ref[0:keys, k_at : k_at + HEAD]
            g = g_ref[rows, q_at : q_at + HEAD]
            scores = masked(dot_nt(q, k), block)
            p = jnp.exp(scores - lse_ref[rows, head : head + 1])
            dp = dot_nt(g, h_ref[0:keys, v_at : v_at + HEAD])
            centre = jnp.sum(p * dp, axis=-1, keepdims=True)
            ds = (p * (dp - centre)).astype(BF)
            out_ref[rows, q_at : q_at + HEAD] = (dot(ds, k) * 0.125).astype(BF)
            dk = dot_tn(ds, q)
            dv = dot_tn(p.astype(BF), g)
            if block == SEQ_LEN // BLOCK - 1:
                dk_ref[...] = dk
                dv_ref[...] = dv
            else:
                dk_ref[0:keys, :] += dk
                dv_ref[0:keys, :] += dv
        out_ref[:, k_at : k_at + HEAD] = dk_ref[...].astype(BF)
        out_ref[:, v_at : v_at + HEAD] = dv_ref[...].astype(BF)


def attend_back(heads, lse, grads):
    return pl.pallas_call(
        attend_back_kernel,
        out_shape=sds((SEQ_LEN, 576), BF),
        scratch_shapes=[pltpu.VMEM((SEQ_LEN, HEAD), F32), pltpu.VMEM((SEQ_LEN, HEAD), F32)],
        compiler_params=BIG,
    )(heads, lse, grads)


def mlp_kernel(x_ref, m_ref, vec_ref, ub_ref, wo_ref, wu_ref, wd_ref, res_ref, mid_ref, raised_ref, n_ref, acc_ref):
    step = pl.program_id(0)

    @pl.when(step == 0)
    def _():
        branch = dot(m_ref[0], wo_ref[0])
        for p in range(1, 4):
            branch += dot(m_ref[p], wo_ref[p])
        middle = x_ref[...].astype(F32) + (branch + vec_ref[6:7, :])
        mid_ref[...] = middle
        n, _ = normalize(middle)
        n_ref[...] = (n * vec_ref[1:2, :] + vec_ref[3:4, :]).astype(BF)
        acc_ref[...] = middle + vec_ref[7:8, :]

    raised = dot(n_ref[...], wu_ref[...]) + ub_ref[0]
    raised_ref[...] = raised
    active = (0.5 * raised * (1.0 + gelu_parts(raised))).astype(BF)
    acc_ref[...] += dot(active, wd_ref[...])

    @pl.when(step == 3)
    def _():
        res_ref[...] = acc_ref[...].astype(BF)


def mlp(x, mixed, vec, ub, wo, wu, wd):
    return pl.pallas_call(
        mlp_kernel,
        grid=(4,),
        out_shape=(sds((TOK, D), BF), sds((TOK, D), F32), sds((TOK, FF), F32)),
        in_specs=[
            whole((TOK, D)),
            whole((4, TOK, HL)),
            whole((16, D)),
            pl.BlockSpec((1, 1, D), lambda j: (j, 0, 0)),
            whole((4, HL, D)),
            pl.BlockSpec((D, D), lambda j: (0, j)),
            pl.BlockSpec((D, D), lambda j: (j, 0)),
        ],
        out_specs=(whole((TOK, D)), whole((TOK, D)), pl.BlockSpec((TOK, D), lambda j: (0, j))),
        scratch_shapes=[pltpu.VMEM((TOK, D), BF), pltpu.VMEM((TOK, D), F32)],
        compiler_params=BIG,
    )(x, mixed, vec, ub, wo, wu, wd)


def mlp_back_kernel(
    g_ref, raised_ref, mid_ref, m_ref, vec_ref, wo_ref, wu_ref, wd_ref,
    gd_ref, gu_ref, go_ref, gm_ref, gmid_ref, sums_ref, gub_ref, n_ref, acc_ref,
):
    step = pl.program_id(0)

    @pl.when(step == 0)
    def _():
        n, _ = normalize(mid_ref[...])
        n_ref[...] = (n * vec_ref[1:2, :] + vec_ref[3:4, :]).astype(BF)
        acc_ref[...] = jnp.zeros_like(acc_ref)

    g = g_ref[...]
    u = raised_ref[...]
    t = gelu_parts(u)
    active = (0.5 * u * (1.0 + t)).astype(BF)
    gd_ref[...] = dot_tn(active, g).astype(BF)
    slope = 0.5 * (1.0 + t) + 0.5 * u * (1.0 - t * t) * (
        0.7978845608 * (1.0 + 3.0 * 0.044715 * (u * u))
    )
    grad_raised = (dot_nt(g, wd_ref[...]) * slope).astype(BF)
    gub_ref[0] = jnp.sum(grad_raised.astype(F32), axis=0, keepdims=True)
    gu_ref[...] = dot_tn(n_ref[...], grad_raised).astype(BF)
    acc_ref[...] += dot_nt(grad_raised, wu_ref[...])

    @pl.when(step == 3)
    def _():
        n, inverse = normalize(mid_ref[...])
        back = acc_ref[...]
        g32 = g.astype(F32)
        grad_middle = g32 + norm_back(back * vec_ref[1:2, :], n, inverse)
        gmid_ref[...] = grad_middle
        branch = grad_middle.astype(BF)
        sums_ref[...] = jnp.zeros_like(sums_ref)
        sums_ref[0:1, :] = jnp.sum(back * n, axis=0, keepdims=True)
        sums_ref[1:2, :] = jnp.sum(back, axis=0, keepdims=True)
        sums_ref[2:3, :] = jnp.sum(branch.astype(F32), axis=0, keepdims=True)
        sums_ref[3:4, :] = jnp.sum(g32, axis=0, keepdims=True)
        for p in range(4):
            go_ref[p] = dot_tn(m_ref[p], branch).astype(BF)
            gm_ref[p] = dot_nt(branch, wo_ref[p]).astype(BF)


def mlp_back(g, raised, middle, mixed, vec, wo, wu, wd):
    return pl.pallas_call(
        mlp_back_kernel,
        grid=(4,),
        out_shape=(
            sds((FF, D), BF),
            sds((D, FF), BF),
            sds((4, HL, D), BF),
            sds((4, TOK, HL), BF),
            sds((TOK, D), F32),
            sds((8, D), F32),
            sds((4, 1, D), F32),
        ),
        in_specs=[
            whole((TOK, D)),
            pl.BlockSpec((TOK, D), lambda j: (0, j)),
            whole((TOK, D)),
            whole((4, TOK, HL)),
            whole((16, D)),
            whole((4, HL, D)),
            pl.BlockSpec((D, D), lambda j: (0, j)),
            pl.BlockSpec((D, D), lambda j: (j, 0)),
        ],
        out_specs=(
            pl.BlockSpec((D, D), lambda j: (j, 0)),
            pl.BlockSpec((D, D), lambda j: (0, j)),
            whole((4, HL, D)),
            whole((4, TOK, HL)),
            whole((TOK, D)),
            whole((8, D)),
            pl.BlockSpec((1, 1, D), lambda j: (j, 0, 0)),
        ),
        scratch_shapes=[pltpu.VMEM((TOK, D), BF), pltpu.VMEM((TOK, D), F32)],
        compiler_params=BIG,
    )(g, raised, middle, mixed, vec, wo, wu, wd)


def project_back_kernel(x_ref, gp_ref, gmid_ref, vec_ref, w_ref, gw_ref, gx_ref, sums_ref, gb_ref, n_ref, acc_ref):
    step = pl.program_id(0)

    @pl.when(step == 0)
    def _():
        n, _ = normalize(x_ref[...].astype(F32))
        n_ref[...] = (n * vec_ref[0:1, :] + vec_ref[2:3, :]).astype(BF)
        acc_ref[...] = jnp.zeros_like(acc_ref)

    gp = gp_ref[0]
    gw_ref[0] = dot_tn(n_ref[...], gp).astype(BF)
    gb_ref[0] = jnp.sum(gp.astype(F32), axis=0, keepdims=True)
    acc_ref[...] += dot_nt(gp, w_ref[0])

    @pl.when(step == 3)
    def _():
        n, inverse = normalize(x_ref[...].astype(F32))
        back = acc_ref[...]
        gx_ref[...] = (gmid_ref[...] + norm_back(back * vec_ref[0:1, :], n, inverse)).astype(BF)
        sums_ref[...] = jnp.zeros_like(sums_ref)
        sums_ref[0:1, :] = jnp.sum(back * n, axis=0, keepdims=True)
        sums_ref[1:2, :] = jnp.sum(back, axis=0, keepdims=True)


def project_back(x, gp, gmid, vec, w):
    return pl.pallas_call(
        project_back_kernel,
        grid=(4,),
        out_shape=(sds((4, D, 576), BF), sds((TOK, D), BF), sds((8, D), F32), sds((4, 1, 576), F32)),
        in_specs=[
            whole((TOK, D)),
            pl.BlockSpec((1, TOK, 576), lambda j: (j, 0, 0)),
            whole((TOK, D)),
            whole((16, D)),
            pl.BlockSpec((1, D, 576), lambda j: (j, 0, 0)),
        ],
        out_specs=(
            pl.BlockSpec((1, D, 576), lambda j: (j, 0, 0)),
            whole((TOK, D)),
            whole((8, D)),
            pl.BlockSpec((1, 1, 576), lambda j: (j, 0, 0)),
        ),
        scratch_shapes=[pltpu.VMEM((TOK, D), BF), pltpu.VMEM((TOK, D), F32)],
        compiler_params=BIG,
    )(x, gp, gmid, vec, w)


def unpack_small(small):
    flat = small.reshape(64, 2048)
    rows = flat[:, :96].reshape(64, 8, 12).transpose(1, 0, 2).reshape(8, D)
    up = flat[:, 96:144].reshape(4, 1, D)
    vec = jnp.concatenate([rows, jnp.zeros((8, D), F32)])
    bias = jnp.concatenate([rows[4].reshape(4, HL), jnp.zeros((4, HL), F32), rows[5].reshape(4, HL)], axis=1)
    return vec, bias.reshape(4, 1, 576), up


def open_weights(raw):
    qkv, out, up, down, small = raw
    vec, bias, ub = unpack_small(small)
    return (
        qkv.reshape(4, D, 576),
        out.reshape(4, HL, D),
        up.reshape(D, FF),
        down.reshape(FF, D),
        vec,
        bias,
        ub,
    )


def forward(live, x, weights, previous, base_id):
    qkv, wo, wu, wd, vec, bias, ub = weights
    projected = project(x, vec, bias, qkv)
    heads4 = to_heads(live, projected.reshape(4, 4, ROWS, 576), previous[0], base_id)
    heads = heads4.reshape(SEQ_LEN, 576)
    mixed_heads, lse = attend(heads)
    mixed4 = to_tokens(live, mixed_heads.reshape(4, 4, ROWS, HL), previous[1], base_id + 1)
    mixed = mixed4.reshape(4, TOK, HL)
    result, middle, raised = mlp(x, mixed, vec, ub, wo, wu, wd)
    return result, (heads, lse, mixed, middle, raised), (heads4, mixed4)


def backward(live, g, x, weights, saved, previous, base_id):
    qkv, wo, wu, wd, vec, bias, ub = weights
    heads, lse, mixed, middle, raised = saved
    g_down, g_up, g_out, g_mixed, g_middle, sums_two, g_ub = mlp_back(
        g, raised, middle, mixed, vec, wo, wu, wd
    )
    g_heads4 = to_heads(live, g_mixed.reshape(4, 4, ROWS, HL), previous[0], base_id)
    g_split = attend_back(heads, lse, g_heads4.reshape(SEQ_LEN, HL))
    g_proj4 = to_tokens(live, g_split.reshape(4, 4, ROWS, 576), previous[1], base_id + 1)
    g_qkv, g_x, sums_one, g_bias = project_back(x, g_proj4.reshape(4, TOK, 576), g_middle, vec, qkv)
    rows = jnp.concatenate(
        [
            sums_one[0:1],
            sums_two[0:1],
            sums_one[1:2],
            sums_two[1:2],
            g_bias[:, 0, :HL].reshape(1, D),
            g_bias[:, 0, 2 * HL :].reshape(1, D),
            sums_two[2:4],
        ]
    )
    small = jnp.concatenate(
        [
            rows.reshape(8, 64, 12).transpose(1, 0, 2).reshape(64, 96),
            g_ub.reshape(64, 48),
            jnp.zeros((64, 1024 - 144), F32),
        ],
        axis=1,
    )
    grads = (
        g_qkv.reshape(4, 4, 4, 48, 576),
        g_out.reshape(4, 4, 48, D),
        g_up.reshape(4, 4, 48, FF),
        g_down.reshape(4, 4, 4, 48, D),
        small.reshape(4, 4, 4, 8, 128),
    )
    return g_x, grads, (g_heads4, g_proj4)


def per_device(ends, w_qkv, w_out, w_up, w_down, norm_gains, biases, up_bias):
    section = lax.axis_index("section")
    own = ends.reshape(TOK, D)
    qkv = w_qkv[0].reshape(12, 3, 4, HL).transpose(2, 0, 1, 3).reshape(4, 12, 576)
    small = jnp.concatenate(
        [norm_gains.reshape(-1), biases.reshape(-1), up_bias.reshape(-1), jnp.zeros((2048 - 144,), BF)]
    ).astype(F32)
    q_y, o_y, u_y, d_x, s_x = gather_first(qkv, w_out[0], w_up[0], w_down[0], small.reshape(2, 8, 128))
    first = (
        q_y.transpose(1, 0, 2, 3).reshape(4, 48, 576),
        o_y.reshape(48, D),
        u_y.reshape(48, FF),
        d_x,
        s_x,
    )
    raw = gather_rest(0, *first, None, None, 1)
    result, _, kept = forward(0, own, open_weights(raw), (None, None), 3)
    arriving = lax.ppermute(result, "section", [(0, 1)])
    token = lax.ppermute(raw[4][0, 0, 0, 0], "section", [(0, 1)])
    raw, token, _ = lax.optimization_barrier((raw, token, result))
    raw = gather_rest(1, *first, raw, token, 2)
    weights = open_weights(raw)
    x = jnp.where(section == 0, own, arriving)
    result, saved, _ = forward(1, x, weights, kept, 5)

    g_x, grads, _ = backward(1, own, x, weights, saved, (None, None), 7)
    arriving = lax.ppermute(g_x, "section", [(1, 0)])
    grads, arriving = lax.optimization_barrier((grads, arriving))
    total_one = reduce_grads(1, *grads, 11)
    total_one, arriving = lax.optimization_barrier((total_one, arriving))
    g = jnp.where(section == 1, own, arriving)
    g_x, grads, _ = backward(0, g, x, weights, saved, (None, None), 9)
    total_zero = reduce_grads(0, *grads, 12)
    q, o, u, d, s = (
        jnp.where(section == 0, zero, one) for zero, one in zip(total_zero, total_one)
    )
    flat = s.reshape(1024)
    boundary = jnp.where(section == 0, g_x, result)
    return (
        boundary.reshape(1, 1, GROUPS, ROWS, D),
        q.reshape(4, 12, 3, HL).transpose(1, 2, 0, 3).reshape(1, 12, 3 * D),
        o[None],
        u[None],
        d[None],
        flat[:24].reshape(1, 2, 12),
        flat[24:96].reshape(1, 6, 12),
        flat[96:144].reshape(1, 48),
    )


def solution(mesh):
    rows = P("section", ("seq", "shard"), None)
    columns = P("section", None, ("seq", "shard"))
    ends = P("section", "shard", None, "seq", None)
    hidden = P("section", ("seq", "shard"))
    placed = (ends, rows, rows, rows, rows, columns, columns, hidden)
    return jax.shard_map(per_device, mesh=mesh, in_specs=placed, out_specs=placed, check_vma=False)
```

```python
import functools

import jax
import jax.numpy as jnp
from jax import lax
from jax.experimental import pallas as pl
from jax.experimental.pallas import tpu as pltpu
from jax.sharding import PartitionSpec as P

HEAD = 64
FF = 3072
D = 768
GROUPS = 4
ROWS = 64
TOK = GROUPS * ROWS
SEQ_LEN = 1024
HL = 192
EPSILON = 1e-05
MASKED = -1e30
BF = jnp.bfloat16
F32 = jnp.float32
MESH = pl.DeviceIdType.MESH
HBM = pltpu.HBM


def sds(shape, dtype):
    return jax.ShapeDtypeStruct(shape, dtype)


def coords():
    shard = lax.axis_index("shard")
    return {"x": shard // 4, "y": lax.rem(shard, 4), "z": lax.axis_index("seq")}


def peer(c, axis, by):
    moved = dict(c)
    moved[axis] = lax.rem(c[axis] + by, 4)
    return {"section": lax.axis_index("section"), "seq": moved["z"], "shard": moved["x"] * 4 + moved["y"]}


def meet(c, axes, steps):
    barrier = pltpu.get_barrier_semaphore()
    for axis in axes:
        for by in steps:
            pl.semaphore_signal(barrier, inc=1, device_id=peer(c, axis, by), device_id_type=MESH)
    pl.semaphore_wait(barrier, len(axes) * len(steps))


class Copies:
    def __init__(self, send, recv):
        self.send, self.recv, self.used, self.sent = send, recv, 0, []

    def remote(self, src, dst, to):
        copy = pltpu.make_async_remote_copy(
            src_ref=src,
            dst_ref=dst,
            send_sem=self.send.at[self.used],
            recv_sem=self.recv.at[self.used],
            device_id=to,
            device_id_type=MESH,
        )
        self.used += 1
        copy.start()
        self.sent.append(copy)
        return copy

    def local(self, src, dst):
        copy = pltpu.make_async_copy(src, dst, self.send.at[self.used])
        self.used += 1
        copy.start()
        return copy

    def drain(self):
        for copy in self.sent:
            copy.wait_send()


class Gather:
    def __init__(self, copies, c, axis, own, dst, half):
        self.copies, self.c, self.axis, self.own, self.dst, self.half = copies, c, axis, own, dst, half

    def first(self):
        a = self.c[self.axis]
        self.right, self.left = peer(self.c, self.axis, 1), peer(self.c, self.axis, 3)
        self.go_right = self.copies.remote(self.own, self.dst(a), self.right)
        self.go_left = self.copies.remote(self.own, self.dst(a), self.left)

    def second(self):
        a = self.c[self.axis]
        before, after = lax.rem(a + 3, 4), lax.rem(a + 1, 4)
        self.go_right.wait_recv()
        self.on_right = self.copies.remote(self.half(before, 0), self.half(before, 0), self.right)
        self.go_left.wait_recv()
        self.on_left = self.copies.remote(self.half(after, 1), self.half(after, 1), self.left)

    def third(self):
        self.on_right.wait_recv()
        self.on_left.wait_recv()


def run_gathers(gathers):
    for g in gathers:
        g.first()
    for g in gathers:
        g.second()


def comm_call(body, live, axes, steps, count, ins, out_shapes, collective_id, aliases=None, in_vmem=0):
    n_in, n_out = len(ins), len(out_shapes)

    def kernel(*refs):
        in_refs, out_refs = refs[:n_in], refs[n_in : n_in + n_out]
        send, recv = refs[n_in + n_out :]

        def act():
            c = coords()
            meet(c, axes, steps)
            body(Copies(send, recv), c, in_refs, out_refs)

        if live is None:
            act()
        else:
            pl.when(lax.axis_index("section") == live)(act)

    return pl.pallas_call(
        kernel,
        out_shape=tuple(out_shapes),
        in_specs=[pl.BlockSpec(memory_space=pltpu.VMEM if i < in_vmem else HBM) for i in range(n_in)],
        out_specs=tuple([pl.BlockSpec(memory_space=HBM)] * n_out),
        scratch_shapes=[pltpu.SemaphoreType.DMA((count,)), pltpu.SemaphoreType.DMA((count,))],
        input_output_aliases=aliases or {},
        compiler_params=pltpu.CompilerParams(
            collective_id=collective_id, has_side_effects=True, vmem_limit_bytes=60 * 1024 * 1024
        ),
    )(*ins)


def gather_first(qkv, out, up, down, small):
    def body(copies, c, ins, outs):
        y, x = c["y"], c["x"]
        q_in, o_in, u_in, d_in, s_in = ins
        q_y, o_y, u_y, d_x, s_x = outs
        gathers = [
            Gather(copies, c, "y", u_in, lambda i: u_y.at[i], lambda i, h: u_y.at[i, :, pl.ds(1536 * h, 1536)]),
            Gather(copies, c, "y", q_in, lambda i: q_y.at[i], lambda i, h: q_y.at[i, pl.ds(2 * h, 2)]),
            Gather(copies, c, "y", o_in, lambda i: o_y.at[i], lambda i, h: o_y.at[i, :, pl.ds(384 * h, 384)]),
            Gather(copies, c, "x", d_in, lambda i: d_x.at[i], lambda i, h: d_x.at[i, :, pl.ds(384 * h, 384)]),
            Gather(copies, c, "x", s_in, lambda i: s_x.at[i], lambda i, h: s_x.at[i, h]),
        ]
        own = [
            copies.local(u_in, u_y.at[y]),
            copies.local(q_in, q_y.at[y]),
            copies.local(o_in, o_y.at[y]),
            copies.local(d_in, d_x.at[x]),
            copies.local(s_in, s_x.at[x]),
        ]
        run_gathers(gathers)
        for g in gathers:
            g.third()
        for copy in own:
            copy.wait()
        copies.drain()

    shapes = (
        sds((4, 4, 12, 576), BF),
        sds((4, 12, D), BF),
        sds((4, 12, FF), BF),
        sds((4, 48, D), BF),
        sds((4, 2, 8, 128), F32),
    )
    return comm_call(body, None, ("x", "y"), (1, 3), 25, (qkv, out, up, down, small), shapes, 0, None, 5)


def gather_rest(live, qkv, out, up, down, small, previous, token, collective_id):
    def body(copies, c, ins, outs):
        x, y, z = c["x"], c["y"], c["z"]
        q_in, o_in, u_in, d_in, s_in = ins[:5]
        q, o, u, d, s = outs
        one = [
            Gather(copies, c, "z", q_in, lambda i: q.at[:, i, x], lambda i, h: q.at[pl.ds(2 * h, 2), i, x]),
            Gather(copies, c, "z", o_in, lambda i: o.at[i, x], lambda i, h: o.at[i, x, :, pl.ds(384 * h, 384)]),
            Gather(copies, c, "x", u_in, lambda i: u.at[z, i], lambda i, h: u.at[z, i, :, pl.ds(1536 * h, 1536)]),
            Gather(copies, c, "z", d_in, lambda i: d.at[i, :, y], lambda i, h: d.at[i, pl.ds(2 * h, 2), y]),
            Gather(copies, c, "z", s_in, lambda i: s.at[i, :, y], lambda i, h: s.at[i, pl.ds(2 * h, 2), y]),
        ]
        own = [
            copies.local(q_in, q.at[:, z, x]),
            copies.local(o_in, o.at[z, x]),
            copies.local(u_in, u.at[z, x]),
            copies.local(d_in, d.at[z, :, y]),
            copies.local(s_in, s.at[z, :, y]),
        ]
        run_gathers(one)
        two = [
            Gather(copies, c, "x", q.at[:, :, x], lambda i: q.at[:, :, i], lambda i, h: q.at[pl.ds(2 * h, 2), :, i]),
            Gather(copies, c, "x", o.at[:, x], lambda i: o.at[:, i], lambda i, h: o.at[pl.ds(2 * h, 2), i]),
            Gather(copies, c, "z", u.at[z], lambda i: u.at[i], lambda i, h: u.at[i, pl.ds(2 * h, 2)]),
            Gather(copies, c, "y", d.at[:, :, y], lambda i: d.at[:, :, i], lambda i, h: d.at[pl.ds(2 * h, 2), :, i]),
            Gather(copies, c, "y", s.at[:, :, y], lambda i: s.at[:, :, i], lambda i, h: s.at[pl.ds(2 * h, 2), :, i]),
        ]
        for k in range(5):
            one[k].third()
            own[k].wait()
            two[k].first()
        for g in two:
            g.second()
        for g in two:
            g.third()
        copies.drain()

    shapes = (
        sds((4, 4, 4, 48, 576), BF),
        sds((4, 4, 48, D), BF),
        sds((4, 4, 48, FF), BF),
        sds((4, 4, 4, 48, D), BF),
        sds((4, 4, 4, 2, 8, 128), F32),
    )
    ins = (qkv, out, up, down, small)
    aliases = None
    if previous is not None:
        ins = ins + tuple(previous) + (token,)
        aliases = {5 + i: i for i in range(5)}
    return comm_call(body, live, ("x", "y", "z"), (1, 3), 45, ins, shapes, collective_id, aliases, 5)


def spread(copies, c, axis, source, target):
    moves = []
    for by in (2, 1, 3):
        there = lax.rem(c[axis] + by, 4)
        moves.append(copies.remote(source(there), target.at[by], peer(c, axis, by)))
    return moves


def arrived(moves):
    for move in moves:
        move.wait_recv()


def add(ref, at):
    total = ref[(0,) + at].astype(F32)
    for k in range(1, 4):
        total += ref[(k,) + at].astype(F32)
    return total


def more(mine, ref, at):
    total = mine.astype(F32)
    for k in range(1, 4):
        total += ref[(k,) + at].astype(F32)
    return total


def reduce_kernel(live, q_in, o_in, u_in, d_in, s_in, u_got, d_got, q, o, u, d, s, *scratch):
    qa1, qb1, o1, u1, d1, s1, qa2, qb2, o2, u2, d2, s2, tmp, qs, os, us, q3, o3, u3, d3, s3, send, recv = scratch

    def act():
        c = coords()
        x, y, z = c["x"], c["y"], c["z"]
        copies = Copies(send, recv)
        own_d = [copies.local(d_in.at[:, :, y], d1.at[0]), copies.local(d_got.at[pl.ds(1, 3)], d1.at[pl.ds(1, 3)])]
        own_u = [copies.local(u_in.at[:, x], u1.at[0]), copies.local(u_got.at[pl.ds(1, 3)], u1.at[pl.ds(1, 3)])]
        own_qa = copies.local(q_in.at[pl.ds(0, 2), :, x], qa1.at[0])
        own_qb = copies.local(q_in.at[pl.ds(2, 2), z], qb1.at[0])
        own_o = copies.local(o_in.at[:, x], o1.at[0])
        own_s = copies.local(s_in.at[:, :, y], s1.at[0])
        meet(c, ("x", "y", "z"), (1, 2, 3))
        one_qa = spread(copies, c, "x", lambda i: q_in.at[pl.ds(0, 2), :, i], qa1)
        one_qb = spread(copies, c, "z", lambda i: q_in.at[pl.ds(2, 2), i], qb1)
        one_o = spread(copies, c, "x", lambda i: o_in.at[:, i], o1)
        one_s = spread(copies, c, "y", lambda i: s_in.at[:, :, i], s1)

        def add_all(ref, rows, kind):
            @pl.loop(0, rows * 4)
            def _(i):
                at = (i // 4, lax.rem(i, 4))
                ref[(0,) + at] = add(ref, at).astype(kind)

        for copy in own_d:
            copy.wait()
        add_all(d1, 4, BF)
        two_d = spread(copies, c, "x", lambda i: d1.at[0, :, i], d2)
        for copy in own_u:
            copy.wait()

        @pl.loop(0, 4)
        def _(i):
            for k in range(4):
                at = (i, slice(None), pl.ds(D * k, D))
                u1[(0,) + at] = add(u1, at).astype(BF)

        two_u = spread(copies, c, "z", lambda i: u1.at[0, i], u2)
        arrived(one_qa)
        own_qa.wait()
        add_all(qa1, 2, BF)
        two_qa = spread(copies, c, "z", lambda i: qa1.at[0, :, i], qa2)
        arrived(one_qb)
        own_qb.wait()
        add_all(qb1, 2, BF)
        two_qb = spread(copies, c, "x", lambda i: qb1.at[0, :, i], qb2)
        arrived(one_o)
        own_o.wait()

        @pl.loop(0, 4)
        def _(i):
            o1[0, i] = add(o1, (i,)).astype(BF)

        two_o = spread(copies, c, "z", lambda i: o1.at[0, i], o2)
        arrived(one_s)
        own_s.wait()
        add_all(s1, 4, F32)
        two_s = spread(copies, c, "z", lambda i: s1.at[0, i], s2)
        arrived(two_d)

        @pl.loop(0, 4)
        def _(i):
            d2[0, i] = more(d1[0, i, x], d2, (i,)).astype(BF)

        three_d = spread(copies, c, "z", lambda i: d2.at[0, i], d3)
        arrived(two_u)
        for k in range(4):
            at = (slice(None), pl.ds(D * k, D))
            tmp[...] = more(u1[(0, z) + at], u2, at)
            for i in range(4):
                us[i, :, D * k : D * k + D] = tmp[12 * i : 12 * i + 12, :].astype(BF)
        three_u = spread(copies, c, "y", lambda i: us.at[i], u3)
        arrived(two_qa)
        arrived(two_qb)
        for p in range(4):
            if p < 2:
                tmp[:, 0:576] = more(qa1[0, p, z], qa2, (p,))
            else:
                tmp[:, 0:576] = more(qb1[0, p - 2, x], qb2, (p - 2,))
            for i in range(4):
                qs[i, p] = tmp[12 * i : 12 * i + 12, 0:576].astype(BF)
        three_q = spread(copies, c, "y", lambda i: qs.at[i], q3)
        arrived(two_o)
        tmp[...] = more(o1[0, z], o2, ())
        for i in range(4):
            os[i] = tmp[12 * i : 12 * i + 12, :].astype(BF)
        three_o = spread(copies, c, "y", lambda i: os.at[i], o3)
        arrived(two_s)

        @pl.loop(0, 4)
        def _(i):
            s2[0, i] = more(s1[0, z, i], s2, (i,))

        three_s = spread(copies, c, "x", lambda i: s2.at[0, i], s3)
        arrived(three_d)
        d[...] = more(d2[0, z], d3, ())
        arrived(three_u)
        u[...] = more(us[y], u3, ())
        arrived(three_q)
        q[...] = more(qs[y], q3, ())
        arrived(three_o)
        o[...] = more(os[y], o3, ())
        arrived(three_s)
        s[...] = more(s2[0, x], s3, ())
        copies.drain()

    pl.when(lax.axis_index("section") == live)(act)


def reduce_grads(live, qkv, out, up, down, small, up_got, down_got, collective_id):
    vmem = pltpu.VMEM
    count = 8 + 12 + 18 + 15
    return pl.pallas_call(
        functools.partial(reduce_kernel, live),
        out_shape=(
            sds((4, 12, 576), F32),
            sds((12, D), F32),
            sds((12, FF), F32),
            sds((48, D), F32),
            sds((2, 8, 128), F32),
        ),
        in_specs=[pl.BlockSpec(memory_space=HBM)] * 7,
        out_specs=tuple([pl.BlockSpec(memory_space=vmem)] * 5),
        scratch_shapes=[
            vmem((4, 2, 4, 48, 576), BF),
            vmem((4, 2, 4, 48, 576), BF),
            vmem((4, 4, 48, D), BF),
            vmem((4, 4, 48, FF), BF),
            vmem((4, 4, 4, 48, D), BF),
            vmem((4, 4, 4, 2, 8, 128), F32),
            vmem((4, 2, 48, 576), BF),
            vmem((4, 2, 48, 576), BF),
            vmem((4, 48, D), BF),
            vmem((4, 48, FF), BF),
            vmem((4, 4, 48, D), BF),
            vmem((4, 4, 2, 8, 128), F32),
            vmem((48, D), F32),
            vmem((4, 4, 12, 576), BF),
            vmem((4, 12, D), BF),
            vmem((4, 12, FF), BF),
            vmem((4, 4, 12, 576), BF),
            vmem((4, 12, D), BF),
            vmem((4, 12, FF), BF),
            vmem((4, 48, D), BF),
            vmem((4, 2, 8, 128), F32),
            pltpu.SemaphoreType.DMA((count,)),
            pltpu.SemaphoreType.DMA((count,)),
        ],
        compiler_params=pltpu.CompilerParams(
            collective_id=collective_id, has_side_effects=True, vmem_limit_bytes=60 * 1024 * 1024
        ),
    )(qkv, out, up, down, small, up_got, down_got)


BIG = pltpu.CompilerParams(vmem_limit_bytes=56 * 1024 * 1024)


def dot(a, b):
    return jnp.dot(a, b, preferred_element_type=F32)


def dot_nt(a, b):
    return lax.dot_general(a, b, (((1,), (1,)), ((), ())), preferred_element_type=F32)


def dot_tn(a, b):
    return lax.dot_general(a, b, (((0,), (0,)), ((), ())), preferred_element_type=F32)


def normalize(values):
    centered = values - jnp.mean(values, axis=-1, keepdims=True)
    spread = jnp.mean(centered * centered, axis=-1, keepdims=True)
    inverse = lax.rsqrt(spread + EPSILON)
    return centered * inverse, inverse


def norm_back(e, n, inverse):
    return inverse * (
        e - jnp.mean(e, axis=-1, keepdims=True) - n * jnp.mean(e * n, axis=-1, keepdims=True)
    )


def gelu_parts(u):
    inner = 0.7978845608 * (u + 0.044715 * (u * u * u))
    t = jnp.tanh(inner)
    return t


def whole(shape):
    zeros = (0,) * len(shape)
    return pl.BlockSpec(shape, lambda j: zeros)


def project_kernel(x_ref, vec_ref, w_ref, out_ref, n_ref, bias_ref):
    step = pl.program_id(0)

    @pl.when(step == 0)
    def _():
        n, _ = normalize(x_ref[...].astype(F32))
        n_ref[...] = (n * vec_ref[0:1, :] + vec_ref[2:3, :]).astype(BF)
        bias_ref[...] = jnp.zeros_like(bias_ref)
        for p in range(4):
            bias_ref[p, :, 0:HL] = vec_ref[4:5, HL * p : HL * p + HL]
            bias_ref[p, :, 2 * HL :] = vec_ref[5:6, HL * p : HL * p + HL]

    out_ref[0] = (dot(n_ref[...], w_ref[0]) + bias_ref[step]).astype(BF)


def project(x, vec, w):
    return pl.pallas_call(
        project_kernel,
        grid=(4,),
        out_shape=sds((4, TOK, 576), BF),
        in_specs=[
            whole((TOK, D)),
            whole((8, D)),
            pl.BlockSpec((1, D, 576), lambda j: (j, 0, 0)),
        ],
        out_specs=pl.BlockSpec((1, TOK, 576), lambda j: (j, 0, 0)),
        scratch_shapes=[pltpu.VMEM((TOK, D), BF), pltpu.VMEM((4, 1, 576), F32)],
        compiler_params=BIG,
    )(x, vec, w)


BLOCK = 256


def masked(scores, block):
    rows = block * BLOCK + lax.broadcasted_iota(jnp.int32, scores.shape, 0)
    cols = lax.broadcasted_iota(jnp.int32, scores.shape, 1)
    return jnp.where(cols <= rows, scores, MASKED)


def attend_kernel(live, with_previous, p_in, *refs):
    if with_previous:
        refs = refs[3:]
    h_out, lse_out, m_out, h_ref, m_ref, lse_ref, send, recv = refs

    def act():
        c = coords()
        z = c["z"]
        copies = Copies(send, recv)
        own = copies.local(p_in.at[z], h_ref.at[:, z])
        meet(c, ("z",), (1, 2, 3))
        coming, kept = [], []
        for g in range(GROUPS):
            for by in (2, 1, 3):
                to = peer(c, "z", by)
                coming.append(copies.remote(p_in.at[to["seq"], g], h_ref.at[g, z], to))
        own.wait()
        leaving = []
        for g in range(GROUPS):
            arrived(coming[3 * g : 3 * g + 3])
            kept.append(copies.local(h_ref.at[g], h_out.at[g]))
            keys = (g + 1) * BLOCK
            for head in range(3):
                q_at, k_at, v_at = HEAD * head, HL + HEAD * head, 2 * HL + HEAD * head
                q = h_ref[g, :, :, q_at : q_at + HEAD].reshape(BLOCK, HEAD) * jnp.asarray(0.125, BF)
                k = h_ref[0 : g + 1, :, :, k_at : k_at + HEAD].reshape(keys, HEAD)
                v = h_ref[0 : g + 1, :, :, v_at : v_at + HEAD].reshape(keys, HEAD)
                scores = masked(dot_nt(q, k), g)
                top = jnp.max(scores, axis=-1, keepdims=True)
                e = jnp.exp(scores - top)
                total = jnp.sum(e, axis=-1, keepdims=True)
                mixed = (dot(e.astype(BF), v) / total).astype(BF)
                m_ref[g, :, :, q_at : q_at + HEAD] = mixed.reshape(4, ROWS, HEAD)
                lse_ref[g, :, head : head + 1] = top + jnp.log(total)
            for by in (2, 1, 3):
                to = peer(c, "z", by)
                leaving.append(copies.remote(m_ref.at[g, to["seq"]], m_out.at[z, g], to))
            kept.append(copies.local(m_ref.at[g, z], m_out.at[z, g]))
        kept.append(copies.local(lse_ref, lse_out))
        arrived(leaving)
        for copy in kept:
            copy.wait()
        copies.drain()

    pl.when(lax.axis_index("section") == live)(act)


def attend(live, projected, previous, collective_id):
    ins, aliases = (projected,), {}
    if previous is not None:
        ins, aliases = ins + tuple(previous), {1: 0, 2: 1, 3: 2}
    count = 1 + 12 + 4 + 12 + 4 + 1
    return pl.pallas_call(
        functools.partial(attend_kernel, live, previous is not None),
        out_shape=(
            sds((4, 4, ROWS, 576), BF),
            sds((GROUPS, BLOCK, 128), F32),
            sds((4, 4, ROWS, HL), BF),
        ),
        in_specs=[pl.BlockSpec(memory_space=HBM)] * len(ins),
        out_specs=tuple([pl.BlockSpec(memory_space=HBM)] * 3),
        scratch_shapes=[
            pltpu.VMEM((4, 4, ROWS, 576), BF),
            pltpu.VMEM((4, 4, ROWS, HL), BF),
            pltpu.VMEM((GROUPS, BLOCK, 128), F32),
            pltpu.SemaphoreType.DMA((count,)),
            pltpu.SemaphoreType.DMA((count,)),
        ],
        input_output_aliases=aliases,
        compiler_params=pltpu.CompilerParams(
            collective_id=collective_id, has_side_effects=True, vmem_limit_bytes=60 * 1024 * 1024
        ),
    )(*ins)


def attend_back_kernel(
    live, g_in, h_hbm, lse_hbm, u_in, d_in, p_out, u_out, d_out, h_ref, lse_ref, gh_ref, gs_ref, dk_ref, dv_ref, send, recv
):
    def act():
        c = coords()
        z = c["z"]
        copies = Copies(send, recv)
        own = [
            copies.local(g_in.at[z], gh_ref.at[:, z]),
            copies.local(h_hbm, h_ref),
            copies.local(lse_hbm, lse_ref),
        ]
        meet(c, ("x", "y", "z"), (1, 2, 3))
        coming, leaving, kept = {}, [], []
        for g in reversed(range(GROUPS)):
            coming[g] = []
            for by in (2, 1, 3):
                to = peer(c, "z", by)
                coming[g].append(copies.remote(g_in.at[to["seq"], g], gh_ref.at[g, z], to))
        weights = spread(copies, c, "y", lambda i: d_in.at[:, :, i], d_out)
        weights += spread(copies, c, "x", lambda i: u_in.at[:, i], u_out)
        for copy in own:
            copy.wait()
        for g in reversed(range(GROUPS)):
            arrived(coming[g])
            keys = (g + 1) * BLOCK
            for head in range(3):
                q_at, k_at, v_at = HEAD * head, HL + HEAD * head, 2 * HL + HEAD * head
                q = h_ref[g, :, :, q_at : q_at + HEAD].reshape(BLOCK, HEAD) * jnp.asarray(0.125, BF)
                k = h_ref[0 : g + 1, :, :, k_at : k_at + HEAD].reshape(keys, HEAD)
                v = h_ref[0 : g + 1, :, :, v_at : v_at + HEAD].reshape(keys, HEAD)
                grad = gh_ref[g, :, :, q_at : q_at + HEAD].reshape(BLOCK, HEAD)
                scores = masked(dot_nt(q, k), g)
                p = jnp.exp(scores - lse_ref[g, :, head : head + 1])
                dp = dot_nt(grad, v)
                centre = jnp.sum(p * dp, axis=-1, keepdims=True)
                ds = (p * (dp - centre)).astype(BF)
                dq = (dot(ds, k) * 0.125).astype(BF)
                gs_ref[g, :, :, q_at : q_at + HEAD] = dq.reshape(4, ROWS, HEAD)
                dk = dot_tn(ds, q)
                dv = dot_tn(p.astype(BF), grad)
                if g < GROUPS - 1:
                    dk += dk_ref[head, 0:keys, :]
                    dv += dv_ref[head, 0:keys, :]
                if g > 0:
                    dk_ref[head, 0 : keys - BLOCK, :] = dk[: keys - BLOCK]
                    dv_ref[head, 0 : keys - BLOCK, :] = dv[: keys - BLOCK]
                gs_ref[g, :, :, k_at : k_at + HEAD] = dk[keys - BLOCK :].astype(BF).reshape(4, ROWS, HEAD)
                gs_ref[g, :, :, v_at : v_at + HEAD] = dv[keys - BLOCK :].astype(BF).reshape(4, ROWS, HEAD)
            for by in (2, 1, 3):
                to = peer(c, "z", by)
                leaving.append(copies.remote(gs_ref.at[g, to["seq"]], p_out.at[z, g], to))
            kept.append(copies.local(gs_ref.at[g, z], p_out.at[z, g]))
        arrived(leaving)
        for copy in kept:
            copy.wait()
        arrived(weights)
        copies.drain()

    pl.when(lax.axis_index("section") == live)(act)


def attend_back(live, grads, heads, lse, up, down, collective_id):
    count = 3 + 12 + 6 + 12 + 4
    return pl.pallas_call(
        functools.partial(attend_back_kernel, live),
        out_shape=(
            sds((4, 4, ROWS, 576), BF),
            sds((4, 4, 48, FF), BF),
            sds((4, 4, 4, 48, D), BF),
        ),
        in_specs=[pl.BlockSpec(memory_space=HBM)] * 5,
        out_specs=tuple([pl.BlockSpec(memory_space=HBM)] * 3),
        scratch_shapes=[
            pltpu.VMEM((4, 4, ROWS, 576), BF),
            pltpu.VMEM((GROUPS, BLOCK, 128), F32),
            pltpu.VMEM((4, 4, ROWS, HL), BF),
            pltpu.VMEM((4, 4, ROWS, 576), BF),
            pltpu.VMEM((3, SEQ_LEN, HEAD), F32),
            pltpu.VMEM((3, SEQ_LEN, HEAD), F32),
            pltpu.SemaphoreType.DMA((count,)),
            pltpu.SemaphoreType.DMA((count,)),
        ],
        compiler_params=pltpu.CompilerParams(
            collective_id=collective_id, has_side_effects=True, vmem_limit_bytes=60 * 1024 * 1024
        ),
    )(grads, heads, lse, up, down)


def mlp_kernel(x_ref, m_ref, vec_ref, ub_ref, wo_ref, wu_ref, wd_ref, res_ref, mid_ref, raised_ref, n_ref, acc_ref):
    step = pl.program_id(0)

    @pl.when(step == 0)
    def _():
        branch = dot(m_ref[0], wo_ref[0])
        for p in range(1, 4):
            branch += dot(m_ref[p], wo_ref[p])
        middle = x_ref[...].astype(F32) + (branch + vec_ref[6:7, :])
        mid_ref[...] = middle
        n, _ = normalize(middle)
        n_ref[...] = (n * vec_ref[1:2, :] + vec_ref[3:4, :]).astype(BF)
        acc_ref[...] = middle + vec_ref[7:8, :]

    raised = dot(n_ref[...], wu_ref[...]) + ub_ref[0]
    raised_ref[...] = raised
    active = (0.5 * raised * (1.0 + gelu_parts(raised))).astype(BF)
    acc_ref[...] += dot(active, wd_ref[...])

    @pl.when(step == 3)
    def _():
        res_ref[...] = acc_ref[...].astype(BF)


def mlp(x, mixed, vec, ub, wo, wu, wd):
    return pl.pallas_call(
        mlp_kernel,
        grid=(4,),
        out_shape=(sds((TOK, D), BF), sds((TOK, D), F32), sds((TOK, FF), F32)),
        in_specs=[
            whole((TOK, D)),
            whole((4, TOK, HL)),
            whole((8, D)),
            pl.BlockSpec((1, 1, D), lambda j: (j, 0, 0)),
            whole((4, HL, D)),
            pl.BlockSpec((D, D), lambda j: (0, j)),
            pl.BlockSpec((D, D), lambda j: (j, 0)),
        ],
        out_specs=(whole((TOK, D)), whole((TOK, D)), pl.BlockSpec((TOK, D), lambda j: (0, j))),
        scratch_shapes=[pltpu.VMEM((TOK, D), BF), pltpu.VMEM((TOK, D), F32)],
        compiler_params=BIG,
    )(x, mixed, vec, ub, wo, wu, wd)


def mlp_back_kernel(
    g_ref, raised_ref, mid_ref, m_ref, vec_ref, wo_ref, wu_ref, wd_ref,
    gd_ref, gu_ref, go_ref, gm_ref, gmid_ref, sums_ref, gub_ref, n_ref, acc_ref,
):
    step = pl.program_id(0)

    @pl.when(step == 0)
    def _():
        n, _ = normalize(mid_ref[...])
        n_ref[...] = (n * vec_ref[1:2, :] + vec_ref[3:4, :]).astype(BF)
        acc_ref[...] = jnp.zeros_like(acc_ref)

    g = g_ref[...]
    u = raised_ref[...]
    t = gelu_parts(u)
    active = (0.5 * u * (1.0 + t)).astype(BF)
    gd_ref[...] = dot_tn(active, g).astype(BF)
    slope = 0.5 * (1.0 + t) + 0.5 * u * (1.0 - t * t) * (
        0.7978845608 * (1.0 + 3.0 * 0.044715 * (u * u))
    )
    grad_raised = (dot_nt(g, wd_ref[...]) * slope).astype(BF)
    gub_ref[0] = jnp.sum(grad_raised.astype(F32), axis=0, keepdims=True)
    gu_ref[...] = dot_tn(n_ref[...], grad_raised).astype(BF)
    acc_ref[...] += dot_nt(grad_raised, wu_ref[...])

    @pl.when(step == 3)
    def _():
        n, inverse = normalize(mid_ref[...])
        back = acc_ref[...]
        g32 = g.astype(F32)
        grad_middle = g32 + norm_back(back * vec_ref[1:2, :], n, inverse)
        gmid_ref[...] = grad_middle
        branch = grad_middle.astype(BF)
        sums_ref[...] = jnp.zeros_like(sums_ref)
        sums_ref[0:1, :] = jnp.sum(back * n, axis=0, keepdims=True)
        sums_ref[1:2, :] = jnp.sum(back, axis=0, keepdims=True)
        sums_ref[2:3, :] = jnp.sum(branch.astype(F32), axis=0, keepdims=True)
        sums_ref[3:4, :] = jnp.sum(g32, axis=0, keepdims=True)
        for p in range(4):
            go_ref[p] = dot_tn(m_ref[p], branch).astype(BF)
            gm_ref[p] = dot_nt(branch, wo_ref[p]).astype(BF)


def mlp_back(g, raised, middle, mixed, vec, wo, wu, wd):
    return pl.pallas_call(
        mlp_back_kernel,
        grid=(4,),
        out_shape=(
            sds((FF, D), BF),
            sds((D, FF), BF),
            sds((4, HL, D), BF),
            sds((4, TOK, HL), BF),
            sds((TOK, D), F32),
            sds((8, D), F32),
            sds((4, 1, D), F32),
        ),
        in_specs=[
            whole((TOK, D)),
            pl.BlockSpec((TOK, D), lambda j: (0, j)),
            whole((TOK, D)),
            whole((4, TOK, HL)),
            whole((8, D)),
            whole((4, HL, D)),
            pl.BlockSpec((D, D), lambda j: (0, j)),
            pl.BlockSpec((D, D), lambda j: (j, 0)),
        ],
        out_specs=(
            pl.BlockSpec((D, D), lambda j: (j, 0)),
            pl.BlockSpec((D, D), lambda j: (0, j)),
            whole((4, HL, D)),
            whole((4, TOK, HL)),
            whole((TOK, D)),
            whole((8, D)),
            pl.BlockSpec((1, 1, D), lambda j: (j, 0, 0)),
        ),
        scratch_shapes=[pltpu.VMEM((TOK, D), BF), pltpu.VMEM((TOK, D), F32)],
        compiler_params=BIG,
    )(g, raised, middle, mixed, vec, wo, wu, wd)


def project_back_kernel(
    x_ref, gp_ref, gmid_ref, vec_ref, w_ref, sums_two_ref, gw_ref, gx_ref, sums_ref, n_ref, acc_ref, gb_ref
):
    step = pl.program_id(0)

    @pl.when(step == 0)
    def _():
        n, _ = normalize(x_ref[...].astype(F32))
        n_ref[...] = (n * vec_ref[0:1, :] + vec_ref[2:3, :]).astype(BF)
        acc_ref[...] = jnp.zeros_like(acc_ref)

    gp = gp_ref[0]
    gw_ref[0] = dot_tn(n_ref[...], gp).astype(BF)
    gb_ref[step] = jnp.sum(gp.astype(F32), axis=0, keepdims=True)
    acc_ref[...] += dot_nt(gp, w_ref[0])

    @pl.when(step == 3)
    def _():
        n, inverse = normalize(x_ref[...].astype(F32))
        back = acc_ref[...]
        gx_ref[...] = (gmid_ref[...] + norm_back(back * vec_ref[0:1, :], n, inverse)).astype(BF)
        sums_ref[0:1, :] = jnp.sum(back * n, axis=0, keepdims=True)
        sums_ref[1:2, :] = sums_two_ref[0:1, :]
        sums_ref[2:3, :] = jnp.sum(back, axis=0, keepdims=True)
        sums_ref[3:4, :] = sums_two_ref[1:2, :]
        for p in range(4):
            sums_ref[4:5, HL * p : HL * p + HL] = gb_ref[p, :, 0:HL]
            sums_ref[5:6, HL * p : HL * p + HL] = gb_ref[p, :, 2 * HL :]
        sums_ref[6:8, :] = sums_two_ref[2:4, :]


def project_back(x, gp, gmid, vec, w, sums_two):
    return pl.pallas_call(
        project_back_kernel,
        grid=(4,),
        out_shape=(sds((4, D, 576), BF), sds((TOK, D), BF), sds((8, D), F32)),
        in_specs=[
            whole((TOK, D)),
            pl.BlockSpec((1, TOK, 576), lambda j: (j, 0, 0)),
            whole((TOK, D)),
            whole((8, D)),
            pl.BlockSpec((1, D, 576), lambda j: (j, 0, 0)),
            whole((8, D)),
        ],
        out_specs=(
            pl.BlockSpec((1, D, 576), lambda j: (j, 0, 0)),
            whole((TOK, D)),
            whole((8, D)),
        ),
        scratch_shapes=[
            pltpu.VMEM((TOK, D), BF),
            pltpu.VMEM((TOK, D), F32),
            pltpu.VMEM((4, 1, 576), F32),
        ],
        compiler_params=BIG,
    )(x, gp, gmid, vec, w, sums_two)


def tile(rows):
    pads = [(0, 0)] * (rows.ndim - 2) + [(0, 8 - rows.shape[-2]), (0, 128 - rows.shape[-1])]
    return jnp.pad(rows, pads)


def open_weights(raw):
    qkv, out, up, down, small = raw
    small = small.reshape(64, 2, 8, 128)
    vec = small[:, 0, :, :12].transpose(1, 0, 2).reshape(8, D)
    ub = small[:, 1, 0, :48].reshape(4, 1, D)
    return (
        qkv.reshape(4, D, 576),
        out.reshape(4, HL, D),
        up.reshape(D, FF),
        down.reshape(FF, D),
        vec,
        ub,
    )


def forward(live, x, weights, previous, base_id):
    qkv, wo, wu, wd, vec, ub = weights
    projected = project(x, vec, qkv)
    kept = attend(live, projected.reshape(4, 4, ROWS, 576), previous, base_id)
    mixed = kept[2].reshape(4, TOK, HL)
    result, middle, raised = mlp(x, mixed, vec, ub, wo, wu, wd)
    return result, (mixed, middle, raised), kept


def backward(live, g, x, weights, saved, kept, base_id):
    qkv, wo, wu, wd, vec, ub = weights
    mixed, middle, raised = saved
    g_down, g_up, g_out, g_mixed, g_middle, sums_two, g_ub = mlp_back(
        g, raised, middle, mixed, vec, wo, wu, wd
    )
    g_up = g_up.reshape(4, 4, 48, FF)
    g_down = g_down.reshape(4, 4, 4, 48, D)
    g_proj, up_got, down_got = attend_back(
        live, g_mixed.reshape(4, 4, ROWS, HL), kept[0], kept[1], g_up, g_down, base_id
    )
    g_qkv, g_x, sums = project_back(x, g_proj.reshape(4, TOK, 576), g_middle, vec, qkv, sums_two)
    small = jnp.stack(
        [tile(sums.reshape(8, 64, 12).transpose(1, 0, 2)), tile(g_ub.reshape(64, 1, 48))], axis=1
    )
    grads = (
        g_qkv.reshape(4, 4, 4, 48, 576),
        g_out.reshape(4, 4, 48, D),
        g_up,
        g_down,
        small.reshape(4, 4, 4, 2, 8, 128),
        up_got,
        down_got,
    )
    return g_x, grads


def per_device(ends, w_qkv, w_out, w_up, w_down, norm_gains, biases, up_bias):
    section = lax.axis_index("section")
    own = ends.reshape(TOK, D)
    qkv = w_qkv[0].reshape(12, 3, 4, HL).transpose(2, 0, 1, 3).reshape(4, 12, 576)
    small = jnp.stack([tile(jnp.concatenate([norm_gains[0], biases[0]])), tile(up_bias)]).astype(F32)
    q_y, o_y, u_y, d_x, s_x = gather_first(qkv, w_out[0], w_up[0], w_down[0], small)
    first = (
        q_y.transpose(1, 0, 2, 3).reshape(4, 48, 576),
        o_y.reshape(48, D),
        u_y.reshape(48, FF),
        d_x,
        s_x,
    )
    raw = gather_rest(0, *first, None, None, 1)
    result, _, kept = forward(0, own, open_weights(raw), None, 3)
    arriving = lax.ppermute(result, "section", [(0, 1)])
    token = lax.ppermute(raw[4][0, 0, 0, 0], "section", [(0, 1)])
    raw, token, _ = lax.optimization_barrier((raw, token, result))
    raw = gather_rest(1, *first, raw, token, 2)
    weights = open_weights(raw)
    x = jnp.where(section == 0, own, arriving)
    result, saved, kept = forward(1, x, weights, kept, 4)

    g_x, grads = backward(1, own, x, weights, saved, kept, 5)
    arriving = lax.ppermute(g_x, "section", [(1, 0)])
    grads, arriving = lax.optimization_barrier((grads, arriving))
    total_one = reduce_grads(1, *grads, 7)
    total_one, arriving = lax.optimization_barrier((total_one, arriving))
    g = jnp.where(section == 1, own, arriving)
    g_x, grads = backward(0, g, x, weights, saved, kept, 6)
    total_zero = reduce_grads(0, *grads, 8)
    q, o, u, d, s = (
        jnp.where(section == 0, zero, one) for zero, one in zip(total_zero, total_one)
    )
    boundary = jnp.where(section == 0, g_x, result)
    return (
        boundary.reshape(1, 1, GROUPS, ROWS, D),
        q.reshape(4, 12, 3, HL).transpose(1, 2, 0, 3).reshape(1, 12, 3 * D),
        o[None],
        u[None],
        d[None],
        s[0:1, 0:2, :12],
        s[0:1, 2:8, :12],
        s[1:2, 0, :48],
    )


def solution(mesh):
    rows = P("section", ("seq", "shard"), None)
    columns = P("section", None, ("seq", "shard"))
    ends = P("section", "shard", None, "seq", None)
    hidden = P("section", ("seq", "shard"))
    placed = (ends, rows, rows, rows, rows, columns, columns, hidden)
    return jax.shard_map(per_device, mesh=mesh, in_specs=placed, out_specs=placed, check_vma=False)
```

```python
import functools

import jax
import jax.numpy as jnp
from jax import lax
from jax.experimental import pallas as pl
from jax.experimental.pallas import tpu as pltpu
from jax.sharding import PartitionSpec as P

HEAD = 64
FF = 3072
D = 768
GROUPS = 4
ROWS = 64
TOK = GROUPS * ROWS
SEQ_LEN = 1024
HL = 192
EPSILON = 1e-05
MASKED = -1e30
BF = jnp.bfloat16
F32 = jnp.float32
MESH = pl.DeviceIdType.MESH
HBM = pltpu.HBM


def sds(shape, dtype):
    return jax.ShapeDtypeStruct(shape, dtype)


def coords():
    shard = lax.axis_index("shard")
    return {"x": shard // 4, "y": lax.rem(shard, 4), "z": lax.axis_index("seq")}


def peer(c, axis, by):
    moved = dict(c)
    moved[axis] = lax.rem(c[axis] + by, 4)
    return {"section": lax.axis_index("section"), "seq": moved["z"], "shard": moved["x"] * 4 + moved["y"]}


def partner():
    return {
        "section": 1 - lax.axis_index("section"),
        "seq": lax.axis_index("seq"),
        "shard": lax.axis_index("shard"),
    }


def meet(c, axes, steps, with_partner=False):
    barrier = pltpu.get_barrier_semaphore()
    if with_partner:
        pl.semaphore_signal(barrier, inc=1, device_id=partner(), device_id_type=MESH)
    for axis in axes:
        for by in steps:
            pl.semaphore_signal(barrier, inc=1, device_id=peer(c, axis, by), device_id_type=MESH)
    pl.semaphore_wait(barrier, len(axes) * len(steps) + int(with_partner))


class Copies:
    def __init__(self, send, recv):
        self.send, self.recv, self.used, self.sent = send, recv, 0, []

    def remote(self, src, dst, to):
        copy = pltpu.make_async_remote_copy(
            src_ref=src,
            dst_ref=dst,
            send_sem=self.send.at[self.used],
            recv_sem=self.recv.at[self.used],
            device_id=to,
            device_id_type=MESH,
        )
        self.used += 1
        copy.start()
        self.sent.append(copy)
        return copy

    def local(self, src, dst):
        copy = pltpu.make_async_copy(src, dst, self.send.at[self.used])
        self.used += 1
        copy.start()
        return copy

    def drain(self):
        for copy in self.sent:
            copy.wait_send()


class Gather:
    def __init__(self, copies, c, axis, own, dst, half):
        self.copies, self.c, self.axis, self.own, self.dst, self.half = copies, c, axis, own, dst, half

    def first(self):
        a = self.c[self.axis]
        self.right, self.left = peer(self.c, self.axis, 1), peer(self.c, self.axis, 3)
        self.go_right = self.copies.remote(self.own, self.dst(a), self.right)
        self.go_left = self.copies.remote(self.own, self.dst(a), self.left)

    def second(self):
        a = self.c[self.axis]
        before, after = lax.rem(a + 3, 4), lax.rem(a + 1, 4)
        self.go_right.wait_recv()
        self.on_right = self.copies.remote(self.half(before, 0), self.half(before, 0), self.right)
        self.go_left.wait_recv()
        self.on_left = self.copies.remote(self.half(after, 1), self.half(after, 1), self.left)

    def third(self):
        self.on_right.wait_recv()
        self.on_left.wait_recv()


def run_gathers(gathers):
    for g in gathers:
        g.first()
    for g in gathers:
        g.second()


def comm_call(body, in_turn, axes, count, ins, out_shapes, collective_id):
    n_in, n_out = len(ins), len(out_shapes)

    def kernel(*refs):
        in_refs, out_refs = refs[:n_in], refs[n_in : n_in + n_out]
        send, recv, turn = refs[n_in + n_out :]
        c = coords()
        meet(c, axes, (1, 3), in_turn)
        body(Copies(send, recv), c, in_refs, out_refs, turn)

    return pl.pallas_call(
        kernel,
        out_shape=tuple(out_shapes),
        in_specs=[pl.BlockSpec(memory_space=pltpu.VMEM)] * n_in,
        out_specs=tuple([pl.BlockSpec(memory_space=HBM)] * n_out),
        scratch_shapes=[
            pltpu.SemaphoreType.DMA((count,)),
            pltpu.SemaphoreType.DMA((count,)),
            pltpu.SemaphoreType.REGULAR,
        ],
        compiler_params=pltpu.CompilerParams(
            collective_id=collective_id, has_side_effects=True, vmem_limit_bytes=60 * 1024 * 1024
        ),
    )(*ins)


def gather_first(qkv, out, up, down, small):
    def body(copies, c, ins, outs, turn):
        y, x = c["y"], c["x"]
        q_in, o_in, u_in, d_in, s_in = ins
        q_y, o_y, u_y, d_x, s_x = outs
        gathers = [
            Gather(copies, c, "y", u_in, lambda i: u_y.at[i], lambda i, h: u_y.at[i, :, pl.ds(1536 * h, 1536)]),
            Gather(copies, c, "y", q_in, lambda i: q_y.at[i], lambda i, h: q_y.at[i, pl.ds(2 * h, 2)]),
            Gather(copies, c, "y", o_in, lambda i: o_y.at[i], lambda i, h: o_y.at[i, :, pl.ds(384 * h, 384)]),
            Gather(copies, c, "x", d_in, lambda i: d_x.at[i], lambda i, h: d_x.at[i, :, pl.ds(384 * h, 384)]),
            Gather(copies, c, "x", s_in, lambda i: s_x.at[i], lambda i, h: s_x.at[i, h]),
        ]
        own = [
            copies.local(u_in, u_y.at[y]),
            copies.local(q_in, q_y.at[y]),
            copies.local(o_in, o_y.at[y]),
            copies.local(d_in, d_x.at[x]),
            copies.local(s_in, s_x.at[x]),
        ]
        run_gathers(gathers)
        for g in gathers:
            g.third()
        for copy in own:
            copy.wait()
        copies.drain()

    shapes = (
        sds((4, 4, 12, 576), BF),
        sds((4, 12, D), BF),
        sds((4, 12, FF), BF),
        sds((4, 48, D), BF),
        sds((4, 2, 8, 128), F32),
    )
    return comm_call(body, False, ("x", "y"), 25, (qkv, out, up, down, small), shapes, 0)


def gather_rest(qkv, out, up, down, small):
    def body(copies, c, ins, outs, turn):
        x, y, z = c["x"], c["y"], c["z"]
        q_in, o_in, u_in, d_in, s_in = ins
        q, o, u, d, s = outs
        one = [
            Gather(copies, c, "z", q_in, lambda i: q.at[:, i, x], lambda i, h: q.at[pl.ds(2 * h, 2), i, x]),
            Gather(copies, c, "z", o_in, lambda i: o.at[i, x], lambda i, h: o.at[i, x, :, pl.ds(384 * h, 384)]),
            Gather(copies, c, "x", u_in, lambda i: u.at[z, i], lambda i, h: u.at[z, i, :, pl.ds(1536 * h, 1536)]),
            Gather(copies, c, "z", d_in, lambda i: d.at[i, :, y], lambda i, h: d.at[i, pl.ds(2 * h, 2), y]),
            Gather(copies, c, "z", s_in, lambda i: s.at[i, :, y], lambda i, h: s.at[i, pl.ds(2 * h, 2), y]),
        ]
        own = [
            copies.local(q_in, q.at[:, z, x]),
            copies.local(o_in, o.at[z, x]),
            copies.local(u_in, u.at[z, x]),
            copies.local(d_in, d.at[z, :, y]),
            copies.local(s_in, s.at[z, :, y]),
        ]
        @pl.when(lax.axis_index("section") == 1)
        def _():
            pl.semaphore_wait(turn, 1)

        run_gathers(one)
        two = [
            Gather(copies, c, "x", q.at[:, :, x], lambda i: q.at[:, :, i], lambda i, h: q.at[pl.ds(2 * h, 2), :, i]),
            Gather(copies, c, "x", o.at[:, x], lambda i: o.at[:, i], lambda i, h: o.at[pl.ds(2 * h, 2), i]),
            Gather(copies, c, "z", u.at[z], lambda i: u.at[i], lambda i, h: u.at[i, pl.ds(2 * h, 2)]),
            Gather(copies, c, "y", d.at[:, :, y], lambda i: d.at[:, :, i], lambda i, h: d.at[pl.ds(2 * h, 2), :, i]),
            Gather(copies, c, "y", s.at[:, :, y], lambda i: s.at[:, :, i], lambda i, h: s.at[pl.ds(2 * h, 2), :, i]),
        ]
        for k in range(5):
            one[k].third()
            own[k].wait()
            two[k].first()
        for g in two:
            g.second()

        @pl.when(lax.axis_index("section") == 0)
        def _():
            pl.semaphore_signal(turn, inc=1, device_id=partner(), device_id_type=MESH)

        for g in two:
            g.third()
        copies.drain()

    shapes = (
        sds((4, 4, 4, 48, 576), BF),
        sds((4, 4, 48, D), BF),
        sds((4, 4, 48, FF), BF),
        sds((4, 4, 4, 48, D), BF),
        sds((4, 4, 4, 2, 8, 128), F32),
    )
    return comm_call(body, True, ("x", "y", "z"), 45, (qkv, out, up, down, small), shapes, 1)


def spread(copies, c, axis, source, target):
    moves = []
    for by in (2, 1, 3):
        there = lax.rem(c[axis] + by, 4)
        moves.append(copies.remote(source(there), target.at[by], peer(c, axis, by)))
    return moves


def arrived(moves):
    for move in moves:
        move.wait_recv()


def add(ref, at):
    total = ref[(0,) + at].astype(F32)
    for k in range(1, 4):
        total += ref[(k,) + at].astype(F32)
    return total


def more(mine, ref, at):
    total = mine.astype(F32)
    for k in range(1, 4):
        total += ref[(k,) + at].astype(F32)
    return total


def reduce_kernel(live, q_in, o_in, u_in, d_in, s_in, u_got, d_got, q, o, u, d, s, *scratch):
    qa1, qb1, o1, u1, d1, s1, qa2, qb2, o2, u2, d2, s2, tmp, qs, os, us, q3, o3, u3, d3, s3, send, recv = scratch

    def act():
        c = coords()
        x, y, z = c["x"], c["y"], c["z"]
        copies = Copies(send, recv)
        own_d = [copies.local(d_in.at[:, :, y], d1.at[0]), copies.local(d_got.at[pl.ds(1, 3)], d1.at[pl.ds(1, 3)])]
        own_u = [copies.local(u_in.at[:, x], u1.at[0]), copies.local(u_got.at[pl.ds(1, 3)], u1.at[pl.ds(1, 3)])]
        own_qa = copies.local(q_in.at[pl.ds(0, 2), :, x], qa1.at[0])
        own_qb = copies.local(q_in.at[pl.ds(2, 2), z], qb1.at[0])
        own_o = copies.local(o_in.at[:, x], o1.at[0])
        own_s = copies.local(s_in.at[:, :, y], s1.at[0])
        meet(c, ("x", "y", "z"), (1, 2, 3))
        one_qa = spread(copies, c, "x", lambda i: q_in.at[pl.ds(0, 2), :, i], qa1)
        one_qb = spread(copies, c, "z", lambda i: q_in.at[pl.ds(2, 2), i], qb1)
        one_o = spread(copies, c, "x", lambda i: o_in.at[:, i], o1)
        one_s = spread(copies, c, "y", lambda i: s_in.at[:, :, i], s1)

        def add_all(ref, rows, kind):
            @pl.loop(0, rows * 4)
            def _(i):
                at = (i // 4, lax.rem(i, 4))
                ref[(0,) + at] = add(ref, at).astype(kind)

        for copy in own_d:
            copy.wait()
        add_all(d1, 4, BF)
        two_d = spread(copies, c, "x", lambda i: d1.at[0, :, i], d2)
        for copy in own_u:
            copy.wait()

        @pl.loop(0, 4)
        def _(i):
            for k in range(4):
                at = (i, slice(None), pl.ds(D * k, D))
                u1[(0,) + at] = add(u1, at).astype(BF)

        two_u = spread(copies, c, "z", lambda i: u1.at[0, i], u2)
        arrived(one_qa)
        own_qa.wait()
        add_all(qa1, 2, BF)
        two_qa = spread(copies, c, "z", lambda i: qa1.at[0, :, i], qa2)
        arrived(one_qb)
        own_qb.wait()
        add_all(qb1, 2, BF)
        two_qb = spread(copies, c, "x", lambda i: qb1.at[0, :, i], qb2)
        arrived(one_o)
        own_o.wait()

        @pl.loop(0, 4)
        def _(i):
            o1[0, i] = add(o1, (i,)).astype(BF)

        two_o = spread(copies, c, "z", lambda i: o1.at[0, i], o2)
        arrived(one_s)
        own_s.wait()
        add_all(s1, 4, F32)
        two_s = spread(copies, c, "z", lambda i: s1.at[0, i], s2)
        arrived(two_d)

        @pl.loop(0, 4)
        def _(i):
            d2[0, i] = more(d1[0, i, x], d2, (i,)).astype(BF)

        three_d = spread(copies, c, "z", lambda i: d2.at[0, i], d3)
        arrived(two_u)
        for k in range(4):
            at = (slice(None), pl.ds(D * k, D))
            tmp[...] = more(u1[(0, z) + at], u2, at)
            for i in range(4):
                us[i, :, D * k : D * k + D] = tmp[12 * i : 12 * i + 12, :].astype(BF)
        three_u = spread(copies, c, "y", lambda i: us.at[i], u3)
        arrived(two_qa)
        arrived(two_qb)
        for p in range(4):
            if p < 2:
                tmp[:, 0:576] = more(qa1[0, p, z], qa2, (p,))
            else:
                tmp[:, 0:576] = more(qb1[0, p - 2, x], qb2, (p - 2,))
            for i in range(4):
                qs[i, p] = tmp[12 * i : 12 * i + 12, 0:576].astype(BF)
        three_q = spread(copies, c, "y", lambda i: qs.at[i], q3)
        arrived(two_o)
        tmp[...] = more(o1[0, z], o2, ())
        for i in range(4):
            os[i] = tmp[12 * i : 12 * i + 12, :].astype(BF)
        three_o = spread(copies, c, "y", lambda i: os.at[i], o3)
        arrived(two_s)

        @pl.loop(0, 4)
        def _(i):
            s2[0, i] = more(s1[0, z, i], s2, (i,))

        three_s = spread(copies, c, "x", lambda i: s2.at[0, i], s3)
        arrived(three_d)
        d[...] = more(d2[0, z], d3, ())
        arrived(three_u)
        u[...] = more(us[y], u3, ())
        arrived(three_q)
        q[...] = more(qs[y], q3, ())
        arrived(three_o)
        o[...] = more(os[y], o3, ())
        arrived(three_s)
        s[...] = more(s2[0, x], s3, ())
        copies.drain()

    pl.when(lax.axis_index("section") == live)(act)


def reduce_grads(live, qkv, out, up, down, small, up_got, down_got, collective_id):
    vmem = pltpu.VMEM
    count = 8 + 12 + 18 + 15
    return pl.pallas_call(
        functools.partial(reduce_kernel, live),
        out_shape=(
            sds((4, 12, 576), F32),
            sds((12, D), F32),
            sds((12, FF), F32),
            sds((48, D), F32),
            sds((2, 8, 128), F32),
        ),
        in_specs=[pl.BlockSpec(memory_space=HBM)] * 7,
        out_specs=tuple([pl.BlockSpec(memory_space=vmem)] * 5),
        scratch_shapes=[
            vmem((4, 2, 4, 48, 576), BF),
            vmem((4, 2, 4, 48, 576), BF),
            vmem((4, 4, 48, D), BF),
            vmem((4, 4, 48, FF), BF),
            vmem((4, 4, 4, 48, D), BF),
            vmem((4, 4, 4, 2, 8, 128), F32),
            vmem((4, 2, 48, 576), BF),
            vmem((4, 2, 48, 576), BF),
            vmem((4, 48, D), BF),
            vmem((4, 48, FF), BF),
            vmem((4, 4, 48, D), BF),
            vmem((4, 4, 2, 8, 128), F32),
            vmem((48, D), F32),
            vmem((4, 4, 12, 576), BF),
            vmem((4, 12, D), BF),
            vmem((4, 12, FF), BF),
            vmem((4, 4, 12, 576), BF),
            vmem((4, 12, D), BF),
            vmem((4, 12, FF), BF),
            vmem((4, 48, D), BF),
            vmem((4, 2, 8, 128), F32),
            pltpu.SemaphoreType.DMA((count,)),
            pltpu.SemaphoreType.DMA((count,)),
        ],
        compiler_params=pltpu.CompilerParams(
            collective_id=collective_id, has_side_effects=True, vmem_limit_bytes=60 * 1024 * 1024
        ),
    )(qkv, out, up, down, small, up_got, down_got)


BIG = pltpu.CompilerParams(vmem_limit_bytes=56 * 1024 * 1024)


def dot(a, b):
    return jnp.dot(a, b, preferred_element_type=F32)


def dot_nt(a, b):
    return lax.dot_general(a, b, (((1,), (1,)), ((), ())), preferred_element_type=F32)


def dot_tn(a, b):
    return lax.dot_general(a, b, (((0,), (0,)), ((), ())), preferred_element_type=F32)


def normalize(values):
    centered = values - jnp.mean(values, axis=-1, keepdims=True)
    spread = jnp.mean(centered * centered, axis=-1, keepdims=True)
    inverse = lax.rsqrt(spread + EPSILON)
    return centered * inverse, inverse


def norm_back(e, n, inverse):
    return inverse * (
        e - jnp.mean(e, axis=-1, keepdims=True) - n * jnp.mean(e * n, axis=-1, keepdims=True)
    )


def gelu_parts(u):
    inner = 0.7978845608 * (u + 0.044715 * (u * u * u))
    t = jnp.tanh(inner)
    return t


def whole(shape):
    zeros = (0,) * len(shape)
    return pl.BlockSpec(shape, lambda *unused: zeros)


def flagged(grid, in_specs, out_specs, scratch):
    return pltpu.PrefetchScalarGridSpec(
        num_scalar_prefetch=1, grid=grid, in_specs=in_specs, out_specs=out_specs, scratch_shapes=scratch
    )


def project_kernel(flag, x_ref, vec_ref, w_ref, out_ref, n_ref, bias_ref):
    step = pl.program_id(0)

    @pl.when((flag[0] == 1) & (step == 0))
    def _():
        n, _ = normalize(x_ref[...].astype(F32))
        n_ref[...] = (n * vec_ref[0:1, :] + vec_ref[2:3, :]).astype(BF)
        bias_ref[...] = jnp.zeros_like(bias_ref)
        for p in range(4):
            bias_ref[p, :, 0:HL] = vec_ref[4:5, HL * p : HL * p + HL]
            bias_ref[p, :, 2 * HL :] = vec_ref[5:6, HL * p : HL * p + HL]

    @pl.when(flag[0] == 1)
    def _():
        out_ref[0] = (dot(n_ref[...], w_ref[0]) + bias_ref[step]).astype(BF)


def project(flag, x, vec, w):
    return pl.pallas_call(
        project_kernel,
        grid_spec=flagged(
            (4,),
            [
                whole((TOK, D)),
                whole((8, D)),
                pl.BlockSpec((1, D, 576), lambda j, f: (j * f[0], 0, 0)),
            ],
            pl.BlockSpec((1, TOK, 576), lambda j, f: (j * f[0], 0, 0)),
            [pltpu.VMEM((TOK, D), BF), pltpu.VMEM((4, 1, 576), F32)],
        ),
        out_shape=sds((4, TOK, 576), BF),
        compiler_params=BIG,
    )(flag, x, vec, w)


BLOCK = 256


def masked(scores, block):
    rows = block * BLOCK + lax.broadcasted_iota(jnp.int32, scores.shape, 0)
    cols = lax.broadcasted_iota(jnp.int32, scores.shape, 1)
    return jnp.where(cols <= rows, scores, MASKED)


def attend_kernel(live, with_previous, p_in, *refs):
    if with_previous:
        refs = refs[3:]
    h_out, lse_out, m_out, h_ref, m_ref, lse_ref, send, recv = refs

    def act():
        c = coords()
        z = c["z"]
        copies = Copies(send, recv)
        own = copies.local(p_in.at[z], h_ref.at[:, z])
        meet(c, ("z",), (1, 2, 3))
        coming, kept = [], []
        for g in range(GROUPS):
            for by in (2, 1, 3):
                to = peer(c, "z", by)
                coming.append(copies.remote(p_in.at[to["seq"], g], h_ref.at[g, z], to))
        own.wait()
        leaving = []
        for g in range(GROUPS):
            arrived(coming[3 * g : 3 * g + 3])
            kept.append(copies.local(h_ref.at[g], h_out.at[g]))
            keys = (g + 1) * BLOCK
            for head in range(3):
                q_at, k_at, v_at = HEAD * head, HL + HEAD * head, 2 * HL + HEAD * head
                q = h_ref[g, :, :, q_at : q_at + HEAD].reshape(BLOCK, HEAD) * jnp.asarray(0.125, BF)
                k = h_ref[0 : g + 1, :, :, k_at : k_at + HEAD].reshape(keys, HEAD)
                v = h_ref[0 : g + 1, :, :, v_at : v_at + HEAD].reshape(keys, HEAD)
                scores = masked(dot_nt(q, k), g)
                top = jnp.max(scores, axis=-1, keepdims=True)
                e = jnp.exp(scores - top)
                total = jnp.sum(e, axis=-1, keepdims=True)
                mixed = (dot(e.astype(BF), v) / total).astype(BF)
                m_ref[g, :, :, q_at : q_at + HEAD] = mixed.reshape(4, ROWS, HEAD)
                lse_ref[g, :, head : head + 1] = top + jnp.log(total)
            for by in (2, 1, 3):
                to = peer(c, "z", by)
                leaving.append(copies.remote(m_ref.at[g, to["seq"]], m_out.at[z, g], to))
            kept.append(copies.local(m_ref.at[g, z], m_out.at[z, g]))
        kept.append(copies.local(lse_ref, lse_out))
        arrived(leaving)
        for copy in kept:
            copy.wait()
        copies.drain()

    pl.when(lax.axis_index("section") == live)(act)


def attend(live, projected, previous, collective_id):
    ins, aliases = (projected,), {}
    if previous is not None:
        ins, aliases = ins + tuple(previous), {1: 0, 2: 1, 3: 2}
    count = 1 + 12 + 4 + 12 + 4 + 1
    return pl.pallas_call(
        functools.partial(attend_kernel, live, previous is not None),
        out_shape=(
            sds((4, 4, ROWS, 576), BF),
            sds((GROUPS, BLOCK, 128), F32),
            sds((4, 4, ROWS, HL), BF),
        ),
        in_specs=[pl.BlockSpec(memory_space=HBM)] * len(ins),
        out_specs=tuple([pl.BlockSpec(memory_space=HBM)] * 3),
        scratch_shapes=[
            pltpu.VMEM((4, 4, ROWS, 576), BF),
            pltpu.VMEM((4, 4, ROWS, HL), BF),
            pltpu.VMEM((GROUPS, BLOCK, 128), F32),
            pltpu.SemaphoreType.DMA((count,)),
            pltpu.SemaphoreType.DMA((count,)),
        ],
        input_output_aliases=aliases,
        compiler_params=pltpu.CompilerParams(
            collective_id=collective_id, has_side_effects=True, vmem_limit_bytes=60 * 1024 * 1024
        ),
    )(*ins)


def attend_back_kernel(
    live, g_in, h_hbm, lse_hbm, u_in, d_in, x_hbm, mid_hbm, w_hbm, vec_ref, sums_two_ref,
    gw_out, u_out, d_out, gx_ref, sums_ref,
    h_ref, lse_ref, gh_ref, gs_ref, dk_ref, dv_ref, p_ref, x_ref, mid_ref, w_ref, gw_ref, send, recv,
):
    def act():
        c = coords()
        z = c["z"]
        copies = Copies(send, recv)
        own = [
            copies.local(g_in.at[z], gh_ref.at[:, z]),
            copies.local(h_hbm, h_ref),
            copies.local(lse_hbm, lse_ref),
        ]
        meet(c, ("x", "y", "z"), (1, 2, 3))
        coming, leaving, kept = {}, [], []
        for g in reversed(range(GROUPS)):
            coming[g] = []
            for by in (2, 1, 3):
                to = peer(c, "z", by)
                coming[g].append(copies.remote(g_in.at[to["seq"], g], gh_ref.at[g, z], to))
        weights = spread(copies, c, "y", lambda i: d_in.at[:, :, i], d_out)
        weights += spread(copies, c, "x", lambda i: u_in.at[:, i], u_out)
        later = [copies.local(x_hbm, x_ref), copies.local(mid_hbm, mid_ref), copies.local(w_hbm, w_ref)]
        for copy in own:
            copy.wait()
        for g in reversed(range(GROUPS)):
            arrived(coming[g])
            keys = (g + 1) * BLOCK
            for head in range(3):
                q_at, k_at, v_at = HEAD * head, HL + HEAD * head, 2 * HL + HEAD * head
                q = h_ref[g, :, :, q_at : q_at + HEAD].reshape(BLOCK, HEAD) * jnp.asarray(0.125, BF)
                k = h_ref[0 : g + 1, :, :, k_at : k_at + HEAD].reshape(keys, HEAD)
                v = h_ref[0 : g + 1, :, :, v_at : v_at + HEAD].reshape(keys, HEAD)
                grad = gh_ref[g, :, :, q_at : q_at + HEAD].reshape(BLOCK, HEAD)
                scores = masked(dot_nt(q, k), g)
                p = jnp.exp(scores - lse_ref[g, :, head : head + 1])
                dp = dot_nt(grad, v)
                centre = jnp.sum(p * dp, axis=-1, keepdims=True)
                ds = (p * (dp - centre)).astype(BF)
                dq = (dot(ds, k) * 0.125).astype(BF)
                gs_ref[g, :, :, q_at : q_at + HEAD] = dq.reshape(4, ROWS, HEAD)
                dk = dot_tn(ds, q)
                dv = dot_tn(p.astype(BF), grad)
                if g < GROUPS - 1:
                    dk += dk_ref[head, 0:keys, :]
                    dv += dv_ref[head, 0:keys, :]
                if g > 0:
                    dk_ref[head, 0 : keys - BLOCK, :] = dk[: keys - BLOCK]
                    dv_ref[head, 0 : keys - BLOCK, :] = dv[: keys - BLOCK]
                gs_ref[g, :, :, k_at : k_at + HEAD] = dk[keys - BLOCK :].astype(BF).reshape(4, ROWS, HEAD)
                gs_ref[g, :, :, v_at : v_at + HEAD] = dv[keys - BLOCK :].astype(BF).reshape(4, ROWS, HEAD)
            for by in (2, 1, 3):
                to = peer(c, "z", by)
                leaving.append(copies.remote(gs_ref.at[g, to["seq"]], p_ref.at[z, g], to))
            kept.append(copies.local(gs_ref.at[g, z], p_ref.at[z, g]))
        for copy in later:
            copy.wait()
        n, inverse = normalize(x_ref[...].astype(F32))
        normed = (n * vec_ref[0:1, :] + vec_ref[2:3, :]).astype(BF)
        arrived(leaving)
        for copy in kept:
            copy.wait()
        back = jnp.zeros((TOK, D), F32)
        written = []
        for p in range(4):
            gp = p_ref[p].reshape(TOK, 576)
            gw_ref[p] = dot_tn(normed, gp).astype(BF)
            written.append(copies.local(gw_ref.at[p], gw_out.at[p]))
            columns = jnp.sum(gp.astype(F32), axis=0, keepdims=True)
            sums_ref[4:5, HL * p : HL * p + HL] = columns[:, 0:HL]
            sums_ref[5:6, HL * p : HL * p + HL] = columns[:, 2 * HL :]
            back += dot_nt(gp, w_ref[p])
        gx_ref[...] = (mid_ref[...] + norm_back(back * vec_ref[0:1, :], n, inverse)).astype(BF)
        sums_ref[0:1, :] = jnp.sum(back * n, axis=0, keepdims=True)
        sums_ref[1:2, :] = sums_two_ref[0:1, :]
        sums_ref[2:3, :] = jnp.sum(back, axis=0, keepdims=True)
        sums_ref[3:4, :] = sums_two_ref[1:2, :]
        sums_ref[6:8, :] = sums_two_ref[2:4, :]
        for copy in written:
            copy.wait()
        arrived(weights)
        copies.drain()

    pl.when(lax.axis_index("section") == live)(act)


def attend_back(live, grads, heads, lse, up, down, x, middle_grad, w, vec, sums_two, collective_id):
    vmem = pltpu.VMEM
    count = 3 + 12 + 6 + 3 + 12 + 4 + 4
    return pl.pallas_call(
        functools.partial(attend_back_kernel, live),
        out_shape=(
            sds((4, D, 576), BF),
            sds((4, 4, 48, FF), BF),
            sds((4, 4, 4, 48, D), BF),
            sds((TOK, D), BF),
            sds((8, D), F32),
        ),
        in_specs=[pl.BlockSpec(memory_space=HBM)] * 8 + [pl.BlockSpec(memory_space=vmem)] * 2,
        out_specs=tuple([pl.BlockSpec(memory_space=HBM)] * 3 + [pl.BlockSpec(memory_space=vmem)] * 2),
        scratch_shapes=[
            vmem((4, 4, ROWS, 576), BF),
            vmem((GROUPS, BLOCK, 128), F32),
            vmem((4, 4, ROWS, HL), BF),
            vmem((4, 4, ROWS, 576), BF),
            vmem((3, SEQ_LEN, HEAD), F32),
            vmem((3, SEQ_LEN, HEAD), F32),
            vmem((4, 4, ROWS, 576), BF),
            vmem((TOK, D), BF),
            vmem((TOK, D), F32),
            vmem((4, D, 576), BF),
            vmem((4, D, 576), BF),
            pltpu.SemaphoreType.DMA((count,)),
            pltpu.SemaphoreType.DMA((count,)),
        ],
        compiler_params=pltpu.CompilerParams(
            collective_id=collective_id, has_side_effects=True, vmem_limit_bytes=60 * 1024 * 1024
        ),
    )(grads, heads, lse, up, down, x, middle_grad, w, vec, sums_two)


def mlp_kernel(
    flag, x_ref, m_ref, vec_ref, ub_ref, wo_ref, wu_ref, wd_ref, res_ref, mid_ref, raised_ref, n_ref, acc_ref
):
    step = pl.program_id(0)

    @pl.when((flag[0] == 1) & (step == 0))
    def _():
        branch = dot(m_ref[0], wo_ref[0])
        for p in range(1, 4):
            branch += dot(m_ref[p], wo_ref[p])
        middle = x_ref[...].astype(F32) + (branch + vec_ref[6:7, :])
        mid_ref[...] = middle
        n, _ = normalize(middle)
        n_ref[...] = (n * vec_ref[1:2, :] + vec_ref[3:4, :]).astype(BF)
        acc_ref[...] = middle + vec_ref[7:8, :]

    @pl.when(flag[0] == 1)
    def _():
        raised = dot(n_ref[...], wu_ref[...]) + ub_ref[0]
        raised_ref[...] = raised
        active = (0.5 * raised * (1.0 + gelu_parts(raised))).astype(BF)
        acc_ref[...] += dot(active, wd_ref[...])

    @pl.when((flag[0] == 1) & (step == 3))
    def _():
        res_ref[...] = acc_ref[...].astype(BF)


def mlp(flag, x, mixed, vec, ub, wo, wu, wd):
    return pl.pallas_call(
        mlp_kernel,
        grid_spec=flagged(
            (4,),
            [
                whole((TOK, D)),
                whole((4, TOK, HL)),
                whole((8, D)),
                pl.BlockSpec((1, 1, D), lambda j, f: (j * f[0], 0, 0)),
                whole((4, HL, D)),
                pl.BlockSpec((D, D), lambda j, f: (0, j * f[0])),
                pl.BlockSpec((D, D), lambda j, f: (j * f[0], 0)),
            ],
            (whole((TOK, D)), whole((TOK, D)), pl.BlockSpec((TOK, D), lambda j, f: (0, j * f[0]))),
            [pltpu.VMEM((TOK, D), BF), pltpu.VMEM((TOK, D), F32)],
        ),
        out_shape=(sds((TOK, D), BF), sds((TOK, D), F32), sds((TOK, FF), F32)),
        compiler_params=BIG,
    )(flag, x, mixed, vec, ub, wo, wu, wd)


def mlp_back_kernel(
    g_ref, raised_ref, mid_ref, m_ref, vec_ref, wo_ref, wu_ref, wd_ref,
    gd_ref, gu_ref, go_ref, gm_ref, gmid_ref, sums_ref, gub_ref, n_ref, acc_ref,
):
    step = pl.program_id(0)

    @pl.when(step == 0)
    def _():
        n, _ = normalize(mid_ref[...])
        n_ref[...] = (n * vec_ref[1:2, :] + vec_ref[3:4, :]).astype(BF)
        acc_ref[...] = jnp.zeros_like(acc_ref)

    g = g_ref[...]
    u = raised_ref[...]
    t = gelu_parts(u)
    active = (0.5 * u * (1.0 + t)).astype(BF)
    gd_ref[...] = dot_tn(active, g).astype(BF)
    slope = 0.5 * (1.0 + t) + 0.5 * u * (1.0 - t * t) * (
        0.7978845608 * (1.0 + 3.0 * 0.044715 * (u * u))
    )
    grad_raised = (dot_nt(g, wd_ref[...]) * slope).astype(BF)
    gub_ref[0] = jnp.sum(grad_raised.astype(F32), axis=0, keepdims=True)
    gu_ref[...] = dot_tn(n_ref[...], grad_raised).astype(BF)
    acc_ref[...] += dot_nt(grad_raised, wu_ref[...])

    @pl.when(step == 3)
    def _():
        n, inverse = normalize(mid_ref[...])
        back = acc_ref[...]
        g32 = g.astype(F32)
        grad_middle = g32 + norm_back(back * vec_ref[1:2, :], n, inverse)
        gmid_ref[...] = grad_middle
        branch = grad_middle.astype(BF)
        sums_ref[...] = jnp.zeros_like(sums_ref)
        sums_ref[0:1, :] = jnp.sum(back * n, axis=0, keepdims=True)
        sums_ref[1:2, :] = jnp.sum(back, axis=0, keepdims=True)
        sums_ref[2:3, :] = jnp.sum(branch.astype(F32), axis=0, keepdims=True)
        sums_ref[3:4, :] = jnp.sum(g32, axis=0, keepdims=True)
        for p in range(4):
            go_ref[p] = dot_tn(m_ref[p], branch).astype(BF)
            gm_ref[p] = dot_nt(branch, wo_ref[p]).astype(BF)


def mlp_back(g, raised, middle, mixed, vec, wo, wu, wd):
    return pl.pallas_call(
        mlp_back_kernel,
        grid=(4,),
        out_shape=(
            sds((FF, D), BF),
            sds((D, FF), BF),
            sds((4, HL, D), BF),
            sds((4, TOK, HL), BF),
            sds((TOK, D), F32),
            sds((8, D), F32),
            sds((4, 1, D), F32),
        ),
        in_specs=[
            whole((TOK, D)),
            pl.BlockSpec((TOK, D), lambda j: (0, j)),
            whole((TOK, D)),
            whole((4, TOK, HL)),
            whole((8, D)),
            whole((4, HL, D)),
            pl.BlockSpec((D, D), lambda j: (0, j)),
            pl.BlockSpec((D, D), lambda j: (j, 0)),
        ],
        out_specs=(
            pl.BlockSpec((D, D), lambda j: (j, 0)),
            pl.BlockSpec((D, D), lambda j: (0, j)),
            whole((4, HL, D)),
            whole((4, TOK, HL)),
            whole((TOK, D)),
            whole((8, D)),
            pl.BlockSpec((1, 1, D), lambda j: (j, 0, 0)),
        ),
        scratch_shapes=[pltpu.VMEM((TOK, D), BF), pltpu.VMEM((TOK, D), F32)],
        compiler_params=BIG,
    )(g, raised, middle, mixed, vec, wo, wu, wd)


def tile(rows):
    pads = [(0, 0)] * (rows.ndim - 2) + [(0, 8 - rows.shape[-2]), (0, 128 - rows.shape[-1])]
    return jnp.pad(rows, pads)


def open_weights(raw):
    qkv, out, up, down, small = raw
    small = small.reshape(64, 2, 8, 128)
    vec = small[:, 0, :, :12].transpose(1, 0, 2).reshape(8, D)
    ub = small[:, 1, 0, :48].reshape(4, 1, D)
    return (
        qkv.reshape(4, D, 576),
        out.reshape(4, HL, D),
        up.reshape(D, FF),
        down.reshape(FF, D),
        vec,
        ub,
    )


def forward(live, flag, x, weights, previous, base_id):
    qkv, wo, wu, wd, vec, ub = weights
    projected = project(flag, x, vec, qkv)
    kept = attend(live, projected.reshape(4, 4, ROWS, 576), previous, base_id)
    mixed = kept[2].reshape(4, TOK, HL)
    result, middle, raised = mlp(flag, x, mixed, vec, ub, wo, wu, wd)
    return result, (mixed, middle, raised), kept


def backward(live, g, x, weights, saved, kept, base_id):
    qkv, wo, wu, wd, vec, ub = weights
    mixed, middle, raised = saved
    g_down, g_up, g_out, g_mixed, g_middle, sums_two, g_ub = mlp_back(
        g, raised, middle, mixed, vec, wo, wu, wd
    )
    g_up = g_up.reshape(4, 4, 48, FF)
    g_down = g_down.reshape(4, 4, 4, 48, D)
    g_qkv, up_got, down_got, g_x, sums = attend_back(
        live, g_mixed.reshape(4, 4, ROWS, HL), kept[0], kept[1], g_up, g_down, x, g_middle, qkv, vec, sums_two, base_id
    )
    small = jnp.stack(
        [tile(sums.reshape(8, 64, 12).transpose(1, 0, 2)), tile(g_ub.reshape(64, 1, 48))], axis=1
    )
    grads = (
        g_qkv.reshape(4, 4, 4, 48, 576),
        g_out.reshape(4, 4, 48, D),
        g_up,
        g_down,
        small.reshape(4, 4, 4, 2, 8, 128),
        up_got,
        down_got,
    )
    return g_x, grads


def per_device(ends, w_qkv, w_out, w_up, w_down, norm_gains, biases, up_bias):
    section = lax.axis_index("section")
    own = ends.reshape(TOK, D)
    qkv = w_qkv[0].reshape(12, 3, 4, HL).transpose(2, 0, 1, 3).reshape(4, 12, 576)
    small = jnp.stack([tile(jnp.concatenate([norm_gains[0], biases[0]])), tile(up_bias)]).astype(F32)
    q_y, o_y, u_y, d_x, s_x = gather_first(qkv, w_out[0], w_up[0], w_down[0], small)
    first = (
        q_y.transpose(1, 0, 2, 3).reshape(4, 48, 576),
        o_y.reshape(48, D),
        u_y.reshape(48, FF),
        d_x,
        s_x,
    )
    weights = open_weights(gather_rest(*first))
    flag = (section == 0).astype(jnp.int32).reshape(1)
    result, _, kept = forward(0, flag, own, weights, None, 3)
    arriving = lax.ppermute(result, "section", [(0, 1)])
    x = jnp.where(section == 0, own, arriving)
    result, saved, kept = forward(1, jnp.ones((1,), jnp.int32), x, weights, kept, 4)

    g_x, grads = backward(1, own, x, weights, saved, kept, 5)
    arriving = lax.ppermute(g_x, "section", [(1, 0)])
    grads, arriving = lax.optimization_barrier((grads, arriving))
    total_one = reduce_grads(1, *grads, 7)
    total_one, arriving = lax.optimization_barrier((total_one, arriving))
    g = jnp.where(section == 1, own, arriving)
    g_x, grads = backward(0, g, x, weights, saved, kept, 6)
    total_zero = reduce_grads(0, *grads, 8)
    q, o, u, d, s = (
        jnp.where(section == 0, zero, one) for zero, one in zip(total_zero, total_one)
    )
    boundary = jnp.where(section == 0, g_x, result)
    return (
        boundary.reshape(1, 1, GROUPS, ROWS, D),
        q.reshape(4, 12, 3, HL).transpose(1, 2, 0, 3).reshape(1, 12, 3 * D),
        o[None],
        u[None],
        d[None],
        s[0:1, 0:2, :12],
        s[0:1, 2:8, :12],
        s[1:2, 0, :48],
    )


def solution(mesh):
    rows = P("section", ("seq", "shard"), None)
    columns = P("section", None, ("seq", "shard"))
    ends = P("section", "shard", None, "seq", None)
    hidden = P("section", ("seq", "shard"))
    placed = (ends, rows, rows, rows, rows, columns, columns, hidden)
    return jax.shard_map(per_device, mesh=mesh, in_specs=placed, out_specs=placed, check_vma=False)
```

```python
import functools

import jax
import jax.numpy as jnp
from jax import lax
from jax.experimental import pallas as pl
from jax.experimental.pallas import tpu as pltpu
from jax.sharding import PartitionSpec as P

HEAD = 64
FF = 3072
D = 768
GROUPS = 4
ROWS = 64
TOK = GROUPS * ROWS
SEQ_LEN = 1024
HL = 192
EPSILON = 1e-05
MASKED = -1e30
BF = jnp.bfloat16
F32 = jnp.float32
MESH = pl.DeviceIdType.MESH
HBM = pltpu.HBM


def sds(shape, dtype):
    return jax.ShapeDtypeStruct(shape, dtype)


def coords():
    shard = lax.axis_index("shard")
    return {"x": shard // 4, "y": lax.rem(shard, 4), "z": lax.axis_index("seq")}


def peer(c, axis, by):
    moved = dict(c)
    moved[axis] = lax.rem(c[axis] + by, 4)
    return {"section": lax.axis_index("section"), "seq": moved["z"], "shard": moved["x"] * 4 + moved["y"]}


def partner():
    return {
        "section": 1 - lax.axis_index("section"),
        "seq": lax.axis_index("seq"),
        "shard": lax.axis_index("shard"),
    }


def meet(c, axes, steps, with_partner=False):
    barrier = pltpu.get_barrier_semaphore()
    if with_partner:
        pl.semaphore_signal(barrier, inc=1, device_id=partner(), device_id_type=MESH)
    for axis in axes:
        for by in steps:
            pl.semaphore_signal(barrier, inc=1, device_id=peer(c, axis, by), device_id_type=MESH)
    pl.semaphore_wait(barrier, len(axes) * len(steps) + int(with_partner))


class Copies:
    def __init__(self, send, recv):
        self.send, self.recv, self.used, self.sent = send, recv, 0, []

    def remote(self, src, dst, to, start=True):
        copy = pltpu.make_async_remote_copy(
            src_ref=src,
            dst_ref=dst,
            send_sem=self.send.at[self.used],
            recv_sem=self.recv.at[self.used],
            device_id=to,
            device_id_type=MESH,
        )
        self.used += 1
        if start:
            copy.start()
            self.sent.append(copy)
        return copy

    def local(self, src, dst, start=True):
        copy = pltpu.make_async_copy(src, dst, self.send.at[self.used])
        self.used += 1
        if start:
            copy.start()
        return copy

    def drain(self):
        for copy in self.sent:
            copy.wait_send()


class Gather:
    def __init__(self, copies, c, axis, own, dst, half):
        self.copies, self.c, self.axis, self.own, self.dst, self.half = copies, c, axis, own, dst, half

    def first(self):
        a = self.c[self.axis]
        self.right, self.left = peer(self.c, self.axis, 1), peer(self.c, self.axis, 3)
        self.go_right = self.copies.remote(self.own, self.dst(a), self.right)
        self.go_left = self.copies.remote(self.own, self.dst(a), self.left)

    def second(self):
        a = self.c[self.axis]
        before, after = lax.rem(a + 3, 4), lax.rem(a + 1, 4)
        self.go_right.wait_recv()
        self.on_right = self.copies.remote(self.half(before, 0), self.half(before, 0), self.right)
        self.go_left.wait_recv()
        self.on_left = self.copies.remote(self.half(after, 1), self.half(after, 1), self.left)

    def third(self):
        self.on_right.wait_recv()
        self.on_left.wait_recv()


def run_gathers(gathers):
    for g in gathers:
        g.first()
    for g in gathers:
        g.second()


def comm_call(body, in_turn, axes, count, ins, out_shapes, collective_id):
    n_in, n_out = len(ins), len(out_shapes)

    def kernel(*refs):
        in_refs, out_refs = refs[:n_in], refs[n_in : n_in + n_out]
        send, recv, turn = refs[n_in + n_out :]
        c = coords()
        meet(c, axes, (1, 3), in_turn)
        body(Copies(send, recv), c, in_refs, out_refs, turn)

    return pl.pallas_call(
        kernel,
        out_shape=tuple(out_shapes),
        in_specs=[pl.BlockSpec(memory_space=pltpu.VMEM)] * n_in,
        out_specs=tuple([pl.BlockSpec(memory_space=HBM)] * n_out),
        scratch_shapes=[
            pltpu.SemaphoreType.DMA((count,)),
            pltpu.SemaphoreType.DMA((count,)),
            pltpu.SemaphoreType.REGULAR,
        ],
        compiler_params=pltpu.CompilerParams(
            collective_id=collective_id, has_side_effects=True, vmem_limit_bytes=60 * 1024 * 1024
        ),
    )(*ins)


def gather_first(qkv, out, up, down, small):
    def body(copies, c, ins, outs, turn):
        y, x = c["y"], c["x"]
        q_in, o_in, u_in, d_in, s_in = ins
        q_y, o_y, u_y, d_x, s_x = outs
        gathers = [
            Gather(copies, c, "y", u_in, lambda i: u_y.at[i], lambda i, h: u_y.at[i, :, pl.ds(1536 * h, 1536)]),
            Gather(copies, c, "y", q_in, lambda i: q_y.at[i], lambda i, h: q_y.at[i, pl.ds(2 * h, 2)]),
            Gather(copies, c, "y", o_in, lambda i: o_y.at[i], lambda i, h: o_y.at[i, :, pl.ds(384 * h, 384)]),
            Gather(copies, c, "x", d_in, lambda i: d_x.at[i], lambda i, h: d_x.at[i, :, pl.ds(384 * h, 384)]),
            Gather(copies, c, "x", s_in, lambda i: s_x.at[i], lambda i, h: s_x.at[i, h]),
        ]
        own = [
            copies.local(u_in, u_y.at[y]),
            copies.local(q_in, q_y.at[y]),
            copies.local(o_in, o_y.at[y]),
            copies.local(d_in, d_x.at[x]),
            copies.local(s_in, s_x.at[x]),
        ]
        run_gathers(gathers)
        for g in gathers:
            g.third()
        for copy in own:
            copy.wait()
        copies.drain()

    shapes = (
        sds((4, 4, 12, 576), BF),
        sds((4, 12, D), BF),
        sds((4, 12, FF), BF),
        sds((4, 48, D), BF),
        sds((4, 2, 8, 128), F32),
    )
    return comm_call(body, False, ("x", "y"), 25, (qkv, out, up, down, small), shapes, 0)


def gather_qkv(qkv, up, down, small):
    def body(copies, c, ins, outs, turn):
        x, y, z = c["x"], c["y"], c["z"]
        q_in, u_in, d_in, s_in = ins
        q, u, da, db, s = outs
        low, high = pl.ds(0, 384), pl.ds(384, 384)
        one = [
            Gather(
                copies, c, "z", q_in.at[pl.ds(0, 2)],
                lambda i: q.at[pl.ds(0, 2), i, x], lambda i, h: q.at[h, i, x],
            ),
            Gather(
                copies, c, "x", q_in.at[pl.ds(2, 2)],
                lambda i: q.at[pl.ds(2, 2), z, i], lambda i, h: q.at[2 + h, z, i],
            ),
            Gather(copies, c, "z", s_in, lambda i: s.at[i, :, y], lambda i, h: s.at[i, pl.ds(2 * h, 2), y]),
            Gather(copies, c, "z", u_in, lambda i: u.at[i], lambda i, h: u.at[i, :, pl.ds(1536 * h, 1536)]),
            Gather(copies, c, "y", d_in.at[:, :, low], lambda i: da.at[:, i], lambda i, h: da.at[pl.ds(2 * h, 2), i]),
            Gather(copies, c, "z", d_in.at[:, :, high], lambda i: db.at[i], lambda i, h: db.at[i, pl.ds(2 * h, 2)]),
        ]
        own = [
            copies.local(q_in.at[pl.ds(0, 2)], q.at[pl.ds(0, 2), z, x]),
            copies.local(q_in.at[pl.ds(2, 2)], q.at[pl.ds(2, 2), z, x]),
            copies.local(s_in, s.at[z, :, y]),
            copies.local(u_in, u.at[z]),
            copies.local(d_in.at[:, :, low], da.at[:, y]),
            copies.local(d_in.at[:, :, high], db.at[z]),
        ]

        @pl.when(lax.axis_index("section") == 1)
        def _():
            pl.semaphore_wait(turn, 1)

        run_gathers(one)
        two = [
            Gather(
                copies, c, "x", q.at[pl.ds(0, 2), :, x],
                lambda i: q.at[pl.ds(0, 2), :, i], lambda i, h: q.at[h, :, i],
            ),
            Gather(
                copies, c, "z", q.at[pl.ds(2, 2), z],
                lambda i: q.at[pl.ds(2, 2), i], lambda i, h: q.at[2 + h, i],
            ),
            Gather(copies, c, "y", s.at[:, :, y], lambda i: s.at[:, :, i], lambda i, h: s.at[pl.ds(2 * h, 2), :, i]),
        ]
        for k in range(3):
            one[k].third()
            own[k].wait()
            two[k].first()
        for k in range(3, 6):
            one[k].third()
            own[k].wait()
        for g in two:
            g.second()

        @pl.when(lax.axis_index("section") == 0)
        def _():
            pl.semaphore_signal(turn, inc=1, device_id=partner(), device_id_type=MESH)

        for g in two:
            g.third()
        copies.drain()

    shapes = (
        sds((4, 4, 4, 48, 576), BF),
        sds((4, 48, FF), BF),
        sds((4, 4, 48, 384), BF),
        sds((4, 4, 48, 384), BF),
        sds((4, 4, 4, 2, 8, 128), F32),
    )
    return comm_call(body, True, ("x", "y", "z"), 42, (qkv, up, down, small), shapes, 1)


def spread(copies, c, axis, source, target):
    moves = []
    for by in (2, 1, 3):
        there = lax.rem(c[axis] + by, 4)
        moves.append(copies.remote(source(there), target.at[by], peer(c, axis, by)))
    return moves


def arrived(moves):
    for move in moves:
        move.wait_recv()


def add(ref, at):
    total = ref[(0,) + at].astype(F32)
    for k in range(1, 4):
        total += ref[(k,) + at].astype(F32)
    return total


def more(mine, ref, at):
    total = mine.astype(F32)
    for k in range(1, 4):
        total += ref[(k,) + at].astype(F32)
    return total


def reduce_kernel(live, with_previous, q_in, o_in, u_in, d_in, s_in, u_got, d_got, *refs):
    if with_previous:
        refs = refs[5:]
    results, final, scratch = refs[:5], refs[5:10], refs[10:]
    q, o, u, d, s = final
    qa1, qb1, o1, u1, d1, s1, qa2, qb2, o2, u2, d2, s2, tmp, qs, os, us, q3, o3, u3, d3, s3, send, recv = scratch

    def act():
        c = coords()
        x, y, z = c["x"], c["y"], c["z"]
        copies = Copies(send, recv)
        own_d = [copies.local(d_in.at[:, :, y], d1.at[0]), copies.local(d_got.at[pl.ds(1, 3)], d1.at[pl.ds(1, 3)])]
        own_u = [copies.local(u_in.at[:, x], u1.at[0]), copies.local(u_got.at[pl.ds(1, 3)], u1.at[pl.ds(1, 3)])]
        own_qa = copies.local(q_in.at[pl.ds(0, 2), :, x], qa1.at[0])
        own_qb = copies.local(q_in.at[pl.ds(2, 2), z], qb1.at[0])
        own_o = copies.local(o_in.at[:, x], o1.at[0])
        own_s = copies.local(s_in.at[:, :, y], s1.at[0])
        meet(c, ("x", "y", "z"), (1, 2, 3))
        one_qa = spread(copies, c, "x", lambda i: q_in.at[pl.ds(0, 2), :, i], qa1)
        one_qb = spread(copies, c, "z", lambda i: q_in.at[pl.ds(2, 2), i], qb1)
        one_o = spread(copies, c, "x", lambda i: o_in.at[:, i], o1)
        one_s = spread(copies, c, "y", lambda i: s_in.at[:, :, i], s1)

        def add_all(ref, rows, kind):
            @pl.loop(0, rows * 4)
            def _(i):
                at = (i // 4, lax.rem(i, 4))
                ref[(0,) + at] = add(ref, at).astype(kind)

        for copy in own_d:
            copy.wait()
        add_all(d1, 4, BF)
        two_d = spread(copies, c, "x", lambda i: d1.at[0, :, i], d2)
        for copy in own_u:
            copy.wait()

        @pl.loop(0, 4)
        def _(i):
            for k in range(4):
                at = (i, slice(None), pl.ds(D * k, D))
                u1[(0,) + at] = add(u1, at).astype(BF)

        two_u = spread(copies, c, "z", lambda i: u1.at[0, i], u2)
        arrived(one_qa)
        own_qa.wait()
        add_all(qa1, 2, BF)
        two_qa = spread(copies, c, "z", lambda i: qa1.at[0, :, i], qa2)
        arrived(one_qb)
        own_qb.wait()
        add_all(qb1, 2, BF)
        two_qb = spread(copies, c, "x", lambda i: qb1.at[0, :, i], qb2)
        arrived(one_o)
        own_o.wait()

        @pl.loop(0, 4)
        def _(i):
            o1[0, i] = add(o1, (i,)).astype(BF)

        two_o = spread(copies, c, "z", lambda i: o1.at[0, i], o2)
        arrived(one_s)
        own_s.wait()
        add_all(s1, 4, F32)
        two_s = spread(copies, c, "z", lambda i: s1.at[0, i], s2)
        arrived(two_d)

        @pl.loop(0, 4)
        def _(i):
            d2[0, i] = more(d1[0, i, x], d2, (i,)).astype(BF)

        three_d = spread(copies, c, "z", lambda i: d2.at[0, i], d3)
        arrived(two_u)
        for k in range(4):
            at = (slice(None), pl.ds(D * k, D))
            tmp[...] = more(u1[(0, z) + at], u2, at)
            for i in range(4):
                us[i, :, D * k : D * k + D] = tmp[12 * i : 12 * i + 12, :].astype(BF)
        three_u = spread(copies, c, "y", lambda i: us.at[i], u3)
        arrived(two_qa)
        arrived(two_qb)
        for p in range(4):
            if p < 2:
                tmp[:, 0:576] = more(qa1[0, p, z], qa2, (p,))
            else:
                tmp[:, 0:576] = more(qb1[0, p - 2, x], qb2, (p - 2,))
            for i in range(4):
                qs[i, p] = tmp[12 * i : 12 * i + 12, 0:576].astype(BF)
        three_q = spread(copies, c, "y", lambda i: qs.at[i], q3)
        arrived(two_o)
        tmp[...] = more(o1[0, z], o2, ())
        for i in range(4):
            os[i] = tmp[12 * i : 12 * i + 12, :].astype(BF)
        three_o = spread(copies, c, "y", lambda i: os.at[i], o3)
        arrived(two_s)

        @pl.loop(0, 4)
        def _(i):
            s2[0, i] = more(s1[0, z, i], s2, (i,))

        three_s = spread(copies, c, "x", lambda i: s2.at[0, i], s3)
        arrived(three_d)
        d[...] = more(d2[0, z], d3, ())
        done = [copies.local(d, results[3].at[0])]
        arrived(three_u)
        u[...] = more(us[y], u3, ())
        done.append(copies.local(u, results[2].at[0]))
        arrived(three_q)
        for p in range(4):
            total = more(qs[y, p], q3, (p,))
            for kind in range(3):
                at = D * kind + HL * p
                q[:, at : at + HL] = total[:, HL * kind : HL * kind + HL]
        done.append(copies.local(q, results[0].at[0]))
        arrived(three_o)
        o[...] = more(os[y], o3, ())
        done.append(copies.local(o, results[1].at[0]))
        arrived(three_s)
        s[...] = more(s2[0, x], s3, ())
        done.append(copies.local(s, results[4]))
        for copy in done:
            copy.wait()
        copies.drain()

    pl.when(lax.axis_index("section") == live)(act)


def reduce_grads(live, qkv, out, up, down, small, up_got, down_got, previous, collective_id):
    vmem = pltpu.VMEM
    count = 8 + 12 + 18 + 15 + 5
    ins, aliases = (qkv, out, up, down, small, up_got, down_got), {}
    if previous is not None:
        ins, aliases = ins + tuple(previous), {7 + i: i for i in range(5)}
    return pl.pallas_call(
        functools.partial(reduce_kernel, live, previous is not None),
        out_shape=(
            sds((1, 12, 3 * D), F32),
            sds((1, 12, D), F32),
            sds((1, 12, FF), F32),
            sds((1, 48, D), F32),
            sds((2, 8, 128), F32),
        ),
        in_specs=[pl.BlockSpec(memory_space=HBM)] * len(ins),
        out_specs=tuple([pl.BlockSpec(memory_space=HBM)] * 5),
        input_output_aliases=aliases,
        scratch_shapes=[
            vmem((12, 3 * D), F32),
            vmem((12, D), F32),
            vmem((12, FF), F32),
            vmem((48, D), F32),
            vmem((2, 8, 128), F32),
            vmem((4, 2, 4, 48, 576), BF),
            vmem((4, 2, 4, 48, 576), BF),
            vmem((4, 4, 48, D), BF),
            vmem((4, 4, 48, FF), BF),
            vmem((4, 4, 4, 48, D), BF),
            vmem((4, 4, 4, 2, 8, 128), F32),
            vmem((4, 2, 48, 576), BF),
            vmem((4, 2, 48, 576), BF),
            vmem((4, 48, D), BF),
            vmem((4, 48, FF), BF),
            vmem((4, 4, 48, D), BF),
            vmem((4, 4, 2, 8, 128), F32),
            vmem((48, D), F32),
            vmem((4, 4, 12, 576), BF),
            vmem((4, 12, D), BF),
            vmem((4, 12, FF), BF),
            vmem((4, 4, 12, 576), BF),
            vmem((4, 12, D), BF),
            vmem((4, 12, FF), BF),
            vmem((4, 48, D), BF),
            vmem((4, 2, 8, 128), F32),
            pltpu.SemaphoreType.DMA((count,)),
            pltpu.SemaphoreType.DMA((count,)),
        ],
        compiler_params=pltpu.CompilerParams(
            collective_id=collective_id, has_side_effects=True, vmem_limit_bytes=60 * 1024 * 1024
        ),
    )(*ins)


BIG = pltpu.CompilerParams(vmem_limit_bytes=56 * 1024 * 1024)


def dot(a, b):
    return jnp.dot(a, b, preferred_element_type=F32)


def dot_nt(a, b):
    return lax.dot_general(a, b, (((1,), (1,)), ((), ())), preferred_element_type=F32)


def dot_tn(a, b):
    return lax.dot_general(a, b, (((0,), (0,)), ((), ())), preferred_element_type=F32)


def normalize(values):
    centered = values - jnp.mean(values, axis=-1, keepdims=True)
    spread = jnp.mean(centered * centered, axis=-1, keepdims=True)
    inverse = lax.rsqrt(spread + EPSILON)
    return centered * inverse, inverse


def norm_back(e, n, inverse):
    return inverse * (
        e - jnp.mean(e, axis=-1, keepdims=True) - n * jnp.mean(e * n, axis=-1, keepdims=True)
    )


def gelu_parts(u):
    inner = 0.7978845608 * (u + 0.044715 * (u * u * u))
    t = jnp.tanh(inner)
    return t


def whole(shape):
    zeros = (0,) * len(shape)
    return pl.BlockSpec(shape, lambda *unused: zeros)


def flagged(grid, in_specs, out_specs, scratch):
    return pltpu.PrefetchScalarGridSpec(
        num_scalar_prefetch=1, grid=grid, in_specs=in_specs, out_specs=out_specs, scratch_shapes=scratch
    )


def project_kernel(flag, x_ref, vec_ref, w_ref, out_ref, n_ref, bias_ref):
    step = pl.program_id(0)

    @pl.when((flag[0] == 1) & (step == 0))
    def _():
        n, _ = normalize(x_ref[...].astype(F32))
        n_ref[...] = (n * vec_ref[0:1, :] + vec_ref[2:3, :]).astype(BF)
        bias_ref[...] = jnp.zeros_like(bias_ref)
        for p in range(4):
            bias_ref[p, :, 0:HL] = vec_ref[4:5, HL * p : HL * p + HL]
            bias_ref[p, :, 2 * HL :] = vec_ref[5:6, HL * p : HL * p + HL]

    @pl.when(flag[0] == 1)
    def _():
        out_ref[0] = (dot(n_ref[...], w_ref[0]) + bias_ref[step]).astype(BF)


def project(flag, x, vec, w):
    return pl.pallas_call(
        project_kernel,
        grid_spec=flagged(
            (4,),
            [
                whole((TOK, D)),
                whole((8, D)),
                pl.BlockSpec((1, D, 576), lambda j, f: (j * f[0], 0, 0)),
            ],
            pl.BlockSpec((1, TOK, 576), lambda j, f: (j * f[0], 0, 0)),
            [pltpu.VMEM((TOK, D), BF), pltpu.VMEM((4, 1, 576), F32)],
        ),
        out_shape=sds((4, TOK, 576), BF),
        compiler_params=BIG,
    )(flag, x, vec, w)


BLOCK = 256


def masked(scores, block):
    rows = block * BLOCK + lax.broadcasted_iota(jnp.int32, scores.shape, 0)
    cols = lax.broadcasted_iota(jnp.int32, scores.shape, 1)
    return jnp.where(cols <= rows, scores, MASKED)


def attend_kernel(first, *refs):
    p_in = refs[0]
    if first:
        o_in, u_in, da_in, db_in = refs[1:5]
        h_out, lse_out, m_out, o, u, d = refs[5:11]
        h_ref, m_ref, lse_ref, o_ref, u_ref, da_ref, db_ref, send, recv, turn = refs[11:]
    else:
        h_out, lse_out, m_out, h_ref, m_ref, lse_ref, send, recv = refs[4:]
    section = lax.axis_index("section")
    live = section == (0 if first else 1)
    c = coords()
    x, y, z = c["x"], c["y"], c["z"]
    copies = Copies(send, recv)
    others = [peer(c, "z", by) for by in (2, 1, 3)]
    own = copies.local(p_in.at[z], h_ref.at[:, z], False)
    coming = [
        [copies.remote(p_in.at[to["seq"], g], h_ref.at[g, z], to, False) for to in others] for g in range(GROUPS)
    ]
    leaving = [
        [copies.remote(m_ref.at[g, to["seq"]], m_out.at[z, g], to, False) for to in others] for g in range(GROUPS)
    ]
    kept = [copies.local(h_ref.at[g], h_out.at[g], False) for g in range(GROUPS)]
    kept_own = [copies.local(m_ref.at[g, z], m_out.at[z, g], False) for g in range(GROUPS)]
    kept_lse = copies.local(lse_ref, lse_out, False)

    def begin():
        own.start()
        for moves in coming:
            for move in moves:
                move.start()

    def work():
        own.wait()
        for g in range(GROUPS):
            arrived(coming[g])
            kept[g].start()
            keys = (g + 1) * BLOCK
            for head in range(3):
                q_at, k_at, v_at = HEAD * head, HL + HEAD * head, 2 * HL + HEAD * head
                q = h_ref[g, :, :, q_at : q_at + HEAD].reshape(BLOCK, HEAD) * jnp.asarray(0.125, BF)
                k = h_ref[0 : g + 1, :, :, k_at : k_at + HEAD].reshape(keys, HEAD)
                v = h_ref[0 : g + 1, :, :, v_at : v_at + HEAD].reshape(keys, HEAD)
                scores = masked(dot_nt(q, k), g)
                top = jnp.max(scores, axis=-1, keepdims=True)
                e = jnp.exp(scores - top)
                total = jnp.sum(e, axis=-1, keepdims=True)
                mixed = (dot(e.astype(BF), v) / total).astype(BF)
                m_ref[g, :, :, q_at : q_at + HEAD] = mixed.reshape(4, ROWS, HEAD)
                lse_ref[g, :, head : head + 1] = top + jnp.log(total)
            for move in leaving[g]:
                move.start()
            kept_own[g].start()
        kept_lse.start()

    def end():
        for g in range(GROUPS):
            arrived(leaving[g])
            kept[g].wait()
            kept_own[g].wait()
        kept_lse.wait()
        for moves in coming + leaving:
            for move in moves:
                move.wait_send()

    if not first:

        @pl.when(live)
        def _():
            meet(c, ("z",), (1, 2, 3))
            begin()
            work()
            end()

        return

    low, high = pl.ds(0, 384), pl.ds(384, 384)
    loads = [
        copies.local(o_in, o_ref),
        copies.local(u_in, u_ref),
        copies.local(da_in, da_ref),
        copies.local(db_in, db_ref),
    ]
    meet(c, ("x", "y", "z"), (1, 2, 3), True)
    pl.when(live)(begin)

    @pl.when(jnp.logical_not(live))
    def _():
        pl.semaphore_wait(turn, 1)

    o_one = Gather(copies, c, "x", o_in, lambda i: o.at[z, i], lambda i, h: o.at[z, i, :, pl.ds(384 * h, 384)])
    bulk = [
        Gather(copies, c, "x", u_in, lambda i: u.at[:, i], lambda i, h: u.at[pl.ds(2 * h, 2), i]),
        Gather(
            copies, c, "y", db_in, lambda i: d.at[:, :, i, :, high], lambda i, h: d.at[pl.ds(2 * h, 2), :, i, :, high]
        ),
        Gather(
            copies, c, "z", da_in, lambda i: d.at[i, :, :, :, low], lambda i, h: d.at[i, pl.ds(2 * h, 2), :, :, low]
        ),
    ]
    o_one.first()
    for g in bulk:
        g.first()
    for copy in loads:
        copy.wait()
    stores = [
        copies.local(o_ref, o.at[z, x]),
        copies.local(u_ref, u.at[:, x]),
        copies.local(da_ref, d.at[z, :, :, :, low]),
        copies.local(db_ref, d.at[:, :, y, :, high]),
    ]
    pl.when(live)(work)
    o_one.second()
    o_one.third()
    stores[0].wait()
    o_two = Gather(copies, c, "z", o.at[z], lambda i: o.at[i], lambda i, h: o.at[i, pl.ds(2 * h, 2)])
    o_two.first()
    for g in bulk:
        g.second()
    o_two.second()

    @pl.when(live)
    def _():
        pl.semaphore_signal(turn, inc=1, device_id=partner(), device_id_type=MESH)

    for g in bulk:
        g.third()
    o_two.third()
    for copy in stores[1:]:
        copy.wait()
    copies.drain()
    pl.when(live)(end)


def attend(first, ins, collective_id):
    count = 1 + 12 + 12 + 4 + 4 + 1 + (4 + 4 + 20 if first else 0)
    shapes = [
        sds((4, 4, ROWS, 576), BF),
        sds((GROUPS, BLOCK, 128), F32),
        sds((4, 4, ROWS, HL), BF),
    ]
    scratch = [
        pltpu.VMEM((4, 4, ROWS, 576), BF),
        pltpu.VMEM((4, 4, ROWS, HL), BF),
        pltpu.VMEM((GROUPS, BLOCK, 128), F32),
    ]
    semaphores = [pltpu.SemaphoreType.DMA((count,)), pltpu.SemaphoreType.DMA((count,))]
    aliases = {1: 0, 2: 1, 3: 2}
    if first:
        aliases = {}
        shapes += [sds((4, 4, 48, D), BF), sds((4, 4, 48, FF), BF), sds((4, 4, 4, 48, D), BF)]
        scratch += [
            pltpu.VMEM((48, D), BF),
            pltpu.VMEM((4, 48, FF), BF),
            pltpu.VMEM((4, 4, 48, 384), BF),
            pltpu.VMEM((4, 4, 48, 384), BF),
        ]
        semaphores += [pltpu.SemaphoreType.REGULAR]
    return pl.pallas_call(
        functools.partial(attend_kernel, first),
        out_shape=tuple(shapes),
        in_specs=[pl.BlockSpec(memory_space=HBM)] * len(ins),
        out_specs=tuple([pl.BlockSpec(memory_space=HBM)] * len(shapes)),
        scratch_shapes=scratch + semaphores,
        input_output_aliases=aliases,
        compiler_params=pltpu.CompilerParams(
            collective_id=collective_id, has_side_effects=True, vmem_limit_bytes=60 * 1024 * 1024
        ),
    )(*ins)


def attend_back_kernel(
    live, g_in, h_hbm, lse_hbm, u_in, d_in, x_hbm, mid_hbm, w_hbm, vec_ref, sums_two_ref,
    gw_out, u_out, d_out, gx_ref, sums_ref,
    h_ref, lse_ref, gh_ref, gs_ref, dk_ref, dv_ref, p_ref, x_ref, mid_ref, w_ref, gw_ref, send, recv,
):
    def act():
        c = coords()
        z = c["z"]
        copies = Copies(send, recv)
        own = [
            copies.local(g_in.at[z], gh_ref.at[:, z]),
            copies.local(h_hbm, h_ref),
            copies.local(lse_hbm, lse_ref),
        ]
        meet(c, ("x", "y", "z"), (1, 2, 3))
        coming, leaving, kept = {}, [], []
        for g in reversed(range(GROUPS)):
            coming[g] = []
            for by in (2, 1, 3):
                to = peer(c, "z", by)
                coming[g].append(copies.remote(g_in.at[to["seq"], g], gh_ref.at[g, z], to))
        weights = spread(copies, c, "y", lambda i: d_in.at[:, :, i], d_out)
        weights += spread(copies, c, "x", lambda i: u_in.at[:, i], u_out)
        later = [copies.local(x_hbm, x_ref), copies.local(mid_hbm, mid_ref), copies.local(w_hbm, w_ref)]
        for copy in own:
            copy.wait()
        for g in reversed(range(GROUPS)):
            arrived(coming[g])
            keys = (g + 1) * BLOCK
            for head in range(3):
                q_at, k_at, v_at = HEAD * head, HL + HEAD * head, 2 * HL + HEAD * head
                q = h_ref[g, :, :, q_at : q_at + HEAD].reshape(BLOCK, HEAD) * jnp.asarray(0.125, BF)
                k = h_ref[0 : g + 1, :, :, k_at : k_at + HEAD].reshape(keys, HEAD)
                v = h_ref[0 : g + 1, :, :, v_at : v_at + HEAD].reshape(keys, HEAD)
                grad = gh_ref[g, :, :, q_at : q_at + HEAD].reshape(BLOCK, HEAD)
                scores = masked(dot_nt(q, k), g)
                p = jnp.exp(scores - lse_ref[g, :, head : head + 1])
                dp = dot_nt(grad, v)
                centre = jnp.sum(p * dp, axis=-1, keepdims=True)
                ds = (p * (dp - centre)).astype(BF)
                dq = (dot(ds, k) * 0.125).astype(BF)
                gs_ref[g, :, :, q_at : q_at + HEAD] = dq.reshape(4, ROWS, HEAD)
                dk = dot_tn(ds, q)
                dv = dot_tn(p.astype(BF), grad)
                if g < GROUPS - 1:
                    dk += dk_ref[head, 0:keys, :]
                    dv += dv_ref[head, 0:keys, :]
                if g > 0:
                    dk_ref[head, 0 : keys - BLOCK, :] = dk[: keys - BLOCK]
                    dv_ref[head, 0 : keys - BLOCK, :] = dv[: keys - BLOCK]
                gs_ref[g, :, :, k_at : k_at + HEAD] = dk[keys - BLOCK :].astype(BF).reshape(4, ROWS, HEAD)
                gs_ref[g, :, :, v_at : v_at + HEAD] = dv[keys - BLOCK :].astype(BF).reshape(4, ROWS, HEAD)
            for by in (2, 1, 3):
                to = peer(c, "z", by)
                leaving.append(copies.remote(gs_ref.at[g, to["seq"]], p_ref.at[z, g], to))
            kept.append(copies.local(gs_ref.at[g, z], p_ref.at[z, g]))
        for copy in later:
            copy.wait()
        n, inverse = normalize(x_ref[...].astype(F32))
        normed = (n * vec_ref[0:1, :] + vec_ref[2:3, :]).astype(BF)
        arrived(leaving)
        for copy in kept:
            copy.wait()
        back = jnp.zeros((TOK, D), F32)
        written = []
        for p in range(4):
            gp = p_ref[p].reshape(TOK, 576)
            gw_ref[p] = dot_tn(normed, gp).astype(BF)
            written.append(copies.local(gw_ref.at[p], gw_out.at[p]))
            columns = jnp.sum(gp.astype(F32), axis=0, keepdims=True)
            sums_ref[4:5, HL * p : HL * p + HL] = columns[:, 0:HL]
            sums_ref[5:6, HL * p : HL * p + HL] = columns[:, 2 * HL :]
            back += dot_nt(gp, w_ref[p])
        gx_ref[...] = (mid_ref[...] + norm_back(back * vec_ref[0:1, :], n, inverse)).astype(BF)
        sums_ref[0:1, :] = jnp.sum(back * n, axis=0, keepdims=True)
        sums_ref[1:2, :] = sums_two_ref[0:1, :]
        sums_ref[2:3, :] = jnp.sum(back, axis=0, keepdims=True)
        sums_ref[3:4, :] = sums_two_ref[1:2, :]
        sums_ref[6:8, :] = sums_two_ref[2:4, :]
        for copy in written:
            copy.wait()
        arrived(weights)
        copies.drain()

    pl.when(lax.axis_index("section") == live)(act)


def attend_back(live, grads, heads, lse, up, down, x, middle_grad, w, vec, sums_two, collective_id):
    vmem = pltpu.VMEM
    count = 3 + 12 + 6 + 3 + 12 + 4 + 4
    return pl.pallas_call(
        functools.partial(attend_back_kernel, live),
        out_shape=(
            sds((4, D, 576), BF),
            sds((4, 4, 48, FF), BF),
            sds((4, 4, 4, 48, D), BF),
            sds((TOK, D), BF),
            sds((8, D), F32),
        ),
        in_specs=[pl.BlockSpec(memory_space=HBM)] * 8 + [pl.BlockSpec(memory_space=vmem)] * 2,
        out_specs=tuple([pl.BlockSpec(memory_space=HBM)] * 3 + [pl.BlockSpec(memory_space=vmem)] * 2),
        scratch_shapes=[
            vmem((4, 4, ROWS, 576), BF),
            vmem((GROUPS, BLOCK, 128), F32),
            vmem((4, 4, ROWS, HL), BF),
            vmem((4, 4, ROWS, 576), BF),
            vmem((3, SEQ_LEN, HEAD), F32),
            vmem((3, SEQ_LEN, HEAD), F32),
            vmem((4, 4, ROWS, 576), BF),
            vmem((TOK, D), BF),
            vmem((TOK, D), F32),
            vmem((4, D, 576), BF),
            vmem((4, D, 576), BF),
            pltpu.SemaphoreType.DMA((count,)),
            pltpu.SemaphoreType.DMA((count,)),
        ],
        compiler_params=pltpu.CompilerParams(
            collective_id=collective_id, has_side_effects=True, vmem_limit_bytes=60 * 1024 * 1024
        ),
    )(grads, heads, lse, up, down, x, middle_grad, w, vec, sums_two)


def mlp_kernel(
    flag, x_ref, m_ref, vec_ref, ub_ref, wo_ref, wu_ref, wd_ref, res_ref, mid_ref, raised_ref, n_ref, acc_ref
):
    step = pl.program_id(0)

    @pl.when((flag[0] == 1) & (step == 0))
    def _():
        branch = dot(m_ref[0], wo_ref[0])
        for p in range(1, 4):
            branch += dot(m_ref[p], wo_ref[p])
        middle = x_ref[...].astype(F32) + (branch + vec_ref[6:7, :])
        mid_ref[...] = middle
        n, _ = normalize(middle)
        n_ref[...] = (n * vec_ref[1:2, :] + vec_ref[3:4, :]).astype(BF)
        acc_ref[...] = middle + vec_ref[7:8, :]

    @pl.when(flag[0] == 1)
    def _():
        raised = dot(n_ref[...], wu_ref[...]) + ub_ref[0]
        raised_ref[...] = raised
        active = (0.5 * raised * (1.0 + gelu_parts(raised))).astype(BF)
        acc_ref[...] += dot(active, wd_ref[...])

    @pl.when((flag[0] == 1) & (step == 3))
    def _():
        res_ref[...] = acc_ref[...].astype(BF)


def mlp(flag, x, mixed, vec, ub, wo, wu, wd):
    return pl.pallas_call(
        mlp_kernel,
        grid_spec=flagged(
            (4,),
            [
                whole((TOK, D)),
                whole((4, TOK, HL)),
                whole((8, D)),
                pl.BlockSpec((1, 1, D), lambda j, f: (j * f[0], 0, 0)),
                whole((4, HL, D)),
                pl.BlockSpec((D, D), lambda j, f: (0, j * f[0])),
                pl.BlockSpec((D, D), lambda j, f: (j * f[0], 0)),
            ],
            (whole((TOK, D)), whole((TOK, D)), pl.BlockSpec((TOK, D), lambda j, f: (0, j * f[0]))),
            [pltpu.VMEM((TOK, D), BF), pltpu.VMEM((TOK, D), F32)],
        ),
        out_shape=(sds((TOK, D), BF), sds((TOK, D), F32), sds((TOK, FF), F32)),
        compiler_params=BIG,
    )(flag, x, mixed, vec, ub, wo, wu, wd)


def mlp_back_kernel(
    g_ref, raised_ref, mid_ref, m_ref, vec_ref, wo_ref, wu_ref, wd_ref,
    gd_ref, gu_ref, go_ref, gm_ref, gmid_ref, sums_ref, gub_ref, n_ref, acc_ref,
):
    step = pl.program_id(0)

    @pl.when(step == 0)
    def _():
        n, _ = normalize(mid_ref[...])
        n_ref[...] = (n * vec_ref[1:2, :] + vec_ref[3:4, :]).astype(BF)
        acc_ref[...] = jnp.zeros_like(acc_ref)

    g = g_ref[...]
    u = raised_ref[...]
    t = gelu_parts(u)
    active = (0.5 * u * (1.0 + t)).astype(BF)
    gd_ref[...] = dot_tn(active, g).astype(BF)
    slope = 0.5 * (1.0 + t) + 0.5 * u * (1.0 - t * t) * (
        0.7978845608 * (1.0 + 3.0 * 0.044715 * (u * u))
    )
    grad_raised = (dot_nt(g, wd_ref[...]) * slope).astype(BF)
    gub_ref[0] = jnp.sum(grad_raised.astype(F32), axis=0, keepdims=True)
    gu_ref[...] = dot_tn(n_ref[...], grad_raised).astype(BF)
    acc_ref[...] += dot_nt(grad_raised, wu_ref[...])

    @pl.when(step == 3)
    def _():
        n, inverse = normalize(mid_ref[...])
        back = acc_ref[...]
        g32 = g.astype(F32)
        grad_middle = g32 + norm_back(back * vec_ref[1:2, :], n, inverse)
        gmid_ref[...] = grad_middle
        branch = grad_middle.astype(BF)
        sums_ref[...] = jnp.zeros_like(sums_ref)
        sums_ref[0:1, :] = jnp.sum(back * n, axis=0, keepdims=True)
        sums_ref[1:2, :] = jnp.sum(back, axis=0, keepdims=True)
        sums_ref[2:3, :] = jnp.sum(branch.astype(F32), axis=0, keepdims=True)
        sums_ref[3:4, :] = jnp.sum(g32, axis=0, keepdims=True)
        for p in range(4):
            go_ref[p] = dot_tn(m_ref[p], branch).astype(BF)
            gm_ref[p] = dot_nt(branch, wo_ref[p]).astype(BF)


def mlp_back(g, raised, middle, mixed, vec, wo, wu, wd):
    return pl.pallas_call(
        mlp_back_kernel,
        grid=(4,),
        out_shape=(
            sds((FF, D), BF),
            sds((D, FF), BF),
            sds((4, HL, D), BF),
            sds((4, TOK, HL), BF),
            sds((TOK, D), F32),
            sds((8, D), F32),
            sds((4, 1, D), F32),
        ),
        in_specs=[
            whole((TOK, D)),
            pl.BlockSpec((TOK, D), lambda j: (0, j)),
            whole((TOK, D)),
            whole((4, TOK, HL)),
            whole((8, D)),
            whole((4, HL, D)),
            pl.BlockSpec((D, D), lambda j: (0, j)),
            pl.BlockSpec((D, D), lambda j: (j, 0)),
        ],
        out_specs=(
            pl.BlockSpec((D, D), lambda j: (j, 0)),
            pl.BlockSpec((D, D), lambda j: (0, j)),
            whole((4, HL, D)),
            whole((4, TOK, HL)),
            whole((TOK, D)),
            whole((8, D)),
            pl.BlockSpec((1, 1, D), lambda j: (j, 0, 0)),
        ),
        scratch_shapes=[pltpu.VMEM((TOK, D), BF), pltpu.VMEM((TOK, D), F32)],
        compiler_params=BIG,
    )(g, raised, middle, mixed, vec, wo, wu, wd)


def tile(rows):
    pads = [(0, 0)] * (rows.ndim - 2) + [(0, 8 - rows.shape[-2]), (0, 128 - rows.shape[-1])]
    return jnp.pad(rows, pads)


def backward(live, g, x, weights, saved, kept, base_id):
    qkv, wo, wu, wd, vec, ub = weights
    mixed, middle, raised = saved
    g_down, g_up, g_out, g_mixed, g_middle, sums_two, g_ub = mlp_back(
        g, raised, middle, mixed, vec, wo, wu, wd
    )
    g_up = g_up.reshape(4, 4, 48, FF)
    g_down = g_down.reshape(4, 4, 4, 48, D)
    g_qkv, up_got, down_got, g_x, sums = attend_back(
        live, g_mixed.reshape(4, 4, ROWS, HL), kept[0], kept[1], g_up, g_down, x, g_middle, qkv, vec, sums_two, base_id
    )
    small = jnp.stack(
        [tile(sums.reshape(8, 64, 12).transpose(1, 0, 2)), tile(g_ub.reshape(64, 1, 48))], axis=1
    )
    grads = (
        g_qkv.reshape(4, 4, 4, 48, 576),
        g_out.reshape(4, 4, 48, D),
        g_up,
        g_down,
        small.reshape(4, 4, 4, 2, 8, 128),
        up_got,
        down_got,
    )
    return g_x, grads


def per_device(ends, w_qkv, w_out, w_up, w_down, norm_gains, biases, up_bias):
    section = lax.axis_index("section")
    own = ends.reshape(TOK, D)
    qkv = w_qkv[0].reshape(12, 3, 4, HL).transpose(2, 0, 1, 3).reshape(4, 12, 576)
    small = jnp.stack([tile(jnp.concatenate([norm_gains[0], biases[0]])), tile(up_bias)]).astype(F32)
    q_y, o_y, u_y, d_x, s_x = gather_first(qkv, w_out[0], w_up[0], w_down[0], small)
    qkv, u_z, d_a, d_b, small = gather_qkv(
        q_y.transpose(1, 0, 2, 3).reshape(4, 48, 576), u_y.reshape(48, FF), d_x, s_x
    )
    qkv = qkv.reshape(4, D, 576)
    small = small.reshape(64, 2, 8, 128)
    vec = small[:, 0, :, :12].transpose(1, 0, 2).reshape(8, D)
    ub = small[:, 1, 0, :48].reshape(4, 1, D)

    flag = (section == 0).astype(jnp.int32).reshape(1)
    projected = project(flag, own, vec, qkv).reshape(4, 4, ROWS, 576)
    *kept, out, up, down = attend(True, (projected, o_y.reshape(48, D), u_z, d_a, d_b), 3)
    out, up, down = out.reshape(4, HL, D), up.reshape(D, FF), down.reshape(FF, D)
    result, _, _ = mlp(flag, own, kept[2].reshape(4, TOK, HL), vec, ub, out, up, down)
    arriving = lax.ppermute(result, "section", [(0, 1)])
    x = jnp.where(section == 0, own, arriving)
    flag = jnp.ones((1,), jnp.int32)
    projected = project(flag, x, vec, qkv).reshape(4, 4, ROWS, 576)
    kept = attend(False, (projected, *kept), 4)
    mixed = kept[2].reshape(4, TOK, HL)
    result, middle, raised = mlp(flag, x, mixed, vec, ub, out, up, down)
    weights, saved = (qkv, out, up, down, vec, ub), (mixed, middle, raised)

    g_x, grads = backward(1, own, x, weights, saved, kept, 5)
    arriving = lax.ppermute(g_x, "section", [(1, 0)])
    grads, arriving = lax.optimization_barrier((grads, arriving))
    totals = reduce_grads(1, *grads, None, 7)
    totals, arriving = lax.optimization_barrier((totals, arriving))
    g = jnp.where(section == 1, own, arriving)
    g_x, grads = backward(0, g, x, weights, saved, kept, 6)
    q, o, u, d, s = reduce_grads(0, *grads, totals, 8)
    boundary = jnp.where(section == 0, g_x, result)
    return (
        boundary.reshape(1, 1, GROUPS, ROWS, D),
        q,
        o,
        u,
        d,
        s[0:1, 0:2, :12],
        s[0:1, 2:8, :12],
        s[1:2, 0, :48],
    )


def solution(mesh):
    rows = P("section", ("seq", "shard"), None)
    columns = P("section", None, ("seq", "shard"))
    ends = P("section", "shard", None, "seq", None)
    hidden = P("section", ("seq", "shard"))
    placed = (ends, rows, rows, rows, rows, columns, columns, hidden)
    return jax.shard_map(per_device, mesh=mesh, in_specs=placed, out_specs=placed, check_vma=False)
```

```python
import functools

import jax
import jax.numpy as jnp
from jax import lax
from jax.experimental import pallas as pl
from jax.experimental.pallas import tpu as pltpu
from jax.sharding import PartitionSpec as P

HEAD = 64
FF = 3072
D = 768
GROUPS = 4
ROWS = 64
TOK = GROUPS * ROWS
SEQ_LEN = 1024
HL = 192
EPSILON = 1e-05
MASKED = -1e30
BF = jnp.bfloat16
F32 = jnp.float32
MESH = pl.DeviceIdType.MESH
HBM = pltpu.HBM


def sds(shape, dtype):
    return jax.ShapeDtypeStruct(shape, dtype)


def coords():
    shard = lax.axis_index("shard")
    return {"x": shard // 4, "y": lax.rem(shard, 4), "z": lax.axis_index("seq")}


def peer(c, axis, by):
    moved = dict(c)
    moved[axis] = lax.rem(c[axis] + by, 4)
    return {"section": lax.axis_index("section"), "seq": moved["z"], "shard": moved["x"] * 4 + moved["y"]}


def partner():
    return {
        "section": 1 - lax.axis_index("section"),
        "seq": lax.axis_index("seq"),
        "shard": lax.axis_index("shard"),
    }


def meet(c, axes, steps, with_partner=False):
    barrier = pltpu.get_barrier_semaphore()
    if with_partner:
        pl.semaphore_signal(barrier, inc=1, device_id=partner(), device_id_type=MESH)
    for axis in axes:
        for by in steps:
            pl.semaphore_signal(barrier, inc=1, device_id=peer(c, axis, by), device_id_type=MESH)
    pl.semaphore_wait(barrier, len(axes) * len(steps) + int(with_partner))


class Copies:
    def __init__(self, send, recv):
        self.send, self.recv, self.used, self.sent = send, recv, 0, []

    def remote(self, src, dst, to):
        copy = pltpu.make_async_remote_copy(
            src_ref=src,
            dst_ref=dst,
            send_sem=self.send.at[self.used],
            recv_sem=self.recv.at[self.used],
            device_id=to,
            device_id_type=MESH,
        )
        self.used += 1
        copy.start()
        self.sent.append(copy)
        return copy

    def local(self, src, dst):
        copy = pltpu.make_async_copy(src, dst, self.send.at[self.used])
        self.used += 1
        copy.start()
        return copy

    def drain(self):
        for copy in self.sent:
            copy.wait_send()


class Gather:
    def __init__(self, copies, c, axis, own, dst, half):
        self.copies, self.c, self.axis, self.own, self.dst, self.half = copies, c, axis, own, dst, half

    def first(self):
        a = self.c[self.axis]
        self.right, self.left = peer(self.c, self.axis, 1), peer(self.c, self.axis, 3)
        self.go_right = self.copies.remote(self.own, self.dst(a), self.right)
        self.go_left = self.copies.remote(self.own, self.dst(a), self.left)

    def second(self):
        a = self.c[self.axis]
        before, after = lax.rem(a + 3, 4), lax.rem(a + 1, 4)
        self.go_right.wait_recv()
        self.on_right = self.copies.remote(self.half(before, 0), self.half(before, 0), self.right)
        self.go_left.wait_recv()
        self.on_left = self.copies.remote(self.half(after, 1), self.half(after, 1), self.left)

    def third(self):
        self.on_right.wait_recv()
        self.on_left.wait_recv()


def run_gathers(gathers):
    for g in gathers:
        g.first()
    for g in gathers:
        g.second()


def gather_kernel(q_in, o_in, u_in, d_in, s_in, q, o, u, d, s, *scratch):
    q_y, o_y, u_y, d_x, s_x, q_b, o_b, u_b, tmp, send, recv, turn = scratch
    c = coords()
    x, y, z = c["x"], c["y"], c["z"]
    copies = Copies(send, recv)
    lanes = lambda ref, i, h, n: ref.at[i, :, pl.ds(n * h, n)]
    zero = [
        Gather(copies, c, "y", u_in, lambda i: u_y.at[i], lambda i, h: lanes(u_y, i, h, 1536)),
        Gather(copies, c, "y", q_in, lambda i: q_y.at[i], lambda i, h: q_y.at[i, pl.ds(2 * h, 2)]),
        Gather(copies, c, "y", o_in, lambda i: o_y.at[i], lambda i, h: lanes(o_y, i, h, 384)),
        Gather(copies, c, "x", d_in, lambda i: d_x.at[i], lambda i, h: lanes(d_x, i, h, 384)),
        Gather(copies, c, "x", s_in, lambda i: s_x.at[i], lambda i, h: s_x.at[i, h]),
    ]
    u_y[y] = u_in[...]
    q_y[y] = q_in[...]
    o_y[y] = o_in[...]
    d_x[x] = d_in[...]
    s_x[x] = s_in[...]
    meet(c, ("x", "y", "z"), (1, 3), True)
    run_gathers(zero)
    zero[0].third()
    for k in range(4):
        for i in range(4):
            tmp[12 * i : 12 * i + 12, :] = u_y[i, :, D * k : D * k + D].astype(F32)
        u_b[:, D * k : D * k + D] = tmp[...].astype(BF)
    zero[1].third()
    for p in range(4):
        for i in range(4):
            tmp[12 * i : 12 * i + 12, 0:576] = q_y[i, p].astype(F32)
        q_b[p] = tmp[:, 0:576].astype(BF)
    zero[2].third()
    for i in range(4):
        tmp[12 * i : 12 * i + 12, :] = o_y[i].astype(F32)
    o_b[...] = tmp[...].astype(BF)
    zero[3].third()
    zero[4].third()

    @pl.when(lax.axis_index("section") == 1)
    def _():
        pl.semaphore_wait(turn, 1)

    one = [
        Gather(copies, c, "z", q_b, lambda i: q.at[:, i, x], lambda i, h: q.at[pl.ds(2 * h, 2), i, x]),
        Gather(copies, c, "z", o_b, lambda i: o.at[i, x], lambda i, h: o.at[i, x, :, pl.ds(384 * h, 384)]),
        Gather(copies, c, "x", u_b, lambda i: u.at[z, i], lambda i, h: u.at[z, i, :, pl.ds(1536 * h, 1536)]),
        Gather(copies, c, "z", d_x, lambda i: d.at[i, :, y], lambda i, h: d.at[i, pl.ds(2 * h, 2), y]),
        Gather(copies, c, "z", s_x, lambda i: s.at[i, :, y], lambda i, h: s.at[i, pl.ds(2 * h, 2), y]),
    ]
    own = [
        copies.local(q_b, q.at[:, z, x]),
        copies.local(o_b, o.at[z, x]),
        copies.local(u_b, u.at[z, x]),
        copies.local(d_x, d.at[z, :, y]),
        copies.local(s_x, s.at[z, :, y]),
    ]
    run_gathers(one)
    two = [
        Gather(copies, c, "x", q.at[:, :, x], lambda i: q.at[:, :, i], lambda i, h: q.at[pl.ds(2 * h, 2), :, i]),
        Gather(copies, c, "x", o.at[:, x], lambda i: o.at[:, i], lambda i, h: o.at[pl.ds(2 * h, 2), i]),
        Gather(copies, c, "z", u.at[z], lambda i: u.at[i], lambda i, h: u.at[i, pl.ds(2 * h, 2)]),
        Gather(copies, c, "y", d.at[:, :, y], lambda i: d.at[:, :, i], lambda i, h: d.at[pl.ds(2 * h, 2), :, i]),
        Gather(copies, c, "y", s.at[:, :, y], lambda i: s.at[:, :, i], lambda i, h: s.at[pl.ds(2 * h, 2), :, i]),
    ]
    for k in range(5):
        one[k].third()
        own[k].wait()
        two[k].first()
    for g in two:
        g.second()

    @pl.when(lax.axis_index("section") == 0)
    def _():
        pl.semaphore_signal(turn, inc=1, device_id=partner(), device_id_type=MESH)

    for g in two:
        g.third()
    copies.drain()


def gather(qkv, out, up, down, small):
    vmem = pltpu.VMEM
    count = 15 * 4 + 5
    return pl.pallas_call(
        gather_kernel,
        out_shape=(
            sds((4, 4, 4, 48, 576), BF),
            sds((4, 4, 48, D), BF),
            sds((4, 4, 48, FF), BF),
            sds((4, 4, 4, 48, D), BF),
            sds((4, 4, 4, 2, 8, 128), F32),
        ),
        in_specs=[pl.BlockSpec(memory_space=vmem)] * 5,
        out_specs=tuple([pl.BlockSpec(memory_space=HBM)] * 5),
        scratch_shapes=[
            vmem((4, 4, 12, 576), BF),
            vmem((4, 12, D), BF),
            vmem((4, 12, FF), BF),
            vmem((4, 48, D), BF),
            vmem((4, 2, 8, 128), F32),
            vmem((4, 48, 576), BF),
            vmem((48, D), BF),
            vmem((48, FF), BF),
            vmem((48, D), F32),
            pltpu.SemaphoreType.DMA((count,)),
            pltpu.SemaphoreType.DMA((count,)),
            pltpu.SemaphoreType.REGULAR,
        ],
        compiler_params=pltpu.CompilerParams(
            collective_id=1, has_side_effects=True, vmem_limit_bytes=60 * 1024 * 1024
        ),
    )(qkv, out, up, down, small)


def spread(copies, c, axis, source, target):
    moves = []
    for by in (2, 1, 3):
        there = lax.rem(c[axis] + by, 4)
        moves.append(copies.remote(source(there), target.at[by], peer(c, axis, by)))
    return moves


def arrived(moves):
    for move in moves:
        move.wait_recv()


def add(ref, at):
    total = ref[(0,) + at].astype(F32)
    for k in range(1, 4):
        total += ref[(k,) + at].astype(F32)
    return total


def more(mine, ref, at):
    total = mine.astype(F32)
    for k in range(1, 4):
        total += ref[(k,) + at].astype(F32)
    return total


def reduce_kernel(live, q_in, o_in, u_in, d_in, s_in, o_got, u_got, d_got, q, o, u, d, s, *scratch):
    qa1, qb1, o1, u1, d1, s1, qa2, qb2, o2, u2, d2, s2, tmp, qs, os, us, q3, o3, u3, d3, s3, send, recv = scratch

    def act():
        c = coords()
        x, y, z = c["x"], c["y"], c["z"]
        copies = Copies(send, recv)
        own_d = [copies.local(d_in.at[:, :, y], d1.at[0]), copies.local(d_got.at[pl.ds(1, 3)], d1.at[pl.ds(1, 3)])]
        own_u = [copies.local(u_in.at[:, x], u1.at[0]), copies.local(u_got.at[pl.ds(1, 3)], u1.at[pl.ds(1, 3)])]
        own_qa = copies.local(q_in.at[pl.ds(0, 2), :, x], qa1.at[0])
        own_qb = copies.local(q_in.at[pl.ds(2, 2), z], qb1.at[0])
        own_o = [copies.local(o_in.at[z], o1.at[0]), copies.local(o_got.at[pl.ds(1, 3)], o1.at[pl.ds(1, 3)])]
        own_s = copies.local(s_in.at[:, :, y], s1.at[0])
        meet(c, ("x", "y", "z"), (1, 2, 3))
        one_qa = spread(copies, c, "x", lambda i: q_in.at[pl.ds(0, 2), :, i], qa1)
        one_qb = spread(copies, c, "z", lambda i: q_in.at[pl.ds(2, 2), i], qb1)
        one_s = spread(copies, c, "y", lambda i: s_in.at[:, :, i], s1)

        def add_all(ref, rows, kind):
            @pl.loop(0, rows * 4)
            def _(i):
                at = (i // 4, lax.rem(i, 4))
                ref[(0,) + at] = add(ref, at).astype(kind)

        for copy in own_d:
            copy.wait()
        add_all(d1, 4, BF)
        two_d = spread(copies, c, "x", lambda i: d1.at[0, :, i], d2)
        for copy in own_u:
            copy.wait()

        @pl.loop(0, 4)
        def _(i):
            for k in range(4):
                at = (i, slice(None), pl.ds(D * k, D))
                u1[(0,) + at] = add(u1, at).astype(BF)

        two_u = spread(copies, c, "z", lambda i: u1.at[0, i], u2)
        for copy in own_o:
            copy.wait()

        @pl.loop(0, 4)
        def _(i):
            o1[0, i] = add(o1, (i,)).astype(BF)

        two_o = spread(copies, c, "x", lambda i: o1.at[0, i], o2)
        arrived(one_qa)
        own_qa.wait()
        add_all(qa1, 2, BF)
        two_qa = spread(copies, c, "z", lambda i: qa1.at[0, :, i], qa2)
        arrived(one_qb)
        own_qb.wait()
        add_all(qb1, 2, BF)
        two_qb = spread(copies, c, "x", lambda i: qb1.at[0, :, i], qb2)
        arrived(one_s)
        own_s.wait()
        add_all(s1, 4, F32)
        two_s = spread(copies, c, "z", lambda i: s1.at[0, i], s2)
        arrived(two_d)

        @pl.loop(0, 4)
        def _(i):
            d2[0, i] = more(d1[0, i, x], d2, (i,)).astype(BF)

        three_d = spread(copies, c, "z", lambda i: d2.at[0, i], d3)
        arrived(two_u)
        for k in range(4):
            at = (slice(None), pl.ds(D * k, D))
            tmp[...] = more(u1[(0, z) + at], u2, at)
            for i in range(4):
                us[i, :, D * k : D * k + D] = tmp[12 * i : 12 * i + 12, :].astype(BF)
        three_u = spread(copies, c, "y", lambda i: us.at[i], u3)
        arrived(two_qa)
        arrived(two_qb)
        for p in range(4):
            if p < 2:
                tmp[:, 0:576] = more(qa1[0, p, z], qa2, (p,))
            else:
                tmp[:, 0:576] = more(qb1[0, p - 2, x], qb2, (p - 2,))
            for i in range(4):
                qs[i, p] = tmp[12 * i : 12 * i + 12, 0:576].astype(BF)
        three_q = spread(copies, c, "y", lambda i: qs.at[i], q3)
        arrived(two_o)
        tmp[...] = more(o1[0, x], o2, ())
        for i in range(4):
            os[i] = tmp[12 * i : 12 * i + 12, :].astype(BF)
        three_o = spread(copies, c, "y", lambda i: os.at[i], o3)
        arrived(two_s)

        @pl.loop(0, 4)
        def _(i):
            s2[0, i] = more(s1[0, z, i], s2, (i,))

        three_s = spread(copies, c, "x", lambda i: s2.at[0, i], s3)
        arrived(three_d)
        d[...] = more(d2[0, z], d3, ())
        arrived(three_u)
        u[...] = more(us[y], u3, ())
        arrived(three_q)
        for p in range(4):
            total = more(qs[y, p], q3, (p,))
            for kind in range(3):
                at = D * kind + HL * p
                q[:, at : at + HL] = total[:, HL * kind : HL * kind + HL]
        arrived(three_o)
        o[...] = more(os[y], o3, ())
        arrived(three_s)
        s[...] = more(s2[0, x], s3, ())
        copies.drain()

    pl.when(lax.axis_index("section") == live)(act)


def reduce_grads(live, qkv, out, up, down, small, out_got, up_got, down_got, collective_id):
    vmem = pltpu.VMEM
    count = 9 + 9 + 18 + 15
    return pl.pallas_call(
        functools.partial(reduce_kernel, live),
        out_shape=(
            sds((12, 3 * D), F32),
            sds((12, D), F32),
            sds((12, FF), F32),
            sds((48, D), F32),
            sds((2, 8, 128), F32),
        ),
        in_specs=[pl.BlockSpec(memory_space=HBM)] * 8,
        out_specs=tuple([pl.BlockSpec(memory_space=vmem)] * 5),
        scratch_shapes=[
            vmem((4, 2, 4, 48, 576), BF),
            vmem((4, 2, 4, 48, 576), BF),
            vmem((4, 4, 48, D), BF),
            vmem((4, 4, 48, FF), BF),
            vmem((4, 4, 4, 48, D), BF),
            vmem((4, 4, 4, 2, 8, 128), F32),
            vmem((4, 2, 48, 576), BF),
            vmem((4, 2, 48, 576), BF),
            vmem((4, 48, D), BF),
            vmem((4, 48, FF), BF),
            vmem((4, 4, 48, D), BF),
            vmem((4, 4, 2, 8, 128), F32),
            vmem((48, D), F32),
            vmem((4, 4, 12, 576), BF),
            vmem((4, 12, D), BF),
            vmem((4, 12, FF), BF),
            vmem((4, 4, 12, 576), BF),
            vmem((4, 12, D), BF),
            vmem((4, 12, FF), BF),
            vmem((4, 48, D), BF),
            vmem((4, 2, 8, 128), F32),
            pltpu.SemaphoreType.DMA((count,)),
            pltpu.SemaphoreType.DMA((count,)),
        ],
        compiler_params=pltpu.CompilerParams(
            collective_id=collective_id, has_side_effects=True, vmem_limit_bytes=60 * 1024 * 1024
        ),
    )(qkv, out, up, down, small, out_got, up_got, down_got)


BIG = pltpu.CompilerParams(vmem_limit_bytes=56 * 1024 * 1024)


def dot(a, b):
    return jnp.dot(a, b, preferred_element_type=F32)


def dot_nt(a, b):
    return lax.dot_general(a, b, (((1,), (1,)), ((), ())), preferred_element_type=F32)


def dot_tn(a, b):
    return lax.dot_general(a, b, (((0,), (0,)), ((), ())), preferred_element_type=F32)


def normalize(values):
    centered = values - jnp.mean(values, axis=-1, keepdims=True)
    spread = jnp.mean(centered * centered, axis=-1, keepdims=True)
    inverse = lax.rsqrt(spread + EPSILON)
    return centered * inverse, inverse


def norm_back(e, n, inverse):
    return inverse * (
        e - jnp.mean(e, axis=-1, keepdims=True) - n * jnp.mean(e * n, axis=-1, keepdims=True)
    )


def gelu_parts(u):
    inner = 0.7978845608 * (u + 0.044715 * (u * u * u))
    t = jnp.tanh(inner)
    return t


def whole(shape):
    zeros = (0,) * len(shape)
    return pl.BlockSpec(shape, lambda *unused: zeros)


def flagged(grid, in_specs, out_specs, scratch):
    return pltpu.PrefetchScalarGridSpec(
        num_scalar_prefetch=1, grid=grid, in_specs=in_specs, out_specs=out_specs, scratch_shapes=scratch
    )


def project_kernel(flag, x_ref, vec_ref, w_ref, out_ref, n_ref, bias_ref):
    step = pl.program_id(0)

    @pl.when((flag[0] == 1) & (step == 0))
    def _():
        n, _ = normalize(x_ref[...].astype(F32))
        n_ref[...] = (n * vec_ref[0:1, :] + vec_ref[2:3, :]).astype(BF)
        bias_ref[...] = jnp.zeros_like(bias_ref)
        for p in range(4):
            bias_ref[p, :, 0:HL] = vec_ref[4:5, HL * p : HL * p + HL]
            bias_ref[p, :, 2 * HL :] = vec_ref[5:6, HL * p : HL * p + HL]

    @pl.when(flag[0] == 1)
    def _():
        out_ref[0] = (dot(n_ref[...], w_ref[0]) + bias_ref[step]).astype(BF)


def project(flag, x, vec, w):
    return pl.pallas_call(
        project_kernel,
        grid_spec=flagged(
            (4,),
            [
                whole((TOK, D)),
                whole((8, D)),
                pl.BlockSpec((1, D, 576), lambda j, f: (j * f[0], 0, 0)),
            ],
            pl.BlockSpec((1, TOK, 576), lambda j, f: (j * f[0], 0, 0)),
            [pltpu.VMEM((TOK, D), BF), pltpu.VMEM((4, 1, 576), F32)],
        ),
        out_shape=sds((4, TOK, 576), BF),
        compiler_params=BIG,
    )(flag, x, vec, w)


BLOCK = 256


def masked(scores, block):
    rows = block * BLOCK + lax.broadcasted_iota(jnp.int32, scores.shape, 0)
    cols = lax.broadcasted_iota(jnp.int32, scores.shape, 1)
    return jnp.where(cols <= rows, scores, MASKED)


def attend_kernel(live, with_previous, p_in, *refs):
    if with_previous:
        refs = refs[3:]
    h_out, lse_out, m_out, h_ref, m_ref, lse_ref, send, recv = refs

    def act():
        c = coords()
        z = c["z"]
        copies = Copies(send, recv)
        own = copies.local(p_in.at[z], h_ref.at[:, z])
        meet(c, ("z",), (1, 2, 3))
        coming, kept = [], []
        for g in range(GROUPS):
            for by in (2, 1, 3):
                to = peer(c, "z", by)
                coming.append(copies.remote(p_in.at[to["seq"], g], h_ref.at[g, z], to))
        own.wait()
        leaving = []
        for g in range(GROUPS):
            arrived(coming[3 * g : 3 * g + 3])
            kept.append(copies.local(h_ref.at[g], h_out.at[g]))
            keys = (g + 1) * BLOCK
            for head in range(3):
                q_at, k_at, v_at = HEAD * head, HL + HEAD * head, 2 * HL + HEAD * head
                q = h_ref[g, :, :, q_at : q_at + HEAD].reshape(BLOCK, HEAD) * jnp.asarray(0.125, BF)
                k = h_ref[0 : g + 1, :, :, k_at : k_at + HEAD].reshape(keys, HEAD)
                v = h_ref[0 : g + 1, :, :, v_at : v_at + HEAD].reshape(keys, HEAD)
                scores = masked(dot_nt(q, k), g)
                top = jnp.max(scores, axis=-1, keepdims=True)
                e = jnp.exp(scores - top)
                total = jnp.sum(e, axis=-1, keepdims=True)
                mixed = (dot(e.astype(BF), v) / total).astype(BF)
                m_ref[g, :, :, q_at : q_at + HEAD] = mixed.reshape(4, ROWS, HEAD)
                lse_ref[g, :, head : head + 1] = top + jnp.log(total)
            for by in (2, 1, 3):
                to = peer(c, "z", by)
                leaving.append(copies.remote(m_ref.at[g, to["seq"]], m_out.at[z, g], to))
            kept.append(copies.local(m_ref.at[g, z], m_out.at[z, g]))
        kept.append(copies.local(lse_ref, lse_out))
        arrived(leaving)
        for copy in kept:
            copy.wait()
        copies.drain()

    pl.when(lax.axis_index("section") == live)(act)


def attend(live, projected, previous, collective_id):
    ins, aliases = (projected,), {}
    if previous is not None:
        ins, aliases = ins + tuple(previous), {1: 0, 2: 1, 3: 2}
    count = 1 + 12 + 4 + 12 + 4 + 1
    return pl.pallas_call(
        functools.partial(attend_kernel, live, previous is not None),
        out_shape=(
            sds((4, 4, ROWS, 576), BF),
            sds((GROUPS, BLOCK, 128), F32),
            sds((4, 4, ROWS, HL), BF),
        ),
        in_specs=[pl.BlockSpec(memory_space=HBM)] * len(ins),
        out_specs=tuple([pl.BlockSpec(memory_space=HBM)] * 3),
        scratch_shapes=[
            pltpu.VMEM((4, 4, ROWS, 576), BF),
            pltpu.VMEM((4, 4, ROWS, HL), BF),
            pltpu.VMEM((GROUPS, BLOCK, 128), F32),
            pltpu.SemaphoreType.DMA((count,)),
            pltpu.SemaphoreType.DMA((count,)),
        ],
        input_output_aliases=aliases,
        compiler_params=pltpu.CompilerParams(
            collective_id=collective_id, has_side_effects=True, vmem_limit_bytes=60 * 1024 * 1024
        ),
    )(*ins)


def attend_back_kernel(
    live, g_in, h_hbm, lse_hbm, o_in, u_in, d_in, x_hbm, mid_hbm, w_hbm, vec_ref, sums_two_ref,
    gw_out, o_out, u_out, d_out, gx_ref, sums_ref,
    h_ref, lse_ref, gh_ref, gs_ref, dk_ref, dv_ref, p_ref, x_ref, mid_ref, w_ref, gw_ref, send, recv,
):
    def act():
        c = coords()
        z = c["z"]
        copies = Copies(send, recv)
        own = [
            copies.local(g_in.at[z], gh_ref.at[:, z]),
            copies.local(h_hbm, h_ref),
            copies.local(lse_hbm, lse_ref),
        ]
        meet(c, ("x", "y", "z"), (1, 2, 3))
        coming, leaving, kept = {}, [], []
        for g in reversed(range(GROUPS)):
            coming[g] = []
            for by in (2, 1, 3):
                to = peer(c, "z", by)
                coming[g].append(copies.remote(g_in.at[to["seq"], g], gh_ref.at[g, z], to))
        weights = spread(copies, c, "y", lambda i: d_in.at[:, :, i], d_out)
        weights += spread(copies, c, "x", lambda i: u_in.at[:, i], u_out)
        weights += spread(copies, c, "z", lambda i: o_in.at[i], o_out)
        later = [copies.local(x_hbm, x_ref), copies.local(mid_hbm, mid_ref), copies.local(w_hbm, w_ref)]
        for copy in own:
            copy.wait()
        for g in reversed(range(GROUPS)):
            arrived(coming[g])
            keys = (g + 1) * BLOCK
            for head in range(3):
                q_at, k_at, v_at = HEAD * head, HL + HEAD * head, 2 * HL + HEAD * head
                q = h_ref[g, :, :, q_at : q_at + HEAD].reshape(BLOCK, HEAD) * jnp.asarray(0.125, BF)
                k = h_ref[0 : g + 1, :, :, k_at : k_at + HEAD].reshape(keys, HEAD)
                v = h_ref[0 : g + 1, :, :, v_at : v_at + HEAD].reshape(keys, HEAD)
                grad = gh_ref[g, :, :, q_at : q_at + HEAD].reshape(BLOCK, HEAD)
                scores = masked(dot_nt(q, k), g)
                p = jnp.exp(scores - lse_ref[g, :, head : head + 1])
                dp = dot_nt(grad, v)
                centre = jnp.sum(p * dp, axis=-1, keepdims=True)
                ds = (p * (dp - centre)).astype(BF)
                dq = (dot(ds, k) * 0.125).astype(BF)
                gs_ref[g, :, :, q_at : q_at + HEAD] = dq.reshape(4, ROWS, HEAD)
                dk = dot_tn(ds, q)
                dv = dot_tn(p.astype(BF), grad)
                if g < GROUPS - 1:
                    dk += dk_ref[head, 0:keys, :]
                    dv += dv_ref[head, 0:keys, :]
                if g > 0:
                    dk_ref[head, 0 : keys - BLOCK, :] = dk[: keys - BLOCK]
                    dv_ref[head, 0 : keys - BLOCK, :] = dv[: keys - BLOCK]
                gs_ref[g, :, :, k_at : k_at + HEAD] = dk[keys - BLOCK :].astype(BF).reshape(4, ROWS, HEAD)
                gs_ref[g, :, :, v_at : v_at + HEAD] = dv[keys - BLOCK :].astype(BF).reshape(4, ROWS, HEAD)
            for by in (2, 1, 3):
                to = peer(c, "z", by)
                leaving.append(copies.remote(gs_ref.at[g, to["seq"]], p_ref.at[z, g], to))
            kept.append(copies.local(gs_ref.at[g, z], p_ref.at[z, g]))
        for copy in later:
            copy.wait()
        n, inverse = normalize(x_ref[...].astype(F32))
        normed = (n * vec_ref[0:1, :] + vec_ref[2:3, :]).astype(BF)
        arrived(leaving)
        for copy in kept:
            copy.wait()
        back = jnp.zeros((TOK, D), F32)
        written = []
        for p in range(4):
            gp = p_ref[p].reshape(TOK, 576)
            gw_ref[p] = dot_tn(normed, gp).astype(BF)
            written.append(copies.local(gw_ref.at[p], gw_out.at[p]))
            columns = jnp.sum(gp.astype(F32), axis=0, keepdims=True)
            sums_ref[4:5, HL * p : HL * p + HL] = columns[:, 0:HL]
            sums_ref[5:6, HL * p : HL * p + HL] = columns[:, 2 * HL :]
            back += dot_nt(gp, w_ref[p])
        gx_ref[...] = (mid_ref[...] + norm_back(back * vec_ref[0:1, :], n, inverse)).astype(BF)
        sums_ref[0:1, :] = jnp.sum(back * n, axis=0, keepdims=True)
        sums_ref[1:2, :] = sums_two_ref[0:1, :]
        sums_ref[2:3, :] = jnp.sum(back, axis=0, keepdims=True)
        sums_ref[3:4, :] = sums_two_ref[1:2, :]
        sums_ref[6:8, :] = sums_two_ref[2:4, :]
        for copy in written:
            copy.wait()
        arrived(weights)
        copies.drain()

    pl.when(lax.axis_index("section") == live)(act)


def attend_back(live, grads, heads, lse, out, up, down, x, middle_grad, w, vec, sums_two, collective_id):
    vmem = pltpu.VMEM
    count = 3 + 12 + 9 + 3 + 12 + 4 + 4
    return pl.pallas_call(
        functools.partial(attend_back_kernel, live),
        out_shape=(
            sds((4, D, 576), BF),
            sds((4, 4, 48, D), BF),
            sds((4, 4, 48, FF), BF),
            sds((4, 4, 4, 48, D), BF),
            sds((TOK, D), BF),
            sds((8, D), F32),
        ),
        in_specs=[pl.BlockSpec(memory_space=HBM)] * 9 + [pl.BlockSpec(memory_space=vmem)] * 2,
        out_specs=tuple([pl.BlockSpec(memory_space=HBM)] * 4 + [pl.BlockSpec(memory_space=vmem)] * 2),
        scratch_shapes=[
            vmem((4, 4, ROWS, 576), BF),
            vmem((GROUPS, BLOCK, 128), F32),
            vmem((4, 4, ROWS, HL), BF),
            vmem((4, 4, ROWS, 576), BF),
            vmem((3, SEQ_LEN, HEAD), F32),
            vmem((3, SEQ_LEN, HEAD), F32),
            vmem((4, 4, ROWS, 576), BF),
            vmem((TOK, D), BF),
            vmem((TOK, D), F32),
            vmem((4, D, 576), BF),
            vmem((4, D, 576), BF),
            pltpu.SemaphoreType.DMA((count,)),
            pltpu.SemaphoreType.DMA((count,)),
        ],
        compiler_params=pltpu.CompilerParams(
            collective_id=collective_id, has_side_effects=True, vmem_limit_bytes=60 * 1024 * 1024
        ),
    )(grads, heads, lse, out, up, down, x, middle_grad, w, vec, sums_two)


def mlp_kernel(
    flag, x_ref, m_ref, vec_ref, ub_ref, wo_ref, wu_ref, wd_ref, res_ref, mid_ref, raised_ref, n_ref, acc_ref
):
    step = pl.program_id(0)

    @pl.when((flag[0] == 1) & (step == 0))
    def _():
        branch = dot(m_ref[0], wo_ref[0])
        for p in range(1, 4):
            branch += dot(m_ref[p], wo_ref[p])
        middle = x_ref[...].astype(F32) + (branch + vec_ref[6:7, :])
        mid_ref[...] = middle
        n, _ = normalize(middle)
        n_ref[...] = (n * vec_ref[1:2, :] + vec_ref[3:4, :]).astype(BF)
        acc_ref[...] = middle + vec_ref[7:8, :]

    @pl.when(flag[0] == 1)
    def _():
        raised = dot(n_ref[...], wu_ref[...]) + ub_ref[0]
        raised_ref[...] = raised
        active = (0.5 * raised * (1.0 + gelu_parts(raised))).astype(BF)
        acc_ref[...] += dot(active, wd_ref[...])

    @pl.when((flag[0] == 1) & (step == 3))
    def _():
        res_ref[...] = acc_ref[...].astype(BF)


def mlp(flag, x, mixed, vec, ub, wo, wu, wd):
    return pl.pallas_call(
        mlp_kernel,
        grid_spec=flagged(
            (4,),
            [
                whole((TOK, D)),
                whole((4, TOK, HL)),
                whole((8, D)),
                pl.BlockSpec((1, 1, D), lambda j, f: (j * f[0], 0, 0)),
                whole((4, HL, D)),
                pl.BlockSpec((D, D), lambda j, f: (0, j * f[0])),
                pl.BlockSpec((D, D), lambda j, f: (j * f[0], 0)),
            ],
            (whole((TOK, D)), whole((TOK, D)), pl.BlockSpec((TOK, D), lambda j, f: (0, j * f[0]))),
            [pltpu.VMEM((TOK, D), BF), pltpu.VMEM((TOK, D), F32)],
        ),
        out_shape=(sds((TOK, D), BF), sds((TOK, D), F32), sds((TOK, FF), F32)),
        compiler_params=BIG,
    )(flag, x, mixed, vec, ub, wo, wu, wd)


def mlp_back_kernel(
    g_ref, raised_ref, mid_ref, m_ref, vec_ref, wo_ref, wu_ref, wd_ref,
    gd_ref, gu_ref, go_ref, gm_ref, gmid_ref, sums_ref, gub_ref, n_ref, acc_ref,
):
    step = pl.program_id(0)

    @pl.when(step == 0)
    def _():
        n, _ = normalize(mid_ref[...])
        n_ref[...] = (n * vec_ref[1:2, :] + vec_ref[3:4, :]).astype(BF)
        acc_ref[...] = jnp.zeros_like(acc_ref)

    g = g_ref[...]
    u = raised_ref[...]
    t = gelu_parts(u)
    active = (0.5 * u * (1.0 + t)).astype(BF)
    gd_ref[...] = dot_tn(active, g).astype(BF)
    slope = 0.5 * (1.0 + t) + 0.5 * u * (1.0 - t * t) * (
        0.7978845608 * (1.0 + 3.0 * 0.044715 * (u * u))
    )
    grad_raised = (dot_nt(g, wd_ref[...]) * slope).astype(BF)
    gub_ref[0] = jnp.sum(grad_raised.astype(F32), axis=0, keepdims=True)
    gu_ref[...] = dot_tn(n_ref[...], grad_raised).astype(BF)
    acc_ref[...] += dot_nt(grad_raised, wu_ref[...])

    @pl.when(step == 3)
    def _():
        n, inverse = normalize(mid_ref[...])
        back = acc_ref[...]
        g32 = g.astype(F32)
        grad_middle = g32 + norm_back(back * vec_ref[1:2, :], n, inverse)
        gmid_ref[...] = grad_middle
        branch = grad_middle.astype(BF)
        sums_ref[...] = jnp.zeros_like(sums_ref)
        sums_ref[0:1, :] = jnp.sum(back * n, axis=0, keepdims=True)
        sums_ref[1:2, :] = jnp.sum(back, axis=0, keepdims=True)
        sums_ref[2:3, :] = jnp.sum(branch.astype(F32), axis=0, keepdims=True)
        sums_ref[3:4, :] = jnp.sum(g32, axis=0, keepdims=True)
        for p in range(4):
            go_ref[p] = dot_tn(m_ref[p], branch).astype(BF)
            gm_ref[p] = dot_nt(branch, wo_ref[p]).astype(BF)


def mlp_back(g, raised, middle, mixed, vec, wo, wu, wd):
    return pl.pallas_call(
        mlp_back_kernel,
        grid=(4,),
        out_shape=(
            sds((FF, D), BF),
            sds((D, FF), BF),
            sds((4, HL, D), BF),
            sds((4, TOK, HL), BF),
            sds((TOK, D), F32),
            sds((8, D), F32),
            sds((4, 1, D), F32),
        ),
        in_specs=[
            whole((TOK, D)),
            pl.BlockSpec((TOK, D), lambda j: (0, j)),
            whole((TOK, D)),
            whole((4, TOK, HL)),
            whole((8, D)),
            whole((4, HL, D)),
            pl.BlockSpec((D, D), lambda j: (0, j)),
            pl.BlockSpec((D, D), lambda j: (j, 0)),
        ],
        out_specs=(
            pl.BlockSpec((D, D), lambda j: (j, 0)),
            pl.BlockSpec((D, D), lambda j: (0, j)),
            whole((4, HL, D)),
            whole((4, TOK, HL)),
            whole((TOK, D)),
            whole((8, D)),
            pl.BlockSpec((1, 1, D), lambda j: (j, 0, 0)),
        ),
        scratch_shapes=[pltpu.VMEM((TOK, D), BF), pltpu.VMEM((TOK, D), F32)],
        compiler_params=BIG,
    )(g, raised, middle, mixed, vec, wo, wu, wd)


def tile(rows):
    pads = [(0, 0)] * (rows.ndim - 2) + [(0, 8 - rows.shape[-2]), (0, 128 - rows.shape[-1])]
    return jnp.pad(rows, pads)


def open_weights(raw):
    qkv, out, up, down, small = raw
    small = small.reshape(64, 2, 8, 128)
    vec = small[:, 0, :, :12].transpose(1, 0, 2).reshape(8, D)
    ub = small[:, 1, 0, :48].reshape(4, 1, D)
    return (
        qkv.reshape(4, D, 576),
        out.reshape(4, HL, D),
        up.reshape(D, FF),
        down.reshape(FF, D),
        vec,
        ub,
    )


def forward(live, flag, x, weights, previous, base_id):
    qkv, wo, wu, wd, vec, ub = weights
    projected = project(flag, x, vec, qkv)
    kept = attend(live, projected.reshape(4, 4, ROWS, 576), previous, base_id)
    mixed = kept[2].reshape(4, TOK, HL)
    result, middle, raised = mlp(flag, x, mixed, vec, ub, wo, wu, wd)
    return result, (mixed, middle, raised), kept


def backward(live, g, x, weights, saved, kept, base_id):
    qkv, wo, wu, wd, vec, ub = weights
    mixed, middle, raised = saved
    g_down, g_up, g_out, g_mixed, g_middle, sums_two, g_ub = mlp_back(
        g, raised, middle, mixed, vec, wo, wu, wd
    )
    g_out = g_out.reshape(4, 4, 48, D)
    g_up = g_up.reshape(4, 4, 48, FF)
    g_down = g_down.reshape(4, 4, 4, 48, D)
    g_qkv, out_got, up_got, down_got, g_x, sums = attend_back(
        live, g_mixed.reshape(4, 4, ROWS, HL), kept[0], kept[1], g_out, g_up, g_down, x, g_middle, qkv, vec, sums_two, base_id
    )
    small = jnp.stack(
        [tile(sums.reshape(8, 64, 12).transpose(1, 0, 2)), tile(g_ub.reshape(64, 1, 48))], axis=1
    )
    grads = (
        g_qkv.reshape(4, 4, 4, 48, 576),
        g_out,
        g_up,
        g_down,
        small.reshape(4, 4, 4, 2, 8, 128),
        out_got,
        up_got,
        down_got,
    )
    return g_x, grads


def per_device(ends, w_qkv, w_out, w_up, w_down, norm_gains, biases, up_bias):
    section = lax.axis_index("section")
    own = ends.reshape(TOK, D)
    qkv = w_qkv[0].reshape(12, 3, 4, HL).transpose(2, 0, 1, 3).reshape(4, 12, 576)
    small = jnp.stack([tile(jnp.concatenate([norm_gains[0], biases[0]])), tile(up_bias)]).astype(F32)
    weights = open_weights(gather(qkv, w_out[0], w_up[0], w_down[0], small))
    flag = (section == 0).astype(jnp.int32).reshape(1)
    result, _, kept = forward(0, flag, own, weights, None, 3)
    arriving = lax.ppermute(result, "section", [(0, 1)])
    x = jnp.where(section == 0, own, arriving)
    result, saved, kept = forward(1, jnp.ones((1,), jnp.int32), x, weights, kept, 4)

    g_x, grads = backward(1, own, x, weights, saved, kept, 5)
    arriving = lax.ppermute(g_x, "section", [(1, 0)])
    grads, arriving = lax.optimization_barrier((grads, arriving))
    total_one = reduce_grads(1, *grads, 7)
    total_one, arriving = lax.optimization_barrier((total_one, arriving))
    g = jnp.where(section == 1, own, arriving)
    g_x, grads = backward(0, g, x, weights, saved, kept, 6)
    total_zero = reduce_grads(0, *grads, 8)
    q, o, u, d, s = (
        jnp.where(section == 0, zero, one) for zero, one in zip(total_zero, total_one)
    )
    boundary = jnp.where(section == 0, g_x, result)
    return (
        boundary.reshape(1, 1, GROUPS, ROWS, D),
        q[None],
        o[None],
        u[None],
        d[None],
        s[0:1, 0:2, :12],
        s[0:1, 2:8, :12],
        s[1:2, 0, :48],
    )


def solution(mesh):
    rows = P("section", ("seq", "shard"), None)
    columns = P("section", None, ("seq", "shard"))
    ends = P("section", "shard", None, "seq", None)
    hidden = P("section", ("seq", "shard"))
    placed = (ends, rows, rows, rows, rows, columns, columns, hidden)
    return jax.shard_map(per_device, mesh=mesh, in_specs=placed, out_specs=placed, check_vma=False)
```

```python
import functools

import jax
import jax.numpy as jnp
from jax import lax
from jax.experimental import pallas as pl
from jax.experimental.pallas import tpu as pltpu
from jax.sharding import PartitionSpec as P

HEAD = 64
FF = 3072
D = 768
GROUPS = 4
ROWS = 64
TOK = GROUPS * ROWS
SEQ_LEN = 1024
HL = 192
EPSILON = 1e-05
MASKED = -1e30
BF = jnp.bfloat16
F32 = jnp.float32
MESH = pl.DeviceIdType.MESH
HBM = pltpu.HBM


def sds(shape, dtype):
    return jax.ShapeDtypeStruct(shape, dtype)


def coords():
    shard = lax.axis_index("shard")
    return {"x": shard // 4, "y": lax.rem(shard, 4), "z": lax.axis_index("seq")}


def peer(c, axis, by):
    moved = dict(c)
    moved[axis] = lax.rem(c[axis] + by, 4)
    return {"section": lax.axis_index("section"), "seq": moved["z"], "shard": moved["x"] * 4 + moved["y"]}


def partner():
    return {
        "section": 1 - lax.axis_index("section"),
        "seq": lax.axis_index("seq"),
        "shard": lax.axis_index("shard"),
    }


def meet(c, axes, steps, with_partner=False):
    barrier = pltpu.get_barrier_semaphore()
    if with_partner:
        pl.semaphore_signal(barrier, inc=1, device_id=partner(), device_id_type=MESH)
    for axis in axes:
        for by in steps:
            pl.semaphore_signal(barrier, inc=1, device_id=peer(c, axis, by), device_id_type=MESH)
    pl.semaphore_wait(barrier, len(axes) * len(steps) + int(with_partner))


class Copies:
    def __init__(self, send, recv):
        self.send, self.recv, self.used, self.sent = send, recv, 0, []

    def remote(self, src, dst, to):
        copy = pltpu.make_async_remote_copy(
            src_ref=src,
            dst_ref=dst,
            send_sem=self.send.at[self.used],
            recv_sem=self.recv.at[self.used],
            device_id=to,
            device_id_type=MESH,
        )
        self.used += 1
        copy.start()
        self.sent.append(copy)
        return copy

    def local(self, src, dst):
        copy = pltpu.make_async_copy(src, dst, self.send.at[self.used])
        self.used += 1
        copy.start()
        return copy

    def drain(self):
        for copy in self.sent:
            copy.wait_send()


class Gather:
    def __init__(self, copies, c, axis, own, dst, half):
        self.copies, self.c, self.axis, self.own, self.dst, self.half = copies, c, axis, own, dst, half

    def first(self):
        a = self.c[self.axis]
        self.right, self.left = peer(self.c, self.axis, 1), peer(self.c, self.axis, 3)
        self.go_right = self.copies.remote(self.own, self.dst(a), self.right)
        self.go_left = self.copies.remote(self.own, self.dst(a), self.left)

    def second(self):
        a = self.c[self.axis]
        before, after = lax.rem(a + 3, 4), lax.rem(a + 1, 4)
        self.go_right.wait_recv()
        self.on_right = self.copies.remote(self.half(before, 0), self.half(before, 0), self.right)
        self.go_left.wait_recv()
        self.on_left = self.copies.remote(self.half(after, 1), self.half(after, 1), self.left)

    def third(self):
        self.on_right.wait_recv()
        self.on_left.wait_recv()


def run_gathers(gathers):
    for g in gathers:
        g.first()
    for g in gathers:
        g.second()


def gather_kernel(q_in, o_in, u_in, d_in, s_in, q, o, u, d, s, *scratch):
    q_y, o_y, u_y, d_x, s_x, q_b, o_b, u_b, tmp, send, recv, turn = scratch
    c = coords()
    x, y, z = c["x"], c["y"], c["z"]
    copies = Copies(send, recv)
    lanes = lambda ref, i, h, n: ref.at[i, :, pl.ds(n * h, n)]
    zero = [
        Gather(copies, c, "y", u_in, lambda i: u_y.at[i], lambda i, h: lanes(u_y, i, h, 1536)),
        Gather(copies, c, "y", q_in, lambda i: q_y.at[i], lambda i, h: q_y.at[i, pl.ds(2 * h, 2)]),
        Gather(copies, c, "y", o_in, lambda i: o_y.at[i], lambda i, h: lanes(o_y, i, h, 384)),
        Gather(copies, c, "x", d_in, lambda i: d_x.at[i], lambda i, h: lanes(d_x, i, h, 384)),
        Gather(copies, c, "x", s_in, lambda i: s_x.at[i], lambda i, h: s_x.at[i, h]),
    ]
    u_y[y] = u_in[...]
    q_y[y] = q_in[...]
    o_y[y] = o_in[...]
    d_x[x] = d_in[...]
    s_x[x] = s_in[...]
    meet(c, ("x", "y", "z"), (1, 3), True)
    run_gathers(zero)
    zero[0].third()
    for k in range(4):
        for i in range(4):
            tmp[12 * i : 12 * i + 12, :] = u_y[i, :, D * k : D * k + D].astype(F32)
        u_b[:, D * k : D * k + D] = tmp[...].astype(BF)
    zero[1].third()
    for p in range(4):
        for i in range(4):
            tmp[12 * i : 12 * i + 12, 0:576] = q_y[i, p].astype(F32)
        q_b[p] = tmp[:, 0:576].astype(BF)
    zero[2].third()
    for i in range(4):
        tmp[12 * i : 12 * i + 12, :] = o_y[i].astype(F32)
    o_b[...] = tmp[...].astype(BF)
    zero[3].third()
    zero[4].third()

    @pl.when(lax.axis_index("section") == 1)
    def _():
        pl.semaphore_wait(turn, 1)

    one = [
        Gather(copies, c, "z", q_b, lambda i: q.at[:, i, x], lambda i, h: q.at[pl.ds(2 * h, 2), i, x]),
        Gather(copies, c, "z", o_b, lambda i: o.at[i, x], lambda i, h: o.at[i, x, :, pl.ds(384 * h, 384)]),
        Gather(copies, c, "x", u_b, lambda i: u.at[z, i], lambda i, h: u.at[z, i, :, pl.ds(1536 * h, 1536)]),
        Gather(copies, c, "z", d_x, lambda i: d.at[i, :, y], lambda i, h: d.at[i, pl.ds(2 * h, 2), y]),
        Gather(copies, c, "z", s_x, lambda i: s.at[i, :, y], lambda i, h: s.at[i, pl.ds(2 * h, 2), y]),
    ]
    own = [
        copies.local(q_b, q.at[:, z, x]),
        copies.local(o_b, o.at[z, x]),
        copies.local(u_b, u.at[z, x]),
        copies.local(d_x, d.at[z, :, y]),
        copies.local(s_x, s.at[z, :, y]),
    ]
    run_gathers(one)
    two = [
        Gather(copies, c, "x", q.at[:, :, x], lambda i: q.at[:, :, i], lambda i, h: q.at[pl.ds(2 * h, 2), :, i]),
        Gather(copies, c, "x", o.at[:, x], lambda i: o.at[:, i], lambda i, h: o.at[pl.ds(2 * h, 2), i]),
        Gather(copies, c, "z", u.at[z], lambda i: u.at[i], lambda i, h: u.at[i, pl.ds(2 * h, 2)]),
        Gather(copies, c, "y", d.at[:, :, y], lambda i: d.at[:, :, i], lambda i, h: d.at[pl.ds(2 * h, 2), :, i]),
        Gather(copies, c, "y", s.at[:, :, y], lambda i: s.at[:, :, i], lambda i, h: s.at[pl.ds(2 * h, 2), :, i]),
    ]
    for k in range(5):
        one[k].third()
        own[k].wait()
        two[k].first()
    for g in two:
        g.second()

    @pl.when(lax.axis_index("section") == 0)
    def _():
        pl.semaphore_signal(turn, inc=1, device_id=partner(), device_id_type=MESH)

    for g in two:
        g.third()
    copies.drain()


def gather(qkv, out, up, down, small):
    vmem = pltpu.VMEM
    count = 15 * 4 + 5
    return pl.pallas_call(
        gather_kernel,
        out_shape=(
            sds((4, 4, 4, 48, 576), BF),
            sds((4, 4, 48, D), BF),
            sds((4, 4, 48, FF), BF),
            sds((4, 4, 4, 48, D), BF),
            sds((4, 4, 4, 2, 8, 128), F32),
        ),
        in_specs=[pl.BlockSpec(memory_space=vmem)] * 5,
        out_specs=tuple([pl.BlockSpec(memory_space=HBM)] * 5),
        scratch_shapes=[
            vmem((4, 4, 12, 576), BF),
            vmem((4, 12, D), BF),
            vmem((4, 12, FF), BF),
            vmem((4, 48, D), BF),
            vmem((4, 2, 8, 128), F32),
            vmem((4, 48, 576), BF),
            vmem((48, D), BF),
            vmem((48, FF), BF),
            vmem((48, D), F32),
            pltpu.SemaphoreType.DMA((count,)),
            pltpu.SemaphoreType.DMA((count,)),
            pltpu.SemaphoreType.REGULAR,
        ],
        compiler_params=pltpu.CompilerParams(
            collective_id=1, has_side_effects=True, vmem_limit_bytes=60 * 1024 * 1024
        ),
    )(qkv, out, up, down, small)


def spread(copies, c, axis, source, target):
    moves = []
    for by in (2, 1, 3):
        there = lax.rem(c[axis] + by, 4)
        moves.append(copies.remote(source(there), target.at[by], peer(c, axis, by)))
    return moves


def arrived(moves):
    for move in moves:
        move.wait_recv()


def add(ref, at):
    total = ref[(0,) + at].astype(F32)
    for k in range(1, 4):
        total += ref[(k,) + at].astype(F32)
    return total


def more(mine, ref, at):
    total = mine.astype(F32)
    for k in range(1, 4):
        total += ref[(k,) + at].astype(F32)
    return total


def reduce_kernel(live, q_in, o_in, u_in, d_in, s_in, o_got, u_got, d_got, q, o, u, d, s, *scratch):
    qa1, qb1, o1, u1, d1, s1, qa2, qb2, o2, u2, d2, s2, tmp, qs, os, us, q3, o3, u3, d3, s3, send, recv = scratch

    def act():
        c = coords()
        x, y, z = c["x"], c["y"], c["z"]
        copies = Copies(send, recv)
        own_d = [copies.local(d_in.at[:, :, y], d1.at[0]), copies.local(d_got.at[pl.ds(1, 3)], d1.at[pl.ds(1, 3)])]
        own_u = [copies.local(u_in.at[:, x], u1.at[0]), copies.local(u_got.at[pl.ds(1, 3)], u1.at[pl.ds(1, 3)])]
        own_qa = copies.local(q_in.at[pl.ds(0, 2), :, x], qa1.at[0])
        own_qb = copies.local(q_in.at[pl.ds(2, 2), z], qb1.at[0])
        own_o = [copies.local(o_in.at[z], o1.at[0]), copies.local(o_got.at[pl.ds(1, 3)], o1.at[pl.ds(1, 3)])]
        own_s = copies.local(s_in.at[:, :, y], s1.at[0])
        meet(c, ("x", "y", "z"), (1, 2, 3))
        one_qa = spread(copies, c, "x", lambda i: q_in.at[pl.ds(0, 2), :, i], qa1)
        one_qb = spread(copies, c, "z", lambda i: q_in.at[pl.ds(2, 2), i], qb1)
        one_s = spread(copies, c, "y", lambda i: s_in.at[:, :, i], s1)

        def add_all(ref, rows, kind):
            @pl.loop(0, rows * 4)
            def _(i):
                at = (i // 4, lax.rem(i, 4))
                ref[(0,) + at] = add(ref, at).astype(kind)

        for copy in own_d:
            copy.wait()
        add_all(d1, 4, BF)
        two_d = spread(copies, c, "x", lambda i: d1.at[0, :, i], d2)
        for copy in own_u:
            copy.wait()

        @pl.loop(0, 4)
        def _(i):
            for k in range(4):
                at = (i, slice(None), pl.ds(D * k, D))
                u1[(0,) + at] = add(u1, at).astype(BF)

        two_u = spread(copies, c, "z", lambda i: u1.at[0, i], u2)
        for copy in own_o:
            copy.wait()

        @pl.loop(0, 4)
        def _(i):
            o1[0, i] = add(o1, (i,)).astype(BF)

        two_o = spread(copies, c, "x", lambda i: o1.at[0, i], o2)
        arrived(one_qa)
        own_qa.wait()
        add_all(qa1, 2, BF)
        two_qa = spread(copies, c, "z", lambda i: qa1.at[0, :, i], qa2)
        arrived(one_qb)
        own_qb.wait()
        add_all(qb1, 2, BF)
        two_qb = spread(copies, c, "x", lambda i: qb1.at[0, :, i], qb2)
        arrived(one_s)
        own_s.wait()
        add_all(s1, 4, F32)
        two_s = spread(copies, c, "z", lambda i: s1.at[0, i], s2)
        arrived(two_d)

        @pl.loop(0, 4)
        def _(i):
            d2[0, i] = more(d1[0, i, x], d2, (i,)).astype(BF)

        three_d = spread(copies, c, "z", lambda i: d2.at[0, i], d3)
        arrived(two_u)
        for k in range(4):
            at = (slice(None), pl.ds(D * k, D))
            tmp[...] = more(u1[(0, z) + at], u2, at)
            for i in range(4):
                us[i, :, D * k : D * k + D] = tmp[12 * i : 12 * i + 12, :].astype(BF)
        three_u = spread(copies, c, "y", lambda i: us.at[i], u3)
        arrived(two_qa)
        arrived(two_qb)
        for p in range(4):
            if p < 2:
                tmp[:, 0:576] = more(qa1[0, p, z], qa2, (p,))
            else:
                tmp[:, 0:576] = more(qb1[0, p - 2, x], qb2, (p - 2,))
            for i in range(4):
                qs[i, p] = tmp[12 * i : 12 * i + 12, 0:576].astype(BF)
        three_q = spread(copies, c, "y", lambda i: qs.at[i], q3)
        arrived(two_o)
        tmp[...] = more(o1[0, x], o2, ())
        for i in range(4):
            os[i] = tmp[12 * i : 12 * i + 12, :].astype(BF)
        three_o = spread(copies, c, "y", lambda i: os.at[i], o3)
        arrived(two_s)

        @pl.loop(0, 4)
        def _(i):
            s2[0, i] = more(s1[0, z, i], s2, (i,))

        three_s = spread(copies, c, "x", lambda i: s2.at[0, i], s3)
        arrived(three_d)
        d[...] = more(d2[0, z], d3, ())
        arrived(three_u)
        u[...] = more(us[y], u3, ())
        arrived(three_q)
        for p in range(4):
            total = more(qs[y, p], q3, (p,))
            for kind in range(3):
                at = D * kind + HL * p
                q[:, at : at + HL] = total[:, HL * kind : HL * kind + HL]
        arrived(three_o)
        o[...] = more(os[y], o3, ())
        arrived(three_s)
        s[...] = more(s2[0, x], s3, ())
        copies.drain()

    pl.when(lax.axis_index("section") == live)(act)


def reduce_grads(live, qkv, out, up, down, small, out_got, up_got, down_got, collective_id):
    vmem = pltpu.VMEM
    count = 9 + 9 + 18 + 15
    return pl.pallas_call(
        functools.partial(reduce_kernel, live),
        out_shape=(
            sds((12, 3 * D), F32),
            sds((12, D), F32),
            sds((12, FF), F32),
            sds((48, D), F32),
            sds((2, 8, 128), F32),
        ),
        in_specs=[pl.BlockSpec(memory_space=HBM)] * 8,
        out_specs=tuple([pl.BlockSpec(memory_space=vmem)] * 5),
        scratch_shapes=[
            vmem((4, 2, 4, 48, 576), BF),
            vmem((4, 2, 4, 48, 576), BF),
            vmem((4, 4, 48, D), BF),
            vmem((4, 4, 48, FF), BF),
            vmem((4, 4, 4, 48, D), BF),
            vmem((4, 4, 4, 2, 8, 128), F32),
            vmem((4, 2, 48, 576), BF),
            vmem((4, 2, 48, 576), BF),
            vmem((4, 48, D), BF),
            vmem((4, 48, FF), BF),
            vmem((4, 4, 48, D), BF),
            vmem((4, 4, 2, 8, 128), F32),
            vmem((48, D), F32),
            vmem((4, 4, 12, 576), BF),
            vmem((4, 12, D), BF),
            vmem((4, 12, FF), BF),
            vmem((4, 4, 12, 576), BF),
            vmem((4, 12, D), BF),
            vmem((4, 12, FF), BF),
            vmem((4, 48, D), BF),
            vmem((4, 2, 8, 128), F32),
            pltpu.SemaphoreType.DMA((count,)),
            pltpu.SemaphoreType.DMA((count,)),
        ],
        compiler_params=pltpu.CompilerParams(
            collective_id=collective_id, has_side_effects=True, vmem_limit_bytes=60 * 1024 * 1024
        ),
    )(qkv, out, up, down, small, out_got, up_got, down_got)


BIG = pltpu.CompilerParams(vmem_limit_bytes=56 * 1024 * 1024)


def dot(a, b):
    return jnp.dot(a, b, preferred_element_type=F32)


def dot_nt(a, b):
    return lax.dot_general(a, b, (((1,), (1,)), ((), ())), preferred_element_type=F32)


def dot_tn(a, b):
    return lax.dot_general(a, b, (((0,), (0,)), ((), ())), preferred_element_type=F32)


def normalize(values):
    centered = values - jnp.mean(values, axis=-1, keepdims=True)
    spread = jnp.mean(centered * centered, axis=-1, keepdims=True)
    inverse = lax.rsqrt(spread + EPSILON)
    return centered * inverse, inverse


def norm_back(e, n, inverse):
    return inverse * (
        e - jnp.mean(e, axis=-1, keepdims=True) - n * jnp.mean(e * n, axis=-1, keepdims=True)
    )


C_ONE = 0.7978845608
C_TWO = 0.7978845608 * 0.044715


def gelu_half(u):
    cube = C_TWO * (u * u)
    return 0.5 + 0.5 * jnp.tanh((C_ONE + cube) * u), cube


def whole(shape):
    zeros = (0,) * len(shape)
    return pl.BlockSpec(shape, lambda *unused: zeros)


def flagged(grid, in_specs, out_specs, scratch):
    return pltpu.PrefetchScalarGridSpec(
        num_scalar_prefetch=1, grid=grid, in_specs=in_specs, out_specs=out_specs, scratch_shapes=scratch
    )


def project_kernel(flag, x_ref, vec_ref, w_ref, out_ref, n_ref, bias_ref):
    step = pl.program_id(0)

    @pl.when((flag[0] == 1) & (step == 0))
    def _():
        n, _ = normalize(x_ref[...].astype(F32))
        n_ref[...] = (n * vec_ref[0:1, :] + vec_ref[2:3, :]).astype(BF)
        bias_ref[...] = jnp.zeros_like(bias_ref)
        for p in range(4):
            bias_ref[p, :, 0:HL] = vec_ref[4:5, HL * p : HL * p + HL]
            bias_ref[p, :, 2 * HL :] = vec_ref[5:6, HL * p : HL * p + HL]

    @pl.when(flag[0] == 1)
    def _():
        out_ref[0] = (dot(n_ref[...], w_ref[0]) + bias_ref[step]).astype(BF)


def project(flag, x, vec, w):
    return pl.pallas_call(
        project_kernel,
        grid_spec=flagged(
            (4,),
            [
                whole((TOK, D)),
                whole((8, D)),
                pl.BlockSpec((1, D, 576), lambda j, f: (j * f[0], 0, 0)),
            ],
            pl.BlockSpec((1, TOK, 576), lambda j, f: (j * f[0], 0, 0)),
            [pltpu.VMEM((TOK, D), BF), pltpu.VMEM((4, 1, 576), F32)],
        ),
        out_shape=sds((4, TOK, 576), BF),
        compiler_params=BIG,
    )(flag, x, vec, w)


BLOCK = 256


def masked(scores, block):
    rows = block * BLOCK + lax.broadcasted_iota(jnp.int32, scores.shape, 0)
    cols = lax.broadcasted_iota(jnp.int32, scores.shape, 1)
    return jnp.where(cols <= rows, scores, MASKED)


def attend_kernel(live, with_previous, p_in, *refs):
    if with_previous:
        refs = refs[3:]
    h_out, lse_out, m_out, h_ref, m_ref, lse_ref, send, recv = refs

    def act():
        c = coords()
        z = c["z"]
        copies = Copies(send, recv)
        own = copies.local(p_in.at[z], h_ref.at[:, z])
        meet(c, ("z",), (1, 2, 3))
        coming, kept = [], []
        for g in range(GROUPS):
            for by in (2, 1, 3):
                to = peer(c, "z", by)
                coming.append(copies.remote(p_in.at[to["seq"], g], h_ref.at[g, z], to))
        own.wait()
        leaving = []
        for g in range(GROUPS):
            arrived(coming[3 * g : 3 * g + 3])
            kept.append(copies.local(h_ref.at[g], h_out.at[g]))
            keys = (g + 1) * BLOCK
            for head in range(3):
                q_at, k_at, v_at = HEAD * head, HL + HEAD * head, 2 * HL + HEAD * head
                q = h_ref[g, :, :, q_at : q_at + HEAD].reshape(BLOCK, HEAD) * jnp.asarray(0.125, BF)
                k = h_ref[0 : g + 1, :, :, k_at : k_at + HEAD].reshape(keys, HEAD)
                v = h_ref[0 : g + 1, :, :, v_at : v_at + HEAD].reshape(keys, HEAD)
                scores = masked(dot_nt(q, k), g)
                top = jnp.max(scores, axis=-1, keepdims=True)
                e = jnp.exp(scores - top)
                total = jnp.sum(e, axis=-1, keepdims=True)
                mixed = (dot(e.astype(BF), v) / total).astype(BF)
                m_ref[g, :, :, q_at : q_at + HEAD] = mixed.reshape(4, ROWS, HEAD)
                lse_ref[g, :, head : head + 1] = top + jnp.log(total)
            for by in (2, 1, 3):
                to = peer(c, "z", by)
                leaving.append(copies.remote(m_ref.at[g, to["seq"]], m_out.at[z, g], to))
            kept.append(copies.local(m_ref.at[g, z], m_out.at[z, g]))
        kept.append(copies.local(lse_ref, lse_out))
        arrived(leaving)
        for copy in kept:
            copy.wait()
        copies.drain()

    pl.when(lax.axis_index("section") == live)(act)


def attend(live, projected, previous, collective_id):
    ins, aliases = (projected,), {}
    if previous is not None:
        ins, aliases = ins + tuple(previous), {1: 0, 2: 1, 3: 2}
    count = 1 + 12 + 4 + 12 + 4 + 1
    return pl.pallas_call(
        functools.partial(attend_kernel, live, previous is not None),
        out_shape=(
            sds((4, 4, ROWS, 576), BF),
            sds((GROUPS, BLOCK, 128), F32),
            sds((4, 4, ROWS, HL), BF),
        ),
        in_specs=[pl.BlockSpec(memory_space=HBM)] * len(ins),
        out_specs=tuple([pl.BlockSpec(memory_space=HBM)] * 3),
        scratch_shapes=[
            pltpu.VMEM((4, 4, ROWS, 576), BF),
            pltpu.VMEM((4, 4, ROWS, HL), BF),
            pltpu.VMEM((GROUPS, BLOCK, 128), F32),
            pltpu.SemaphoreType.DMA((count,)),
            pltpu.SemaphoreType.DMA((count,)),
        ],
        input_output_aliases=aliases,
        compiler_params=pltpu.CompilerParams(
            collective_id=collective_id, has_side_effects=True, vmem_limit_bytes=60 * 1024 * 1024
        ),
    )(*ins)


def attend_back_kernel(
    live, g_in, h_hbm, lse_hbm, o_in, u_in, d_in, x_hbm, mid_hbm, w_hbm, vec_ref, sums_two_ref,
    gw_out, o_out, u_out, d_out, gx_ref, sums_ref,
    h_ref, lse_ref, gh_ref, gs_ref, dk_ref, dv_ref, p_ref, x_ref, mid_ref, w_ref, gw_ref, send, recv,
):
    def act():
        c = coords()
        z = c["z"]
        copies = Copies(send, recv)
        own = [
            copies.local(g_in.at[z], gh_ref.at[:, z]),
            copies.local(h_hbm, h_ref),
            copies.local(lse_hbm, lse_ref),
        ]
        meet(c, ("x", "y", "z"), (1, 2, 3))
        coming, leaving, kept = {}, [], []
        for g in reversed(range(GROUPS)):
            coming[g] = []
            for by in (2, 1, 3):
                to = peer(c, "z", by)
                coming[g].append(copies.remote(g_in.at[to["seq"], g], gh_ref.at[g, z], to))
        weights = spread(copies, c, "y", lambda i: d_in.at[:, :, i], d_out)
        weights += spread(copies, c, "x", lambda i: u_in.at[:, i], u_out)
        weights += spread(copies, c, "z", lambda i: o_in.at[i], o_out)
        later = [copies.local(x_hbm, x_ref), copies.local(mid_hbm, mid_ref), copies.local(w_hbm, w_ref)]
        for copy in own:
            copy.wait()
        for g in reversed(range(GROUPS)):
            arrived(coming[g])
            keys = (g + 1) * BLOCK
            for head in range(3):
                q_at, k_at, v_at = HEAD * head, HL + HEAD * head, 2 * HL + HEAD * head
                q = h_ref[g, :, :, q_at : q_at + HEAD].reshape(BLOCK, HEAD) * jnp.asarray(0.125, BF)
                k = h_ref[0 : g + 1, :, :, k_at : k_at + HEAD].reshape(keys, HEAD)
                v = h_ref[0 : g + 1, :, :, v_at : v_at + HEAD].reshape(keys, HEAD)
                grad = gh_ref[g, :, :, q_at : q_at + HEAD].reshape(BLOCK, HEAD)
                scores = masked(dot_nt(q, k), g)
                p = jnp.exp(scores - lse_ref[g, :, head : head + 1])
                dp = dot_nt(grad, v)
                centre = jnp.sum(p * dp, axis=-1, keepdims=True)
                ds = (p * (dp - centre)).astype(BF)
                dq = (dot(ds, k) * 0.125).astype(BF)
                gs_ref[g, :, :, q_at : q_at + HEAD] = dq.reshape(4, ROWS, HEAD)
                dk = dot_tn(ds, q)
                dv = dot_tn(p.astype(BF), grad)
                if g < GROUPS - 1:
                    dk += dk_ref[head, 0:keys, :]
                    dv += dv_ref[head, 0:keys, :]
                if g > 0:
                    dk_ref[head, 0 : keys - BLOCK, :] = dk[: keys - BLOCK]
                    dv_ref[head, 0 : keys - BLOCK, :] = dv[: keys - BLOCK]
                gs_ref[g, :, :, k_at : k_at + HEAD] = dk[keys - BLOCK :].astype(BF).reshape(4, ROWS, HEAD)
                gs_ref[g, :, :, v_at : v_at + HEAD] = dv[keys - BLOCK :].astype(BF).reshape(4, ROWS, HEAD)
            for by in (2, 1, 3):
                to = peer(c, "z", by)
                leaving.append(copies.remote(gs_ref.at[g, to["seq"]], p_ref.at[z, g], to))
            kept.append(copies.local(gs_ref.at[g, z], p_ref.at[z, g]))
        for copy in later:
            copy.wait()
        n, inverse = normalize(x_ref[...].astype(F32))
        normed = jnp.transpose(n * vec_ref[0:1, :] + vec_ref[2:3, :]).astype(BF)
        arrived(leaving)
        for copy in kept:
            copy.wait()
        back = jnp.zeros((TOK, D), F32)
        written = []
        for p in range(4):
            gp = p_ref[p].reshape(TOK, 576)
            gw_ref[p] = dot(normed, gp).astype(BF)
            written.append(copies.local(gw_ref.at[p], gw_out.at[p]))
            columns = jnp.sum(gp.astype(F32), axis=0, keepdims=True)
            sums_ref[4:5, HL * p : HL * p + HL] = columns[:, 0:HL]
            sums_ref[5:6, HL * p : HL * p + HL] = columns[:, 2 * HL :]
            back += dot_nt(gp, w_ref[p])
        gx_ref[...] = (mid_ref[...] + norm_back(back * vec_ref[0:1, :], n, inverse)).astype(BF)
        sums_ref[0:1, :] = jnp.sum(back * n, axis=0, keepdims=True)
        sums_ref[1:2, :] = sums_two_ref[0:1, :]
        sums_ref[2:3, :] = jnp.sum(back, axis=0, keepdims=True)
        sums_ref[3:4, :] = sums_two_ref[1:2, :]
        sums_ref[6:8, :] = sums_two_ref[2:4, :]
        for copy in written:
            copy.wait()
        arrived(weights)
        copies.drain()

    pl.when(lax.axis_index("section") == live)(act)


def attend_back(live, grads, heads, lse, out, up, down, x, middle_grad, w, vec, sums_two, collective_id):
    vmem = pltpu.VMEM
    count = 3 + 12 + 9 + 3 + 12 + 4 + 4
    return pl.pallas_call(
        functools.partial(attend_back_kernel, live),
        out_shape=(
            sds((4, D, 576), BF),
            sds((4, 4, 48, D), BF),
            sds((4, 4, 48, FF), BF),
            sds((4, 4, 4, 48, D), BF),
            sds((TOK, D), BF),
            sds((8, D), F32),
        ),
        in_specs=[pl.BlockSpec(memory_space=HBM)] * 9 + [pl.BlockSpec(memory_space=vmem)] * 2,
        out_specs=tuple([pl.BlockSpec(memory_space=HBM)] * 4 + [pl.BlockSpec(memory_space=vmem)] * 2),
        scratch_shapes=[
            vmem((4, 4, ROWS, 576), BF),
            vmem((GROUPS, BLOCK, 128), F32),
            vmem((4, 4, ROWS, HL), BF),
            vmem((4, 4, ROWS, 576), BF),
            vmem((3, SEQ_LEN, HEAD), F32),
            vmem((3, SEQ_LEN, HEAD), F32),
            vmem((4, 4, ROWS, 576), BF),
            vmem((TOK, D), BF),
            vmem((TOK, D), F32),
            vmem((4, D, 576), BF),
            vmem((4, D, 576), BF),
            pltpu.SemaphoreType.DMA((count,)),
            pltpu.SemaphoreType.DMA((count,)),
        ],
        compiler_params=pltpu.CompilerParams(
            collective_id=collective_id, has_side_effects=True, vmem_limit_bytes=60 * 1024 * 1024
        ),
    )(grads, heads, lse, out, up, down, x, middle_grad, w, vec, sums_two)


def mlp_kernel(
    flag, x_ref, m_ref, vec_ref, ub_ref, wo_ref, wu_ref, wd_ref, res_ref, mid_ref, raised_ref, n_ref, acc_ref
):
    step = pl.program_id(0)

    @pl.when((flag[0] == 1) & (step == 0))
    def _():
        branch = dot(m_ref[0], wo_ref[0])
        for p in range(1, 4):
            branch += dot(m_ref[p], wo_ref[p])
        middle = x_ref[...].astype(F32) + (branch + vec_ref[6:7, :])
        mid_ref[...] = middle
        n, _ = normalize(middle)
        n_ref[...] = (n * vec_ref[1:2, :] + vec_ref[3:4, :]).astype(BF)
        acc_ref[...] = middle + vec_ref[7:8, :]

    @pl.when(flag[0] == 1)
    def _():
        raised = dot(n_ref[...], wu_ref[...]) + ub_ref[0]
        raised_ref[...] = raised
        active = (raised * gelu_half(raised)[0]).astype(BF)
        acc_ref[...] += dot(active, wd_ref[...])

    @pl.when((flag[0] == 1) & (step == 3))
    def _():
        res_ref[...] = acc_ref[...].astype(BF)


def mlp(flag, x, mixed, vec, ub, wo, wu, wd):
    return pl.pallas_call(
        mlp_kernel,
        grid_spec=flagged(
            (4,),
            [
                whole((TOK, D)),
                whole((4, TOK, HL)),
                whole((8, D)),
                pl.BlockSpec((1, 1, D), lambda j, f: (j * f[0], 0, 0)),
                whole((4, HL, D)),
                pl.BlockSpec((D, D), lambda j, f: (0, j * f[0])),
                pl.BlockSpec((D, D), lambda j, f: (j * f[0], 0)),
            ],
            (whole((TOK, D)), whole((TOK, D)), pl.BlockSpec((TOK, D), lambda j, f: (0, j * f[0]))),
            [pltpu.VMEM((TOK, D), BF), pltpu.VMEM((TOK, D), F32)],
        ),
        out_shape=(sds((TOK, D), BF), sds((TOK, D), F32), sds((TOK, FF), F32)),
        compiler_params=BIG,
    )(flag, x, mixed, vec, ub, wo, wu, wd)


def mlp_back_kernel(
    g_ref, raised_ref, mid_ref, m_ref, vec_ref, wo_ref, wu_ref, wd_ref,
    gd_ref, gu_ref, go_ref, gm_ref, gmid_ref, sums_ref, gub_ref, n_ref, acc_ref,
):
    step = pl.program_id(0)

    @pl.when(step == 0)
    def _():
        n, _ = normalize(mid_ref[...])
        n_ref[...] = jnp.transpose(n * vec_ref[1:2, :] + vec_ref[3:4, :]).astype(BF)
        acc_ref[...] = jnp.zeros_like(acc_ref)

    g = g_ref[...]
    u = raised_ref[...]
    h, cube = gelu_half(u)
    active = (u * h).astype(BF)
    gd_ref[...] = dot_tn(active, g).astype(BF)
    slope = h + (h * (1.0 - h)) * (u * (2.0 * C_ONE + 6.0 * cube))
    grad_raised = (dot_nt(g, wd_ref[...]) * slope).astype(BF)
    gub_ref[0] = jnp.sum(grad_raised.astype(F32), axis=0, keepdims=True)
    gu_ref[...] = dot(n_ref[...], grad_raised).astype(BF)
    acc_ref[...] += dot_nt(grad_raised, wu_ref[...])

    @pl.when(step == 3)
    def _():
        n, inverse = normalize(mid_ref[...])
        back = acc_ref[...]
        g32 = g.astype(F32)
        grad_middle = g32 + norm_back(back * vec_ref[1:2, :], n, inverse)
        gmid_ref[...] = grad_middle
        branch = grad_middle.astype(BF)
        sums_ref[...] = jnp.zeros_like(sums_ref)
        sums_ref[0:1, :] = jnp.sum(back * n, axis=0, keepdims=True)
        sums_ref[1:2, :] = jnp.sum(back, axis=0, keepdims=True)
        sums_ref[2:3, :] = jnp.sum(branch.astype(F32), axis=0, keepdims=True)
        sums_ref[3:4, :] = jnp.sum(g32, axis=0, keepdims=True)
        for p in range(4):
            go_ref[p] = dot_tn(m_ref[p], branch).astype(BF)
            gm_ref[p] = dot_nt(branch, wo_ref[p]).astype(BF)


def mlp_back(g, raised, middle, mixed, vec, wo, wu, wd):
    return pl.pallas_call(
        mlp_back_kernel,
        grid=(4,),
        out_shape=(
            sds((FF, D), BF),
            sds((D, FF), BF),
            sds((4, HL, D), BF),
            sds((4, TOK, HL), BF),
            sds((TOK, D), F32),
            sds((8, D), F32),
            sds((4, 1, D), F32),
        ),
        in_specs=[
            whole((TOK, D)),
            pl.BlockSpec((TOK, D), lambda j: (0, j)),
            whole((TOK, D)),
            whole((4, TOK, HL)),
            whole((8, D)),
            whole((4, HL, D)),
            pl.BlockSpec((D, D), lambda j: (0, j)),
            pl.BlockSpec((D, D), lambda j: (j, 0)),
        ],
        out_specs=(
            pl.BlockSpec((D, D), lambda j: (j, 0)),
            pl.BlockSpec((D, D), lambda j: (0, j)),
            whole((4, HL, D)),
            whole((4, TOK, HL)),
            whole((TOK, D)),
            whole((8, D)),
            pl.BlockSpec((1, 1, D), lambda j: (j, 0, 0)),
        ),
        scratch_shapes=[pltpu.VMEM((D, TOK), BF), pltpu.VMEM((TOK, D), F32)],
        compiler_params=BIG,
    )(g, raised, middle, mixed, vec, wo, wu, wd)


def tile(rows):
    pads = [(0, 0)] * (rows.ndim - 2) + [(0, 8 - rows.shape[-2]), (0, 128 - rows.shape[-1])]
    return jnp.pad(rows, pads)


def open_weights(raw):
    qkv, out, up, down, small = raw
    small = small.reshape(64, 2, 8, 128)
    vec = small[:, 0, :, :12].transpose(1, 0, 2).reshape(8, D)
    ub = small[:, 1, 0, :48].reshape(4, 1, D)
    return (
        qkv.reshape(4, D, 576),
        out.reshape(4, HL, D),
        up.reshape(D, FF),
        down.reshape(FF, D),
        vec,
        ub,
    )


def forward(live, flag, x, weights, previous, base_id):
    qkv, wo, wu, wd, vec, ub = weights
    projected = project(flag, x, vec, qkv)
    kept = attend(live, projected.reshape(4, 4, ROWS, 576), previous, base_id)
    mixed = kept[2].reshape(4, TOK, HL)
    result, middle, raised = mlp(flag, x, mixed, vec, ub, wo, wu, wd)
    return result, (mixed, middle, raised), kept


def backward(live, g, x, weights, saved, kept, base_id):
    qkv, wo, wu, wd, vec, ub = weights
    mixed, middle, raised = saved
    g_down, g_up, g_out, g_mixed, g_middle, sums_two, g_ub = mlp_back(
        g, raised, middle, mixed, vec, wo, wu, wd
    )
    g_out = g_out.reshape(4, 4, 48, D)
    g_up = g_up.reshape(4, 4, 48, FF)
    g_down = g_down.reshape(4, 4, 4, 48, D)
    g_qkv, out_got, up_got, down_got, g_x, sums = attend_back(
        live, g_mixed.reshape(4, 4, ROWS, HL), kept[0], kept[1], g_out, g_up, g_down, x, g_middle, qkv, vec, sums_two, base_id
    )
    small = jnp.stack(
        [tile(sums.reshape(8, 64, 12).transpose(1, 0, 2)), tile(g_ub.reshape(64, 1, 48))], axis=1
    )
    grads = (
        g_qkv.reshape(4, 4, 4, 48, 576),
        g_out,
        g_up,
        g_down,
        small.reshape(4, 4, 4, 2, 8, 128),
        out_got,
        up_got,
        down_got,
    )
    return g_x, grads


def per_device(ends, w_qkv, w_out, w_up, w_down, norm_gains, biases, up_bias):
    section = lax.axis_index("section")
    own = ends.reshape(TOK, D)
    qkv = w_qkv[0].reshape(12, 3, 4, HL).transpose(2, 0, 1, 3).reshape(4, 12, 576)
    small = jnp.stack([tile(jnp.concatenate([norm_gains[0], biases[0]])), tile(up_bias)]).astype(F32)
    weights = open_weights(gather(qkv, w_out[0], w_up[0], w_down[0], small))
    flag = (section == 0).astype(jnp.int32).reshape(1)
    result, _, kept = forward(0, flag, own, weights, None, 3)
    arriving = lax.ppermute(result, "section", [(0, 1)])
    x = jnp.where(section == 0, own, arriving)
    result, saved, kept = forward(1, jnp.ones((1,), jnp.int32), x, weights, kept, 4)

    g_x, grads = backward(1, own, x, weights, saved, kept, 5)
    arriving = lax.ppermute(g_x, "section", [(1, 0)])
    grads, arriving = lax.optimization_barrier((grads, arriving))
    total_one = reduce_grads(1, *grads, 7)
    total_one, arriving = lax.optimization_barrier((total_one, arriving))
    g = jnp.where(section == 1, own, arriving)
    g_x, grads = backward(0, g, x, weights, saved, kept, 6)
    total_zero = reduce_grads(0, *grads, 8)
    q, o, u, d, s = (
        jnp.where(section == 0, zero, one) for zero, one in zip(total_zero, total_one)
    )
    boundary = jnp.where(section == 0, g_x, result)
    return (
        boundary.reshape(1, 1, GROUPS, ROWS, D),
        q[None],
        o[None],
        u[None],
        d[None],
        s[0:1, 0:2, :12],
        s[0:1, 2:8, :12],
        s[1:2, 0, :48],
    )


def solution(mesh):
    rows = P("section", ("seq", "shard"), None)
    columns = P("section", None, ("seq", "shard"))
    ends = P("section", "shard", None, "seq", None)
    hidden = P("section", ("seq", "shard"))
    placed = (ends, rows, rows, rows, rows, columns, columns, hidden)
    return jax.shard_map(per_device, mesh=mesh, in_specs=placed, out_specs=placed, check_vma=False)
```

```python
import functools

import jax
import jax.numpy as jnp
from jax import lax
from jax.experimental import pallas as pl
from jax.experimental.pallas import tpu as pltpu
from jax.sharding import PartitionSpec as P

HEAD = 64
FF = 3072
D = 768
GROUPS = 4
ROWS = 64
TOK = GROUPS * ROWS
SEQ_LEN = 1024
HL = 192
CHUNK = 512
STEPS = FF // CHUNK
EPSILON = 1e-05
MASKED = -1e30
BF = jnp.bfloat16
F32 = jnp.float32
MESH = pl.DeviceIdType.MESH
HBM = pltpu.HBM


def sds(shape, dtype):
    return jax.ShapeDtypeStruct(shape, dtype)


def coords():
    shard = lax.axis_index("shard")
    return {"x": shard // 4, "y": lax.rem(shard, 4), "z": lax.axis_index("seq")}


def peer(c, axis, by):
    moved = dict(c)
    moved[axis] = lax.rem(c[axis] + by, 4)
    return {"section": lax.axis_index("section"), "seq": moved["z"], "shard": moved["x"] * 4 + moved["y"]}


def partner():
    return {
        "section": 1 - lax.axis_index("section"),
        "seq": lax.axis_index("seq"),
        "shard": lax.axis_index("shard"),
    }


def meet(c, axes, steps, with_partner=False):
    barrier = pltpu.get_barrier_semaphore()
    if with_partner:
        pl.semaphore_signal(barrier, inc=1, device_id=partner(), device_id_type=MESH)
    for axis in axes:
        for by in steps:
            pl.semaphore_signal(barrier, inc=1, device_id=peer(c, axis, by), device_id_type=MESH)
    pl.semaphore_wait(barrier, len(axes) * len(steps) + int(with_partner))


class Copies:
    def __init__(self, send, recv):
        self.send, self.recv, self.used, self.sent = send, recv, 0, []

    def remote(self, src, dst, to):
        copy = pltpu.make_async_remote_copy(
            src_ref=src,
            dst_ref=dst,
            send_sem=self.send.at[self.used],
            recv_sem=self.recv.at[self.used],
            device_id=to,
            device_id_type=MESH,
        )
        self.used += 1
        copy.start()
        self.sent.append(copy)
        return copy

    def local(self, src, dst):
        copy = pltpu.make_async_copy(src, dst, self.send.at[self.used])
        self.used += 1
        copy.start()
        return copy

    def drain(self):
        for copy in self.sent:
            copy.wait_send()


class Gather:
    def __init__(self, copies, c, axis, own, dst, half):
        self.copies, self.c, self.axis, self.own, self.dst, self.half = copies, c, axis, own, dst, half

    def first(self):
        a = self.c[self.axis]
        self.right, self.left = peer(self.c, self.axis, 1), peer(self.c, self.axis, 3)
        self.go_right = self.copies.remote(self.own, self.dst(a), self.right)
        self.go_left = self.copies.remote(self.own, self.dst(a), self.left)

    def second(self):
        a = self.c[self.axis]
        before, after = lax.rem(a + 3, 4), lax.rem(a + 1, 4)
        self.go_right.wait_recv()
        self.on_right = self.copies.remote(self.half(before, 0), self.half(before, 0), self.right)
        self.go_left.wait_recv()
        self.on_left = self.copies.remote(self.half(after, 1), self.half(after, 1), self.left)

    def third(self):
        self.on_right.wait_recv()
        self.on_left.wait_recv()


def run_gathers(gathers):
    for g in gathers:
        g.first()
    for g in gathers:
        g.second()


def gather_kernel(q_in, o_in, u_in, d_in, s_in, q, o, u, d, vec, ub, *scratch):
    q_y, o_y, u_y, d_x, s_x, q_b, o_b, u_b, tmp, s, send, recv, turn = scratch
    c = coords()
    x, y, z = c["x"], c["y"], c["z"]
    copies = Copies(send, recv)
    lanes = lambda ref, i, h, n: ref.at[i, :, pl.ds(n * h, n)]
    zero = [
        Gather(copies, c, "y", u_in, lambda i: u_y.at[i], lambda i, h: lanes(u_y, i, h, 1536)),
        Gather(copies, c, "y", q_in, lambda i: q_y.at[i], lambda i, h: q_y.at[i, pl.ds(2 * h, 2)]),
        Gather(copies, c, "y", o_in, lambda i: o_y.at[i], lambda i, h: lanes(o_y, i, h, 384)),
        Gather(copies, c, "x", d_in, lambda i: d_x.at[i], lambda i, h: lanes(d_x, i, h, 384)),
        Gather(copies, c, "x", s_in, lambda i: s_x.at[i], lambda i, h: s_x.at[i, h]),
    ]
    u_y[y] = u_in[...]
    q_y[y] = q_in[...]
    o_y[y] = o_in[...]
    d_x[x] = d_in[...]
    s_x[x] = s_in[...]
    meet(c, ("x", "y", "z"), (1, 3), True)
    run_gathers(zero)
    zero[0].third()
    for k in range(4):
        for i in range(4):
            tmp[12 * i : 12 * i + 12, :] = u_y[i, :, D * k : D * k + D].astype(F32)
        u_b[:, D * k : D * k + D] = tmp[...].astype(BF)
    zero[1].third()
    for p in range(4):
        for i in range(4):
            tmp[12 * i : 12 * i + 12, 0:576] = q_y[i, p].astype(F32)
        q_b[p] = tmp[:, 0:576].astype(BF)
    zero[2].third()
    for i in range(4):
        tmp[12 * i : 12 * i + 12, :] = o_y[i].astype(F32)
    o_b[...] = tmp[...].astype(BF)
    zero[3].third()
    zero[4].third()

    @pl.when(lax.axis_index("section") == 1)
    def _():
        pl.semaphore_wait(turn, 1)

    one = [
        Gather(copies, c, "z", q_b, lambda i: q.at[:, i, x], lambda i, h: q.at[pl.ds(2 * h, 2), i, x]),
        Gather(copies, c, "z", o_b, lambda i: o.at[i, x], lambda i, h: o.at[i, x, :, pl.ds(384 * h, 384)]),
        Gather(copies, c, "x", u_b, lambda i: u.at[z, i], lambda i, h: u.at[z, i, :, pl.ds(1536 * h, 1536)]),
        Gather(copies, c, "z", d_x, lambda i: d.at[i, :, y], lambda i, h: d.at[i, pl.ds(2 * h, 2), y]),
        Gather(copies, c, "z", s_x, lambda i: s.at[i, :, y], lambda i, h: s.at[i, pl.ds(2 * h, 2), y]),
    ]
    own = [
        copies.local(q_b, q.at[:, z, x]),
        copies.local(o_b, o.at[z, x]),
        copies.local(u_b, u.at[z, x]),
        copies.local(d_x, d.at[z, :, y]),
        copies.local(s_x, s.at[z, :, y]),
    ]
    run_gathers(one)
    two = [
        Gather(copies, c, "x", q.at[:, :, x], lambda i: q.at[:, :, i], lambda i, h: q.at[pl.ds(2 * h, 2), :, i]),
        Gather(copies, c, "x", o.at[:, x], lambda i: o.at[:, i], lambda i, h: o.at[pl.ds(2 * h, 2), i]),
        Gather(copies, c, "z", u.at[z], lambda i: u.at[i], lambda i, h: u.at[i, pl.ds(2 * h, 2)]),
        Gather(copies, c, "y", d.at[:, :, y], lambda i: d.at[:, :, i], lambda i, h: d.at[pl.ds(2 * h, 2), :, i]),
        Gather(copies, c, "y", s.at[:, :, y], lambda i: s.at[:, :, i], lambda i, h: s.at[pl.ds(2 * h, 2), :, i]),
    ]
    for k in range(5):
        one[k].third()
        own[k].wait()
        two[k].first()
    for g in two:
        g.second()

    @pl.when(lax.axis_index("section") == 0)
    def _():
        pl.semaphore_signal(turn, inc=1, device_id=partner(), device_id_type=MESH)

    two[4].third()
    for i in range(64):
        here = s.at[i // 16, i // 4 % 4, i % 4]
        vec[:, 12 * i : 12 * i + 12] = here[0, :, 0:12]
        at = 48 * i % CHUNK
        if at + 48 <= CHUNK:
            ub[48 * i // CHUNK, :, at : at + 48] = here[1, 0:1, 0:48]
        else:
            n = CHUNK - at
            ub[48 * i // CHUNK, :, at:CHUNK] = here[1, 0:1, 0:n]
            ub[48 * i // CHUNK + 1, :, 0 : 48 - n] = here[1, 0:1, n:48]
    for g in two[:4]:
        g.third()
    copies.drain()


def gather(qkv, out, up, down, small):
    vmem = pltpu.VMEM
    count = 15 * 4 + 5
    return pl.pallas_call(
        gather_kernel,
        out_shape=(
            sds((4, 4, 4, 48, 576), BF),
            sds((4, 4, 48, D), BF),
            sds((4, 4, 48, FF), BF),
            sds((4, 4, 4, 48, D), BF),
            sds((8, D), F32),
            sds((STEPS, 1, CHUNK), F32),
        ),
        in_specs=[pl.BlockSpec(memory_space=vmem)] * 5,
        out_specs=tuple([pl.BlockSpec(memory_space=HBM)] * 4 + [pl.BlockSpec(memory_space=vmem)] * 2),
        scratch_shapes=[
            vmem((4, 4, 12, 576), BF),
            vmem((4, 12, D), BF),
            vmem((4, 12, FF), BF),
            vmem((4, 48, D), BF),
            vmem((4, 2, 8, 128), F32),
            vmem((4, 48, 576), BF),
            vmem((48, D), BF),
            vmem((48, FF), BF),
            vmem((48, D), F32),
            vmem((4, 4, 4, 2, 8, 128), F32),
            pltpu.SemaphoreType.DMA((count,)),
            pltpu.SemaphoreType.DMA((count,)),
            pltpu.SemaphoreType.REGULAR,
        ],
        compiler_params=pltpu.CompilerParams(
            collective_id=1, has_side_effects=True, vmem_limit_bytes=60 * 1024 * 1024
        ),
    )(qkv, out, up, down, small)


def spread(copies, c, axis, source, target):
    moves = []
    for by in (2, 1, 3):
        there = lax.rem(c[axis] + by, 4)
        moves.append(copies.remote(source(there), target.at[by], peer(c, axis, by)))
    return moves


def arrived(moves):
    for move in moves:
        move.wait_recv()


def add(ref, at):
    total = ref[(0,) + at].astype(F32)
    for k in range(1, 4):
        total += ref[(k,) + at].astype(F32)
    return total


def more(mine, ref, at):
    total = mine.astype(F32)
    for k in range(1, 4):
        total += ref[(k,) + at].astype(F32)
    return total


def reduce_kernel(live, q_in, o_in, u_in, d_in, s_in, o_got, u_got, d_got, q, o, u, d, s, *scratch):
    qa1, qb1, o1, u1, d1, s1, qa2, qb2, o2, u2, d2, s2, tmp, qs, os, us, q3, o3, u3, d3, s3, send, recv = scratch

    def act():
        c = coords()
        x, y, z = c["x"], c["y"], c["z"]
        copies = Copies(send, recv)
        own_d = [copies.local(d_in.at[:, :, y], d1.at[0]), copies.local(d_got.at[pl.ds(1, 3)], d1.at[pl.ds(1, 3)])]
        own_u = [copies.local(u_in.at[:, x], u1.at[0]), copies.local(u_got.at[pl.ds(1, 3)], u1.at[pl.ds(1, 3)])]
        own_qa = copies.local(q_in.at[pl.ds(0, 2), :, x], qa1.at[0])
        own_qb = copies.local(q_in.at[pl.ds(2, 2), z], qb1.at[0])
        own_o = [copies.local(o_in.at[z], o1.at[0]), copies.local(o_got.at[pl.ds(1, 3)], o1.at[pl.ds(1, 3)])]
        own_s = copies.local(s_in.at[:, :, y], s1.at[0])
        meet(c, ("x", "y", "z"), (1, 2, 3))
        one_qa = spread(copies, c, "x", lambda i: q_in.at[pl.ds(0, 2), :, i], qa1)
        one_qb = spread(copies, c, "z", lambda i: q_in.at[pl.ds(2, 2), i], qb1)
        one_s = spread(copies, c, "y", lambda i: s_in.at[:, :, i], s1)

        def add_all(ref, rows, kind):
            @pl.loop(0, rows * 4)
            def _(i):
                at = (i // 4, lax.rem(i, 4))
                ref[(0,) + at] = add(ref, at).astype(kind)

        for copy in own_d:
            copy.wait()
        add_all(d1, 4, BF)
        two_d = spread(copies, c, "x", lambda i: d1.at[0, :, i], d2)
        for copy in own_u:
            copy.wait()

        @pl.loop(0, 4)
        def _(i):
            for k in range(4):
                at = (i, slice(None), pl.ds(D * k, D))
                u1[(0,) + at] = add(u1, at).astype(BF)

        two_u = spread(copies, c, "z", lambda i: u1.at[0, i], u2)
        for copy in own_o:
            copy.wait()

        @pl.loop(0, 4)
        def _(i):
            o1[0, i] = add(o1, (i,)).astype(BF)

        two_o = spread(copies, c, "x", lambda i: o1.at[0, i], o2)
        arrived(one_qa)
        own_qa.wait()
        add_all(qa1, 2, BF)
        two_qa = spread(copies, c, "z", lambda i: qa1.at[0, :, i], qa2)
        arrived(one_qb)
        own_qb.wait()
        add_all(qb1, 2, BF)
        two_qb = spread(copies, c, "x", lambda i: qb1.at[0, :, i], qb2)
        arrived(one_s)
        own_s.wait()
        add_all(s1, 4, F32)
        two_s = spread(copies, c, "z", lambda i: s1.at[0, i], s2)
        arrived(two_d)

        @pl.loop(0, 4)
        def _(i):
            d2[0, i] = more(d1[0, i, x], d2, (i,)).astype(BF)

        three_d = spread(copies, c, "z", lambda i: d2.at[0, i], d3)
        arrived(two_u)
        for k in range(4):
            at = (slice(None), pl.ds(D * k, D))
            tmp[...] = more(u1[(0, z) + at], u2, at)
            for i in range(4):
                us[i, :, D * k : D * k + D] = tmp[12 * i : 12 * i + 12, :].astype(BF)
        three_u = spread(copies, c, "y", lambda i: us.at[i], u3)
        arrived(two_qa)
        arrived(two_qb)
        for p in range(4):
            if p < 2:
                tmp[:, 0:576] = more(qa1[0, p, z], qa2, (p,))
            else:
                tmp[:, 0:576] = more(qb1[0, p - 2, x], qb2, (p - 2,))
            for i in range(4):
                qs[i, p] = tmp[12 * i : 12 * i + 12, 0:576].astype(BF)
        three_q = spread(copies, c, "y", lambda i: qs.at[i], q3)
        arrived(two_o)
        tmp[...] = more(o1[0, x], o2, ())
        for i in range(4):
            os[i] = tmp[12 * i : 12 * i + 12, :].astype(BF)
        three_o = spread(copies, c, "y", lambda i: os.at[i], o3)
        arrived(two_s)

        @pl.loop(0, 4)
        def _(i):
            s2[0, i] = more(s1[0, z, i], s2, (i,))

        three_s = spread(copies, c, "x", lambda i: s2.at[0, i], s3)
        arrived(three_d)
        d[...] = more(d2[0, z], d3, ())
        arrived(three_u)
        u[...] = more(us[y], u3, ())
        arrived(three_q)
        for p in range(4):
            total = more(qs[y, p], q3, (p,))
            for kind in range(3):
                at = D * kind + HL * p
                q[:, at : at + HL] = total[:, HL * kind : HL * kind + HL]
        arrived(three_o)
        o[...] = more(os[y], o3, ())
        arrived(three_s)
        s[...] = more(s2[0, x], s3, ())
        copies.drain()

    pl.when(lax.axis_index("section") == live)(act)


def reduce_grads(live, qkv, out, up, down, small, out_got, up_got, down_got, collective_id):
    vmem = pltpu.VMEM
    count = 9 + 9 + 18 + 15
    return pl.pallas_call(
        functools.partial(reduce_kernel, live),
        out_shape=(
            sds((12, 3 * D), F32),
            sds((12, D), F32),
            sds((12, FF), F32),
            sds((48, D), F32),
            sds((2, 8, 128), F32),
        ),
        in_specs=[pl.BlockSpec(memory_space=HBM)] * 8,
        out_specs=tuple([pl.BlockSpec(memory_space=vmem)] * 5),
        scratch_shapes=[
            vmem((4, 2, 4, 48, 576), BF),
            vmem((4, 2, 4, 48, 576), BF),
            vmem((4, 4, 48, D), BF),
            vmem((4, 4, 48, FF), BF),
            vmem((4, 4, 4, 48, D), BF),
            vmem((4, 4, 4, 2, 8, 128), F32),
            vmem((4, 2, 48, 576), BF),
            vmem((4, 2, 48, 576), BF),
            vmem((4, 48, D), BF),
            vmem((4, 48, FF), BF),
            vmem((4, 4, 48, D), BF),
            vmem((4, 4, 2, 8, 128), F32),
            vmem((48, D), F32),
            vmem((4, 4, 12, 576), BF),
            vmem((4, 12, D), BF),
            vmem((4, 12, FF), BF),
            vmem((4, 4, 12, 576), BF),
            vmem((4, 12, D), BF),
            vmem((4, 12, FF), BF),
            vmem((4, 48, D), BF),
            vmem((4, 2, 8, 128), F32),
            pltpu.SemaphoreType.DMA((count,)),
            pltpu.SemaphoreType.DMA((count,)),
        ],
        compiler_params=pltpu.CompilerParams(
            collective_id=collective_id, has_side_effects=True, vmem_limit_bytes=60 * 1024 * 1024
        ),
    )(qkv, out, up, down, small, out_got, up_got, down_got)


BIG = pltpu.CompilerParams(vmem_limit_bytes=56 * 1024 * 1024)


def dot(a, b):
    return jnp.dot(a, b, preferred_element_type=F32)


def dot_nt(a, b):
    return lax.dot_general(a, b, (((1,), (1,)), ((), ())), preferred_element_type=F32)


def dot_tn(a, b):
    return lax.dot_general(a, b, (((0,), (0,)), ((), ())), preferred_element_type=F32)


def normalize(values):
    centered = values - jnp.mean(values, axis=-1, keepdims=True)
    spread = jnp.mean(centered * centered, axis=-1, keepdims=True)
    inverse = lax.rsqrt(spread + EPSILON)
    return centered * inverse, inverse


def norm_back(e, n, inverse):
    return inverse * (
        e - jnp.mean(e, axis=-1, keepdims=True) - n * jnp.mean(e * n, axis=-1, keepdims=True)
    )


C_ONE = 0.7978845608
C_TWO = 0.7978845608 * 0.044715


def gelu_half(u):
    cube = C_TWO * (u * u)
    return 0.5 + 0.5 * jnp.tanh((C_ONE + cube) * u), cube


def whole(shape):
    zeros = (0,) * len(shape)
    return pl.BlockSpec(shape, lambda *unused: zeros)


def flagged(grid, in_specs, out_specs, scratch):
    return pltpu.PrefetchScalarGridSpec(
        num_scalar_prefetch=1, grid=grid, in_specs=in_specs, out_specs=out_specs, scratch_shapes=scratch
    )


def project_kernel(flag, x_ref, vec_ref, w_ref, out_ref, n_ref, bias_ref):
    step = pl.program_id(0)

    @pl.when((flag[0] == 1) & (step == 0))
    def _():
        n, _ = normalize(x_ref[...].astype(F32))
        n_ref[...] = (n * vec_ref[0:1, :] + vec_ref[2:3, :]).astype(BF)
        bias_ref[...] = jnp.zeros_like(bias_ref)
        for p in range(4):
            bias_ref[p, :, 0:HL] = vec_ref[4:5, HL * p : HL * p + HL]
            bias_ref[p, :, 2 * HL :] = vec_ref[5:6, HL * p : HL * p + HL]

    @pl.when(flag[0] == 1)
    def _():
        out_ref[0] = (dot(n_ref[...], w_ref[0]) + bias_ref[step]).astype(BF)


def project(flag, x, vec, w):
    return pl.pallas_call(
        project_kernel,
        grid_spec=flagged(
            (4,),
            [
                whole((TOK, D)),
                whole((8, D)),
                pl.BlockSpec((1, D, 576), lambda j, f: (j * f[0], 0, 0)),
            ],
            pl.BlockSpec((1, TOK, 576), lambda j, f: (j * f[0], 0, 0)),
            [pltpu.VMEM((TOK, D), BF), pltpu.VMEM((4, 1, 576), F32)],
        ),
        out_shape=sds((4, TOK, 576), BF),
        compiler_params=BIG,
    )(flag, x, vec, w)


BLOCK = 256


def masked(scores, block):
    rows = block * BLOCK + lax.broadcasted_iota(jnp.int32, scores.shape, 0)
    cols = lax.broadcasted_iota(jnp.int32, scores.shape, 1)
    return jnp.where(cols <= rows, scores, MASKED)


def attend_kernel(live, with_previous, p_in, *refs):
    if with_previous:
        refs = refs[3:]
    h_out, lse_out, m_out, h_ref, m_ref, lse_ref, send, recv = refs

    def act():
        c = coords()
        z = c["z"]
        copies = Copies(send, recv)
        own = copies.local(p_in.at[z], h_ref.at[:, z])
        meet(c, ("z",), (1, 2, 3))
        coming, kept = [], []
        for g in range(GROUPS):
            for by in (2, 1, 3):
                to = peer(c, "z", by)
                coming.append(copies.remote(p_in.at[to["seq"], g], h_ref.at[g, z], to))
        own.wait()
        leaving = []
        for g in range(GROUPS):
            arrived(coming[3 * g : 3 * g + 3])
            kept.append(copies.local(h_ref.at[g], h_out.at[g]))
            keys = (g + 1) * BLOCK
            for head in range(3):
                q_at, k_at, v_at = HEAD * head, HL + HEAD * head, 2 * HL + HEAD * head
                q = h_ref[g, :, :, q_at : q_at + HEAD].reshape(BLOCK, HEAD) * jnp.asarray(0.125, BF)
                k = h_ref[0 : g + 1, :, :, k_at : k_at + HEAD].reshape(keys, HEAD)
                v = h_ref[0 : g + 1, :, :, v_at : v_at + HEAD].reshape(keys, HEAD)
                scores = masked(dot_nt(q, k), g)
                top = jnp.max(scores, axis=-1, keepdims=True)
                e = jnp.exp(scores - top)
                total = jnp.sum(e, axis=-1, keepdims=True)
                mixed = (dot(e.astype(BF), v) / total).astype(BF)
                m_ref[g, :, :, q_at : q_at + HEAD] = mixed.reshape(4, ROWS, HEAD)
                lse_ref[g, :, head : head + 1] = top + jnp.log(total)
            for by in (2, 1, 3):
                to = peer(c, "z", by)
                leaving.append(copies.remote(m_ref.at[g, to["seq"]], m_out.at[z, g], to))
            kept.append(copies.local(m_ref.at[g, z], m_out.at[z, g]))
        kept.append(copies.local(lse_ref, lse_out))
        arrived(leaving)
        for copy in kept:
            copy.wait()
        copies.drain()

    pl.when(lax.axis_index("section") == live)(act)


def attend(live, projected, previous, collective_id):
    ins, aliases = (projected,), {}
    if previous is not None:
        ins, aliases = ins + tuple(previous), {1: 0, 2: 1, 3: 2}
    count = 1 + 12 + 4 + 12 + 4 + 1
    return pl.pallas_call(
        functools.partial(attend_kernel, live, previous is not None),
        out_shape=(
            sds((4, 4, ROWS, 576), BF),
            sds((GROUPS, BLOCK, 128), F32),
            sds((4, 4, ROWS, HL), BF),
        ),
        in_specs=[pl.BlockSpec(memory_space=HBM)] * len(ins),
        out_specs=tuple([pl.BlockSpec(memory_space=HBM)] * 3),
        scratch_shapes=[
            pltpu.VMEM((4, 4, ROWS, 576), BF),
            pltpu.VMEM((4, 4, ROWS, HL), BF),
            pltpu.VMEM((GROUPS, BLOCK, 128), F32),
            pltpu.SemaphoreType.DMA((count,)),
            pltpu.SemaphoreType.DMA((count,)),
        ],
        input_output_aliases=aliases,
        compiler_params=pltpu.CompilerParams(
            collective_id=collective_id, has_side_effects=True, vmem_limit_bytes=60 * 1024 * 1024
        ),
    )(*ins)


def attend_back_kernel(
    live, g_in, h_hbm, lse_hbm, o_in, u_in, d_in, x_hbm, mid_hbm, w_hbm, vec_ref, sums_two_ref,
    gw_out, o_out, u_out, d_out, gx_ref, sums_ref,
    h_ref, lse_ref, gh_ref, gs_ref, dk_ref, dv_ref, p_ref, x_ref, mid_ref, w_ref, gw_ref, send, recv,
):
    def act():
        c = coords()
        z = c["z"]
        copies = Copies(send, recv)
        own = [
            copies.local(g_in.at[z], gh_ref.at[:, z]),
            copies.local(h_hbm, h_ref),
            copies.local(lse_hbm, lse_ref),
        ]
        meet(c, ("x", "y", "z"), (1, 2, 3))
        coming, leaving, kept = {}, [], []
        for g in reversed(range(GROUPS)):
            coming[g] = []
            for by in (2, 1, 3):
                to = peer(c, "z", by)
                coming[g].append(copies.remote(g_in.at[to["seq"], g], gh_ref.at[g, z], to))
        weights = spread(copies, c, "y", lambda i: d_in.at[:, :, i], d_out)
        weights += spread(copies, c, "x", lambda i: u_in.at[:, i], u_out)
        weights += spread(copies, c, "z", lambda i: o_in.at[i], o_out)
        later = [copies.local(x_hbm, x_ref), copies.local(mid_hbm, mid_ref), copies.local(w_hbm, w_ref)]
        for copy in own:
            copy.wait()
        for g in reversed(range(GROUPS)):
            arrived(coming[g])
            keys = (g + 1) * BLOCK
            for head in range(3):
                q_at, k_at, v_at = HEAD * head, HL + HEAD * head, 2 * HL + HEAD * head
                q = h_ref[g, :, :, q_at : q_at + HEAD].reshape(BLOCK, HEAD) * jnp.asarray(0.125, BF)
                k = h_ref[0 : g + 1, :, :, k_at : k_at + HEAD].reshape(keys, HEAD)
                v = h_ref[0 : g + 1, :, :, v_at : v_at + HEAD].reshape(keys, HEAD)
                grad = gh_ref[g, :, :, q_at : q_at + HEAD].reshape(BLOCK, HEAD)
                scores = masked(dot_nt(q, k), g)
                p = jnp.exp(scores - lse_ref[g, :, head : head + 1])
                dp = dot_nt(grad, v)
                centre = jnp.sum(p * dp, axis=-1, keepdims=True)
                ds = (p * (dp - centre)).astype(BF)
                dq = (dot(ds, k) * 0.125).astype(BF)
                gs_ref[g, :, :, q_at : q_at + HEAD] = dq.reshape(4, ROWS, HEAD)
                dk = dot_tn(ds, q)
                dv = dot_tn(p.astype(BF), grad)
                if g < GROUPS - 1:
                    dk += dk_ref[head, 0:keys, :]
                    dv += dv_ref[head, 0:keys, :]
                if g > 0:
                    dk_ref[head, 0 : keys - BLOCK, :] = dk[: keys - BLOCK]
                    dv_ref[head, 0 : keys - BLOCK, :] = dv[: keys - BLOCK]
                gs_ref[g, :, :, k_at : k_at + HEAD] = dk[keys - BLOCK :].astype(BF).reshape(4, ROWS, HEAD)
                gs_ref[g, :, :, v_at : v_at + HEAD] = dv[keys - BLOCK :].astype(BF).reshape(4, ROWS, HEAD)
            for by in (2, 1, 3):
                to = peer(c, "z", by)
                leaving.append(copies.remote(gs_ref.at[g, to["seq"]], p_ref.at[z, g], to))
            kept.append(copies.local(gs_ref.at[g, z], p_ref.at[z, g]))
        for copy in later:
            copy.wait()
        n, inverse = normalize(x_ref[...].astype(F32))
        normed = jnp.transpose(n * vec_ref[0:1, :] + vec_ref[2:3, :]).astype(BF)
        arrived(leaving)
        for copy in kept:
            copy.wait()
        back = jnp.zeros((TOK, D), F32)
        written = []
        for p in range(4):
            gp = p_ref[p].reshape(TOK, 576)
            gw_ref[p] = dot(normed, gp).astype(BF)
            written.append(copies.local(gw_ref.at[p], gw_out.at[p]))
            columns = jnp.sum(gp.astype(F32), axis=0, keepdims=True)
            sums_ref[4:5, HL * p : HL * p + HL] = columns[:, 0:HL]
            sums_ref[5:6, HL * p : HL * p + HL] = columns[:, 2 * HL :]
            back += dot_nt(gp, w_ref[p])
        gx_ref[...] = (mid_ref[...] + norm_back(back * vec_ref[0:1, :], n, inverse)).astype(BF)
        sums_ref[0:1, :] = jnp.sum(back * n, axis=0, keepdims=True)
        sums_ref[1:2, :] = sums_two_ref[0:1, :]
        sums_ref[2:3, :] = jnp.sum(back, axis=0, keepdims=True)
        sums_ref[3:4, :] = sums_two_ref[1:2, :]
        sums_ref[6:8, :] = sums_two_ref[2:4, :]
        for copy in written:
            copy.wait()
        arrived(weights)
        copies.drain()

    pl.when(lax.axis_index("section") == live)(act)


def attend_back(live, grads, heads, lse, out, up, down, x, middle_grad, w, vec, sums_two, collective_id):
    vmem = pltpu.VMEM
    count = 3 + 12 + 9 + 3 + 12 + 4 + 4
    return pl.pallas_call(
        functools.partial(attend_back_kernel, live),
        out_shape=(
            sds((4, D, 576), BF),
            sds((4, 4, 48, D), BF),
            sds((4, 4, 48, FF), BF),
            sds((4, 4, 4, 48, D), BF),
            sds((TOK, D), BF),
            sds((8, D), F32),
        ),
        in_specs=[pl.BlockSpec(memory_space=HBM)] * 9 + [pl.BlockSpec(memory_space=vmem)] * 2,
        out_specs=tuple([pl.BlockSpec(memory_space=HBM)] * 4 + [pl.BlockSpec(memory_space=vmem)] * 2),
        scratch_shapes=[
            vmem((4, 4, ROWS, 576), BF),
            vmem((GROUPS, BLOCK, 128), F32),
            vmem((4, 4, ROWS, HL), BF),
            vmem((4, 4, ROWS, 576), BF),
            vmem((3, SEQ_LEN, HEAD), F32),
            vmem((3, SEQ_LEN, HEAD), F32),
            vmem((4, 4, ROWS, 576), BF),
            vmem((TOK, D), BF),
            vmem((TOK, D), F32),
            vmem((4, D, 576), BF),
            vmem((4, D, 576), BF),
            pltpu.SemaphoreType.DMA((count,)),
            pltpu.SemaphoreType.DMA((count,)),
        ],
        compiler_params=pltpu.CompilerParams(
            collective_id=collective_id, has_side_effects=True, vmem_limit_bytes=60 * 1024 * 1024
        ),
    )(grads, heads, lse, out, up, down, x, middle_grad, w, vec, sums_two)


def mlp_kernel(
    flag, x_ref, m_ref, vec_ref, ub_ref, wo_ref, wu_ref, wd_ref, res_ref, mid_ref, raised_ref, n_ref, acc_ref
):
    step = pl.program_id(0)

    @pl.when((flag[0] == 1) & (step == 0))
    def _():
        branch = dot(m_ref[0], wo_ref[0])
        for p in range(1, 4):
            branch += dot(m_ref[p], wo_ref[p])
        middle = x_ref[...].astype(F32) + (branch + vec_ref[6:7, :])
        mid_ref[...] = middle
        n, _ = normalize(middle)
        n_ref[...] = (n * vec_ref[1:2, :] + vec_ref[3:4, :]).astype(BF)
        acc_ref[...] = middle + vec_ref[7:8, :]

    @pl.when(flag[0] == 1)
    def _():
        raised = dot(n_ref[...], wu_ref[...]) + ub_ref[0]
        raised_ref[...] = raised.astype(BF)
        active = (raised * gelu_half(raised)[0]).astype(BF)
        acc_ref[...] += dot(active, wd_ref[...])

    @pl.when((flag[0] == 1) & (step == STEPS - 1))
    def _():
        res_ref[...] = acc_ref[...].astype(BF)


def mlp(flag, x, mixed, vec, ub, wo, wu, wd):
    return pl.pallas_call(
        mlp_kernel,
        grid_spec=flagged(
            (STEPS,),
            [
                whole((TOK, D)),
                whole((4, TOK, HL)),
                whole((8, D)),
                pl.BlockSpec((1, 1, CHUNK), lambda j, f: (j * f[0], 0, 0)),
                whole((4, HL, D)),
                pl.BlockSpec((D, CHUNK), lambda j, f: (0, j * f[0])),
                pl.BlockSpec((CHUNK, D), lambda j, f: (j * f[0], 0)),
            ],
            (whole((TOK, D)), whole((TOK, D)), pl.BlockSpec((TOK, CHUNK), lambda j, f: (0, j * f[0]))),
            [pltpu.VMEM((TOK, D), BF), pltpu.VMEM((TOK, D), F32)],
        ),
        out_shape=(sds((TOK, D), BF), sds((TOK, D), F32), sds((TOK, FF), BF)),
        compiler_params=BIG,
    )(flag, x, mixed, vec, ub, wo, wu, wd)


def mlp_back_kernel(
    g_ref, raised_ref, mid_ref, m_ref, vec_ref, wo_ref, wu_ref, wd_ref,
    gd_ref, gu_ref, go_ref, gm_ref, gmid_ref, sums_ref, gub_ref, n_ref, acc_ref,
):
    step = pl.program_id(0)

    @pl.when(step == 0)
    def _():
        n, _ = normalize(mid_ref[...])
        n_ref[...] = jnp.transpose(n * vec_ref[1:2, :] + vec_ref[3:4, :]).astype(BF)
        acc_ref[...] = jnp.zeros_like(acc_ref)

    g = g_ref[...]
    u = raised_ref[...].astype(F32)
    h, cube = gelu_half(u)
    active = (u * h).astype(BF)
    gd_ref[...] = dot_tn(active, g).astype(BF)
    slope = h + (h * (1.0 - h)) * (u * (2.0 * C_ONE + 6.0 * cube))
    grad_raised = (dot_nt(g, wd_ref[...]) * slope).astype(BF)
    gub_ref[0] = jnp.sum(grad_raised.astype(F32), axis=0, keepdims=True)
    gu_ref[...] = dot(n_ref[...], grad_raised).astype(BF)
    acc_ref[...] += dot_nt(grad_raised, wu_ref[...])

    @pl.when(step == STEPS - 1)
    def _():
        n, inverse = normalize(mid_ref[...])
        back = acc_ref[...]
        g32 = g.astype(F32)
        grad_middle = g32 + norm_back(back * vec_ref[1:2, :], n, inverse)
        gmid_ref[...] = grad_middle
        branch = grad_middle.astype(BF)
        sums_ref[...] = jnp.zeros_like(sums_ref)
        sums_ref[0:1, :] = jnp.sum(back * n, axis=0, keepdims=True)
        sums_ref[1:2, :] = jnp.sum(back, axis=0, keepdims=True)
        sums_ref[2:3, :] = jnp.sum(branch.astype(F32), axis=0, keepdims=True)
        sums_ref[3:4, :] = jnp.sum(g32, axis=0, keepdims=True)
        for p in range(4):
            go_ref[p] = dot_tn(m_ref[p], branch).astype(BF)
            gm_ref[p] = dot_nt(branch, wo_ref[p]).astype(BF)


def mlp_back(g, raised, middle, mixed, vec, wo, wu, wd):
    return pl.pallas_call(
        mlp_back_kernel,
        grid=(STEPS,),
        out_shape=(
            sds((FF, D), BF),
            sds((D, FF), BF),
            sds((4, HL, D), BF),
            sds((4, TOK, HL), BF),
            sds((TOK, D), F32),
            sds((8, D), F32),
            sds((STEPS, 1, CHUNK), F32),
        ),
        in_specs=[
            whole((TOK, D)),
            pl.BlockSpec((TOK, CHUNK), lambda j: (0, j)),
            whole((TOK, D)),
            whole((4, TOK, HL)),
            whole((8, D)),
            whole((4, HL, D)),
            pl.BlockSpec((D, CHUNK), lambda j: (0, j)),
            pl.BlockSpec((CHUNK, D), lambda j: (j, 0)),
        ],
        out_specs=(
            pl.BlockSpec((CHUNK, D), lambda j: (j, 0)),
            pl.BlockSpec((D, CHUNK), lambda j: (0, j)),
            whole((4, HL, D)),
            whole((4, TOK, HL)),
            whole((TOK, D)),
            whole((8, D)),
            pl.BlockSpec((1, 1, CHUNK), lambda j: (j, 0, 0)),
        ),
        scratch_shapes=[pltpu.VMEM((D, TOK), BF), pltpu.VMEM((TOK, D), F32)],
        compiler_params=BIG,
    )(g, raised, middle, mixed, vec, wo, wu, wd)


def tile(rows):
    pads = [(0, 0)] * (rows.ndim - 2) + [(0, 8 - rows.shape[-2]), (0, 128 - rows.shape[-1])]
    return jnp.pad(rows, pads)


def open_weights(raw):
    qkv, out, up, down, vec, ub = raw
    return (
        qkv.reshape(4, D, 576),
        out.reshape(4, HL, D),
        up.reshape(D, FF),
        down.reshape(FF, D),
        vec,
        ub,
    )


def forward(live, flag, x, weights, previous, base_id):
    qkv, wo, wu, wd, vec, ub = weights
    projected = project(flag, x, vec, qkv)
    kept = attend(live, projected.reshape(4, 4, ROWS, 576), previous, base_id)
    mixed = kept[2].reshape(4, TOK, HL)
    result, middle, raised = mlp(flag, x, mixed, vec, ub, wo, wu, wd)
    return result, (mixed, middle, raised), kept


def backward(live, g, x, weights, saved, kept, base_id):
    qkv, wo, wu, wd, vec, ub = weights
    mixed, middle, raised = saved
    g_down, g_up, g_out, g_mixed, g_middle, sums_two, g_ub = mlp_back(
        g, raised, middle, mixed, vec, wo, wu, wd
    )
    g_out = g_out.reshape(4, 4, 48, D)
    g_up = g_up.reshape(4, 4, 48, FF)
    g_down = g_down.reshape(4, 4, 4, 48, D)
    g_qkv, out_got, up_got, down_got, g_x, sums = attend_back(
        live, g_mixed.reshape(4, 4, ROWS, HL), kept[0], kept[1], g_out, g_up, g_down, x, g_middle, qkv, vec, sums_two, base_id
    )
    small = jnp.stack(
        [tile(sums.reshape(8, 64, 12).transpose(1, 0, 2)), tile(g_ub.reshape(64, 1, 48))], axis=1
    )
    grads = (
        g_qkv.reshape(4, 4, 4, 48, 576),
        g_out,
        g_up,
        g_down,
        small.reshape(4, 4, 4, 2, 8, 128),
        out_got,
        up_got,
        down_got,
    )
    return g_x, grads


def per_device(ends, w_qkv, w_out, w_up, w_down, norm_gains, biases, up_bias):
    section = lax.axis_index("section")
    own = ends.reshape(TOK, D)
    qkv = w_qkv[0].reshape(12, 3, 4, HL).transpose(2, 0, 1, 3).reshape(4, 12, 576)
    small = jnp.stack([tile(jnp.concatenate([norm_gains[0], biases[0]])), tile(up_bias)]).astype(F32)
    weights = open_weights(gather(qkv, w_out[0], w_up[0], w_down[0], small))
    flag = (section == 0).astype(jnp.int32).reshape(1)
    result, _, kept = forward(0, flag, own, weights, None, 3)
    arriving = lax.ppermute(result, "section", [(0, 1)])
    x = jnp.where(section == 0, own, arriving)
    result, saved, kept = forward(1, jnp.ones((1,), jnp.int32), x, weights, kept, 4)

    g_x, grads = backward(1, own, x, weights, saved, kept, 5)
    arriving = lax.ppermute(g_x, "section", [(1, 0)])
    grads, arriving = lax.optimization_barrier((grads, arriving))
    total_one = reduce_grads(1, *grads, 7)
    total_one, arriving = lax.optimization_barrier((total_one, arriving))
    g = jnp.where(section == 1, own, arriving)
    g_x, grads = backward(0, g, x, weights, saved, kept, 6)
    total_zero = reduce_grads(0, *grads, 8)
    q, o, u, d, s = (
        jnp.where(section == 0, zero, one) for zero, one in zip(total_zero, total_one)
    )
    boundary = jnp.where(section == 0, g_x, result)
    return (
        boundary.reshape(1, 1, GROUPS, ROWS, D),
        q[None],
        o[None],
        u[None],
        d[None],
        s[0:1, 0:2, :12],
        s[0:1, 2:8, :12],
        s[1:2, 0, :48],
    )


def solution(mesh):
    rows = P("section", ("seq", "shard"), None)
    columns = P("section", None, ("seq", "shard"))
    ends = P("section", "shard", None, "seq", None)
    hidden = P("section", ("seq", "shard"))
    placed = (ends, rows, rows, rows, rows, columns, columns, hidden)
    return jax.shard_map(per_device, mesh=mesh, in_specs=placed, out_specs=placed, check_vma=False)
```

```python
import functools

import jax
import jax.numpy as jnp
from jax import lax
from jax.experimental import pallas as pl
from jax.experimental.pallas import tpu as pltpu
from jax.sharding import PartitionSpec as P

HEAD = 64
FF = 3072
D = 768
GROUPS = 4
ROWS = 64
TOK = GROUPS * ROWS
SEQ_LEN = 1024
HL = 192
CHUNK = 1024
STEPS = FF // CHUNK
EPSILON = 1e-05
MASKED = -1e30
BF = jnp.bfloat16
F32 = jnp.float32
MESH = pl.DeviceIdType.MESH
HBM = pltpu.HBM


def sds(shape, dtype):
    return jax.ShapeDtypeStruct(shape, dtype)


def coords():
    shard = lax.axis_index("shard")
    return {"x": shard // 4, "y": lax.rem(shard, 4), "z": lax.axis_index("seq")}


def peer(c, axis, by):
    moved = dict(c)
    moved[axis] = lax.rem(c[axis] + by, 4)
    return {"section": lax.axis_index("section"), "seq": moved["z"], "shard": moved["x"] * 4 + moved["y"]}


def partner():
    return {
        "section": 1 - lax.axis_index("section"),
        "seq": lax.axis_index("seq"),
        "shard": lax.axis_index("shard"),
    }


def meet(c, axes, steps, with_partner=False):
    barrier = pltpu.get_barrier_semaphore()
    if with_partner:
        pl.semaphore_signal(barrier, inc=1, device_id=partner(), device_id_type=MESH)
    for axis in axes:
        for by in steps:
            pl.semaphore_signal(barrier, inc=1, device_id=peer(c, axis, by), device_id_type=MESH)
    pl.semaphore_wait(barrier, len(axes) * len(steps) + int(with_partner))


class Copies:
    def __init__(self, send, recv):
        self.send, self.recv, self.used, self.sent = send, recv, 0, []

    def remote(self, src, dst, to):
        copy = pltpu.make_async_remote_copy(
            src_ref=src,
            dst_ref=dst,
            send_sem=self.send.at[self.used],
            recv_sem=self.recv.at[self.used],
            device_id=to,
            device_id_type=MESH,
        )
        self.used += 1
        copy.start()
        self.sent.append(copy)
        return copy

    def local(self, src, dst):
        copy = pltpu.make_async_copy(src, dst, self.send.at[self.used])
        self.used += 1
        copy.start()
        return copy

    def drain(self):
        for copy in self.sent:
            copy.wait_send()


class Gather:
    def __init__(self, copies, c, axis, own, dst, half):
        self.copies, self.c, self.axis, self.own, self.dst, self.half = copies, c, axis, own, dst, half

    def first(self):
        a = self.c[self.axis]
        self.right, self.left = peer(self.c, self.axis, 1), peer(self.c, self.axis, 3)
        self.go_right = self.copies.remote(self.own, self.dst(a), self.right)
        self.go_left = self.copies.remote(self.own, self.dst(a), self.left)

    def second(self):
        a = self.c[self.axis]
        before, after = lax.rem(a + 3, 4), lax.rem(a + 1, 4)
        self.go_right.wait_recv()
        self.on_right = self.copies.remote(self.half(before, 0), self.half(before, 0), self.right)
        self.go_left.wait_recv()
        self.on_left = self.copies.remote(self.half(after, 1), self.half(after, 1), self.left)

    def third(self):
        self.on_right.wait_recv()
        self.on_left.wait_recv()


def run_gathers(gathers):
    for g in gathers:
        g.first()
    for g in gathers:
        g.second()


def gather_kernel(q_in, o_in, u_in, d_in, s_in, q, o, u, d, vec, ub, *scratch):
    q_y, o_y, u_y, d_x, s_x, q_b, o_b, u_b, tmp, s, send, recv, turn = scratch
    c = coords()
    x, y, z = c["x"], c["y"], c["z"]
    copies = Copies(send, recv)
    lanes = lambda ref, i, h, n: ref.at[i, :, pl.ds(n * h, n)]
    zero = [
        Gather(copies, c, "y", u_in, lambda i: u_y.at[i], lambda i, h: lanes(u_y, i, h, 1536)),
        Gather(copies, c, "y", q_in, lambda i: q_y.at[i], lambda i, h: q_y.at[i, pl.ds(2 * h, 2)]),
        Gather(copies, c, "y", o_in, lambda i: o_y.at[i], lambda i, h: lanes(o_y, i, h, 384)),
        Gather(copies, c, "x", d_in, lambda i: d_x.at[i], lambda i, h: lanes(d_x, i, h, 384)),
        Gather(copies, c, "x", s_in, lambda i: s_x.at[i], lambda i, h: s_x.at[i, h]),
    ]
    u_y[y] = u_in[...]
    q_y[y] = q_in[...]
    o_y[y] = o_in[...]
    d_x[x] = d_in[...]
    s_x[x] = s_in[...]
    meet(c, ("x", "y", "z"), (1, 3), True)
    run_gathers(zero)
    zero[0].third()
    for k in range(4):
        for i in range(4):
            tmp[12 * i : 12 * i + 12, :] = u_y[i, :, D * k : D * k + D].astype(F32)
        u_b[:, D * k : D * k + D] = tmp[...].astype(BF)
    zero[1].third()
    for p in range(4):
        for i in range(4):
            tmp[12 * i : 12 * i + 12, 0:576] = q_y[i, p].astype(F32)
        q_b[p] = tmp[:, 0:576].astype(BF)
    zero[2].third()
    for i in range(4):
        tmp[12 * i : 12 * i + 12, :] = o_y[i].astype(F32)
    o_b[...] = tmp[...].astype(BF)
    zero[3].third()
    zero[4].third()

    @pl.when(lax.axis_index("section") == 1)
    def _():
        pl.semaphore_wait(turn, 1)

    one = [
        Gather(copies, c, "z", q_b, lambda i: q.at[:, i, x], lambda i, h: q.at[pl.ds(2 * h, 2), i, x]),
        Gather(copies, c, "z", o_b, lambda i: o.at[i, x], lambda i, h: o.at[i, x, :, pl.ds(384 * h, 384)]),
        Gather(copies, c, "x", u_b, lambda i: u.at[z, i], lambda i, h: u.at[z, i, :, pl.ds(1536 * h, 1536)]),
        Gather(copies, c, "z", d_x, lambda i: d.at[i, :, y], lambda i, h: d.at[i, pl.ds(2 * h, 2), y]),
        Gather(copies, c, "z", s_x, lambda i: s.at[i, :, y], lambda i, h: s.at[i, pl.ds(2 * h, 2), y]),
    ]
    own = [
        copies.local(q_b, q.at[:, z, x]),
        copies.local(o_b, o.at[z, x]),
        copies.local(u_b, u.at[z, x]),
        copies.local(d_x, d.at[z, :, y]),
        copies.local(s_x, s.at[z, :, y]),
    ]
    run_gathers(one)
    two = [
        Gather(copies, c, "x", q.at[:, :, x], lambda i: q.at[:, :, i], lambda i, h: q.at[pl.ds(2 * h, 2), :, i]),
        Gather(copies, c, "x", o.at[:, x], lambda i: o.at[:, i], lambda i, h: o.at[pl.ds(2 * h, 2), i]),
        Gather(copies, c, "z", u.at[z], lambda i: u.at[i], lambda i, h: u.at[i, pl.ds(2 * h, 2)]),
        Gather(copies, c, "y", d.at[:, :, y], lambda i: d.at[:, :, i], lambda i, h: d.at[pl.ds(2 * h, 2), :, i]),
        Gather(copies, c, "y", s.at[:, :, y], lambda i: s.at[:, :, i], lambda i, h: s.at[pl.ds(2 * h, 2), :, i]),
    ]
    for k in range(5):
        one[k].third()
        own[k].wait()
        two[k].first()
    for g in two:
        g.second()

    @pl.when(lax.axis_index("section") == 0)
    def _():
        pl.semaphore_signal(turn, inc=1, device_id=partner(), device_id_type=MESH)

    two[4].third()
    for i in range(64):
        here = s.at[i // 16, i // 4 % 4, i % 4]
        vec[:, 12 * i : 12 * i + 12] = here[0, :, 0:12]
        at = 48 * i % CHUNK
        if at + 48 <= CHUNK:
            ub[48 * i // CHUNK, :, at : at + 48] = here[1, 0:1, 0:48]
        else:
            n = CHUNK - at
            ub[48 * i // CHUNK, :, at:CHUNK] = here[1, 0:1, 0:n]
            ub[48 * i // CHUNK + 1, :, 0 : 48 - n] = here[1, 0:1, n:48]
    for g in two[:4]:
        g.third()
    copies.drain()


def gather(qkv, out, up, down, small):
    vmem = pltpu.VMEM
    count = 15 * 4 + 5
    return pl.pallas_call(
        gather_kernel,
        out_shape=(
            sds((4, 4, 4, 48, 576), BF),
            sds((4, 4, 48, D), BF),
            sds((4, 4, 48, FF), BF),
            sds((4, 4, 4, 48, D), BF),
            sds((8, D), F32),
            sds((STEPS, 1, CHUNK), F32),
        ),
        in_specs=[pl.BlockSpec(memory_space=vmem)] * 5,
        out_specs=tuple([pl.BlockSpec(memory_space=HBM)] * 4 + [pl.BlockSpec(memory_space=vmem)] * 2),
        scratch_shapes=[
            vmem((4, 4, 12, 576), BF),
            vmem((4, 12, D), BF),
            vmem((4, 12, FF), BF),
            vmem((4, 48, D), BF),
            vmem((4, 2, 8, 128), F32),
            vmem((4, 48, 576), BF),
            vmem((48, D), BF),
            vmem((48, FF), BF),
            vmem((48, D), F32),
            vmem((4, 4, 4, 2, 8, 128), F32),
            pltpu.SemaphoreType.DMA((count,)),
            pltpu.SemaphoreType.DMA((count,)),
            pltpu.SemaphoreType.REGULAR,
        ],
        compiler_params=pltpu.CompilerParams(
            collective_id=1, has_side_effects=True, vmem_limit_bytes=60 * 1024 * 1024
        ),
    )(qkv, out, up, down, small)


def spread(copies, c, axis, source, target):
    moves = []
    for by in (2, 1, 3):
        there = lax.rem(c[axis] + by, 4)
        moves.append(copies.remote(source(there), target.at[by], peer(c, axis, by)))
    return moves


def arrived(moves):
    for move in moves:
        move.wait_recv()


def add(ref, at):
    total = ref[(0,) + at].astype(F32)
    for k in range(1, 4):
        total += ref[(k,) + at].astype(F32)
    return total


def more(mine, ref, at):
    total = mine.astype(F32)
    for k in range(1, 4):
        total += ref[(k,) + at].astype(F32)
    return total


def reduce_kernel(live, q_in, o_in, u_in, d_in, s_in, o_got, u_got, d_got, q, o, u, d, s, *scratch):
    qa1, qb1, o1, u1, d1, s1, qa2, qb2, o2, u2, d2, s2, tmp, qs, os, us, q3, o3, u3, d3, s3, send, recv = scratch

    def act():
        c = coords()
        x, y, z = c["x"], c["y"], c["z"]
        copies = Copies(send, recv)
        own_d = [copies.local(d_in.at[:, :, y], d1.at[0]), copies.local(d_got.at[pl.ds(1, 3)], d1.at[pl.ds(1, 3)])]
        own_u = [copies.local(u_in.at[:, x], u1.at[0]), copies.local(u_got.at[pl.ds(1, 3)], u1.at[pl.ds(1, 3)])]
        own_qa = copies.local(q_in.at[pl.ds(0, 2), :, x], qa1.at[0])
        own_qb = copies.local(q_in.at[pl.ds(2, 2), z], qb1.at[0])
        own_o = [copies.local(o_in.at[z], o1.at[0]), copies.local(o_got.at[pl.ds(1, 3)], o1.at[pl.ds(1, 3)])]
        own_s = copies.local(s_in.at[:, :, y], s1.at[0])
        meet(c, ("x", "y", "z"), (1, 2, 3))
        one_qa = spread(copies, c, "x", lambda i: q_in.at[pl.ds(0, 2), :, i], qa1)
        one_qb = spread(copies, c, "z", lambda i: q_in.at[pl.ds(2, 2), i], qb1)
        one_s = spread(copies, c, "y", lambda i: s_in.at[:, :, i], s1)

        def add_all(ref, rows, kind):
            @pl.loop(0, rows * 4)
            def _(i):
                at = (i // 4, lax.rem(i, 4))
                ref[(0,) + at] = add(ref, at).astype(kind)

        for copy in own_d:
            copy.wait()
        add_all(d1, 4, BF)
        two_d = spread(copies, c, "x", lambda i: d1.at[0, :, i], d2)
        for copy in own_u:
            copy.wait()

        @pl.loop(0, 4)
        def _(i):
            for k in range(4):
                at = (i, slice(None), pl.ds(D * k, D))
                u1[(0,) + at] = add(u1, at).astype(BF)

        two_u = spread(copies, c, "z", lambda i: u1.at[0, i], u2)
        for copy in own_o:
            copy.wait()

        @pl.loop(0, 4)
        def _(i):
            o1[0, i] = add(o1, (i,)).astype(BF)

        two_o = spread(copies, c, "x", lambda i: o1.at[0, i], o2)
        arrived(one_qa)
        own_qa.wait()
        add_all(qa1, 2, BF)
        two_qa = spread(copies, c, "z", lambda i: qa1.at[0, :, i], qa2)
        arrived(one_qb)
        own_qb.wait()
        add_all(qb1, 2, BF)
        two_qb = spread(copies, c, "x", lambda i: qb1.at[0, :, i], qb2)
        arrived(one_s)
        own_s.wait()
        add_all(s1, 4, F32)
        two_s = spread(copies, c, "z", lambda i: s1.at[0, i], s2)
        arrived(two_d)

        @pl.loop(0, 4)
        def _(i):
            d2[0, i] = more(d1[0, i, x], d2, (i,)).astype(BF)

        three_d = spread(copies, c, "z", lambda i: d2.at[0, i], d3)
        arrived(two_u)
        for k in range(4):
            at = (slice(None), pl.ds(D * k, D))
            tmp[...] = more(u1[(0, z) + at], u2, at)
            for i in range(4):
                us[i, :, D * k : D * k + D] = tmp[12 * i : 12 * i + 12, :].astype(BF)
        three_u = spread(copies, c, "y", lambda i: us.at[i], u3)
        arrived(two_qa)
        arrived(two_qb)
        for p in range(4):
            if p < 2:
                tmp[:, 0:576] = more(qa1[0, p, z], qa2, (p,))
            else:
                tmp[:, 0:576] = more(qb1[0, p - 2, x], qb2, (p - 2,))
            for i in range(4):
                qs[i, p] = tmp[12 * i : 12 * i + 12, 0:576].astype(BF)
        three_q = spread(copies, c, "y", lambda i: qs.at[i], q3)
        arrived(two_o)
        tmp[...] = more(o1[0, x], o2, ())
        for i in range(4):
            os[i] = tmp[12 * i : 12 * i + 12, :].astype(BF)
        three_o = spread(copies, c, "y", lambda i: os.at[i], o3)
        arrived(two_s)

        @pl.loop(0, 4)
        def _(i):
            s2[0, i] = more(s1[0, z, i], s2, (i,))

        three_s = spread(copies, c, "x", lambda i: s2.at[0, i], s3)
        arrived(three_d)
        d[...] = more(d2[0, z], d3, ())
        arrived(three_u)
        u[...] = more(us[y], u3, ())
        arrived(three_q)
        for p in range(4):
            total = more(qs[y, p], q3, (p,))
            for kind in range(3):
                at = D * kind + HL * p
                q[:, at : at + HL] = total[:, HL * kind : HL * kind + HL]
        arrived(three_o)
        o[...] = more(os[y], o3, ())
        arrived(three_s)
        s[...] = more(s2[0, x], s3, ())
        copies.drain()

    pl.when(lax.axis_index("section") == live)(act)


def reduce_grads(live, qkv, out, up, down, small, out_got, up_got, down_got, collective_id):
    vmem = pltpu.VMEM
    count = 9 + 9 + 18 + 15
    return pl.pallas_call(
        functools.partial(reduce_kernel, live),
        out_shape=(
            sds((12, 3 * D), F32),
            sds((12, D), F32),
            sds((12, FF), F32),
            sds((48, D), F32),
            sds((2, 8, 128), F32),
        ),
        in_specs=[pl.BlockSpec(memory_space=HBM)] * 8,
        out_specs=tuple([pl.BlockSpec(memory_space=vmem)] * 5),
        scratch_shapes=[
            vmem((4, 2, 4, 48, 576), BF),
            vmem((4, 2, 4, 48, 576), BF),
            vmem((4, 4, 48, D), BF),
            vmem((4, 4, 48, FF), BF),
            vmem((4, 4, 4, 48, D), BF),
            vmem((4, 4, 4, 2, 8, 128), F32),
            vmem((4, 2, 48, 576), BF),
            vmem((4, 2, 48, 576), BF),
            vmem((4, 48, D), BF),
            vmem((4, 48, FF), BF),
            vmem((4, 4, 48, D), BF),
            vmem((4, 4, 2, 8, 128), F32),
            vmem((48, D), F32),
            vmem((4, 4, 12, 576), BF),
            vmem((4, 12, D), BF),
            vmem((4, 12, FF), BF),
            vmem((4, 4, 12, 576), BF),
            vmem((4, 12, D), BF),
            vmem((4, 12, FF), BF),
            vmem((4, 48, D), BF),
            vmem((4, 2, 8, 128), F32),
            pltpu.SemaphoreType.DMA((count,)),
            pltpu.SemaphoreType.DMA((count,)),
        ],
        compiler_params=pltpu.CompilerParams(
            collective_id=collective_id, has_side_effects=True, vmem_limit_bytes=60 * 1024 * 1024
        ),
    )(qkv, out, up, down, small, out_got, up_got, down_got)


BIG = pltpu.CompilerParams(vmem_limit_bytes=56 * 1024 * 1024)


def dot(a, b):
    return jnp.dot(a, b, preferred_element_type=F32)


def dot_nt(a, b):
    return lax.dot_general(a, b, (((1,), (1,)), ((), ())), preferred_element_type=F32)


def dot_tn(a, b):
    return lax.dot_general(a, b, (((0,), (0,)), ((), ())), preferred_element_type=F32)


def normalize(values):
    centered = values - jnp.mean(values, axis=-1, keepdims=True)
    spread = jnp.mean(centered * centered, axis=-1, keepdims=True)
    inverse = lax.rsqrt(spread + EPSILON)
    return centered * inverse, inverse


def norm_back(e, n, inverse):
    return inverse * (
        e - jnp.mean(e, axis=-1, keepdims=True) - n * jnp.mean(e * n, axis=-1, keepdims=True)
    )


C_ONE = 0.7978845608
C_TWO = 0.7978845608 * 0.044715


def gelu_half(u):
    cube = C_TWO * (u * u)
    return 0.5 + 0.5 * jnp.tanh((C_ONE + cube) * u), cube


def whole(shape):
    zeros = (0,) * len(shape)
    return pl.BlockSpec(shape, lambda *unused: zeros)


def flagged(grid, in_specs, out_specs, scratch):
    return pltpu.PrefetchScalarGridSpec(
        num_scalar_prefetch=1, grid=grid, in_specs=in_specs, out_specs=out_specs, scratch_shapes=scratch
    )


def project_kernel(flag, x_ref, vec_ref, w_ref, out_ref, n_ref, bias_ref):
    step = pl.program_id(0)

    @pl.when((flag[0] == 1) & (step == 0))
    def _():
        n, _ = normalize(x_ref[...].astype(F32))
        n_ref[...] = (n * vec_ref[0:1, :] + vec_ref[2:3, :]).astype(BF)
        bias_ref[...] = jnp.zeros_like(bias_ref)
        for p in range(4):
            bias_ref[p, :, 0:HL] = vec_ref[4:5, HL * p : HL * p + HL]
            bias_ref[p, :, 2 * HL :] = vec_ref[5:6, HL * p : HL * p + HL]

    @pl.when(flag[0] == 1)
    def _():
        out_ref[0] = (dot(n_ref[...], w_ref[0]) + bias_ref[step]).astype(BF)


def project(flag, x, vec, w):
    return pl.pallas_call(
        project_kernel,
        grid_spec=flagged(
            (4,),
            [
                whole((TOK, D)),
                whole((8, D)),
                pl.BlockSpec((1, D, 576), lambda j, f: (j * f[0], 0, 0)),
            ],
            pl.BlockSpec((1, TOK, 576), lambda j, f: (j * f[0], 0, 0)),
            [pltpu.VMEM((TOK, D), BF), pltpu.VMEM((4, 1, 576), F32)],
        ),
        out_shape=sds((4, TOK, 576), BF),
        compiler_params=BIG,
    )(flag, x, vec, w)


BLOCK = 256


def masked(scores, block):
    rows = block * BLOCK + lax.broadcasted_iota(jnp.int32, scores.shape, 0)
    cols = lax.broadcasted_iota(jnp.int32, scores.shape, 1)
    return jnp.where(cols <= rows, scores, MASKED)


def attend_kernel(live, with_previous, p_in, *refs):
    if with_previous:
        refs = refs[3:]
    h_out, lse_out, m_out, h_ref, m_ref, lse_ref, send, recv = refs

    def act():
        c = coords()
        z = c["z"]
        copies = Copies(send, recv)
        own = copies.local(p_in.at[z], h_ref.at[:, z])
        meet(c, ("z",), (1, 2, 3))
        coming, kept = [], []
        for g in range(GROUPS):
            for by in (2, 1, 3):
                to = peer(c, "z", by)
                coming.append(copies.remote(p_in.at[to["seq"], g], h_ref.at[g, z], to))
        own.wait()
        leaving = []
        for g in range(GROUPS):
            arrived(coming[3 * g : 3 * g + 3])
            kept.append(copies.local(h_ref.at[g], h_out.at[g]))
            keys = (g + 1) * BLOCK
            for head in range(3):
                q_at, k_at, v_at = HEAD * head, HL + HEAD * head, 2 * HL + HEAD * head
                q = h_ref[g, :, :, q_at : q_at + HEAD].reshape(BLOCK, HEAD) * jnp.asarray(0.125, BF)
                k = h_ref[0 : g + 1, :, :, k_at : k_at + HEAD].reshape(keys, HEAD)
                v = h_ref[0 : g + 1, :, :, v_at : v_at + HEAD].reshape(keys, HEAD)
                scores = masked(dot_nt(q, k), g)
                top = jnp.max(scores, axis=-1, keepdims=True)
                e = jnp.exp(scores - top)
                total = jnp.sum(e, axis=-1, keepdims=True)
                mixed = (dot(e.astype(BF), v) / total).astype(BF)
                m_ref[g, :, :, q_at : q_at + HEAD] = mixed.reshape(4, ROWS, HEAD)
                lse_ref[g, :, head : head + 1] = top + jnp.log(total)
            for by in (2, 1, 3):
                to = peer(c, "z", by)
                leaving.append(copies.remote(m_ref.at[g, to["seq"]], m_out.at[z, g], to))
            kept.append(copies.local(m_ref.at[g, z], m_out.at[z, g]))
        kept.append(copies.local(lse_ref, lse_out))
        arrived(leaving)
        for copy in kept:
            copy.wait()
        copies.drain()

    pl.when(lax.axis_index("section") == live)(act)


def attend(live, projected, previous, collective_id):
    ins, aliases = (projected,), {}
    if previous is not None:
        ins, aliases = ins + tuple(previous), {1: 0, 2: 1, 3: 2}
    count = 1 + 12 + 4 + 12 + 4 + 1
    return pl.pallas_call(
        functools.partial(attend_kernel, live, previous is not None),
        out_shape=(
            sds((4, 4, ROWS, 576), BF),
            sds((GROUPS, BLOCK, 128), F32),
            sds((4, 4, ROWS, HL), BF),
        ),
        in_specs=[pl.BlockSpec(memory_space=HBM)] * len(ins),
        out_specs=tuple([pl.BlockSpec(memory_space=HBM)] * 3),
        scratch_shapes=[
            pltpu.VMEM((4, 4, ROWS, 576), BF),
            pltpu.VMEM((4, 4, ROWS, HL), BF),
            pltpu.VMEM((GROUPS, BLOCK, 128), F32),
            pltpu.SemaphoreType.DMA((count,)),
            pltpu.SemaphoreType.DMA((count,)),
        ],
        input_output_aliases=aliases,
        compiler_params=pltpu.CompilerParams(
            collective_id=collective_id, has_side_effects=True, vmem_limit_bytes=60 * 1024 * 1024
        ),
    )(*ins)


def attend_back_kernel(
    live, g_in, h_hbm, lse_hbm, o_in, u_in, d_in, x_hbm, mid_hbm, w_hbm, vec_ref, sums_two_ref,
    gw_out, o_out, u_out, d_out, gx_ref, sums_ref,
    h_ref, lse_ref, gh_ref, gs_ref, dk_ref, dv_ref, p_ref, x_ref, mid_ref, w_ref, gw_ref, send, recv,
):
    def act():
        c = coords()
        z = c["z"]
        copies = Copies(send, recv)
        own = [
            copies.local(g_in.at[z], gh_ref.at[:, z]),
            copies.local(h_hbm, h_ref),
            copies.local(lse_hbm, lse_ref),
        ]
        meet(c, ("x", "y", "z"), (1, 2, 3))
        coming, leaving, kept = {}, [], []
        for g in reversed(range(GROUPS)):
            coming[g] = []
            for by in (2, 1, 3):
                to = peer(c, "z", by)
                coming[g].append(copies.remote(g_in.at[to["seq"], g], gh_ref.at[g, z], to))
        weights = spread(copies, c, "y", lambda i: d_in.at[:, :, i], d_out)
        weights += spread(copies, c, "x", lambda i: u_in.at[:, i], u_out)
        weights += spread(copies, c, "z", lambda i: o_in.at[i], o_out)
        later = [copies.local(x_hbm, x_ref), copies.local(mid_hbm, mid_ref), copies.local(w_hbm, w_ref)]
        for copy in own:
            copy.wait()
        for g in reversed(range(GROUPS)):
            arrived(coming[g])
            keys = (g + 1) * BLOCK
            for head in range(3):
                q_at, k_at, v_at = HEAD * head, HL + HEAD * head, 2 * HL + HEAD * head
                q = h_ref[g, :, :, q_at : q_at + HEAD].reshape(BLOCK, HEAD) * jnp.asarray(0.125, BF)
                k = h_ref[0 : g + 1, :, :, k_at : k_at + HEAD].reshape(keys, HEAD)
                v = h_ref[0 : g + 1, :, :, v_at : v_at + HEAD].reshape(keys, HEAD)
                grad = gh_ref[g, :, :, q_at : q_at + HEAD].reshape(BLOCK, HEAD)
                scores = masked(dot_nt(q, k), g)
                p = jnp.exp(scores - lse_ref[g, :, head : head + 1])
                dp = dot_nt(grad, v)
                centre = jnp.sum(p * dp, axis=-1, keepdims=True)
                ds = (p * (dp - centre)).astype(BF)
                dq = (dot(ds, k) * 0.125).astype(BF)
                gs_ref[g, :, :, q_at : q_at + HEAD] = dq.reshape(4, ROWS, HEAD)
                dk = dot_tn(ds, q)
                dv = dot_tn(p.astype(BF), grad)
                if g < GROUPS - 1:
                    dk += dk_ref[head, 0:keys, :]
                    dv += dv_ref[head, 0:keys, :]
                if g > 0:
                    dk_ref[head, 0 : keys - BLOCK, :] = dk[: keys - BLOCK]
                    dv_ref[head, 0 : keys - BLOCK, :] = dv[: keys - BLOCK]
                gs_ref[g, :, :, k_at : k_at + HEAD] = dk[keys - BLOCK :].astype(BF).reshape(4, ROWS, HEAD)
                gs_ref[g, :, :, v_at : v_at + HEAD] = dv[keys - BLOCK :].astype(BF).reshape(4, ROWS, HEAD)
            for by in (2, 1, 3):
                to = peer(c, "z", by)
                leaving.append(copies.remote(gs_ref.at[g, to["seq"]], p_ref.at[z, g], to))
            kept.append(copies.local(gs_ref.at[g, z], p_ref.at[z, g]))
        for copy in later:
            copy.wait()
        n, inverse = normalize(x_ref[...].astype(F32))
        normed = jnp.transpose(n * vec_ref[0:1, :] + vec_ref[2:3, :]).astype(BF)
        arrived(leaving)
        for copy in kept:
            copy.wait()
        back = jnp.zeros((TOK, D), F32)
        written = []
        for p in range(4):
            gp = p_ref[p].reshape(TOK, 576)
            gw_ref[p] = dot(normed, gp).astype(BF)
            written.append(copies.local(gw_ref.at[p], gw_out.at[p]))
            columns = jnp.sum(gp.astype(F32), axis=0, keepdims=True)
            sums_ref[4:5, HL * p : HL * p + HL] = columns[:, 0:HL]
            sums_ref[5:6, HL * p : HL * p + HL] = columns[:, 2 * HL :]
            back += dot_nt(gp, w_ref[p])
        gx_ref[...] = (mid_ref[...] + norm_back(back * vec_ref[0:1, :], n, inverse)).astype(BF)
        sums_ref[0:1, :] = jnp.sum(back * n, axis=0, keepdims=True)
        sums_ref[1:2, :] = sums_two_ref[0:1, :]
        sums_ref[2:3, :] = jnp.sum(back, axis=0, keepdims=True)
        sums_ref[3:4, :] = sums_two_ref[1:2, :]
        sums_ref[6:8, :] = sums_two_ref[2:4, :]
        for copy in written:
            copy.wait()
        arrived(weights)
        copies.drain()

    pl.when(lax.axis_index("section") == live)(act)


def attend_back(live, grads, heads, lse, out, up, down, x, middle_grad, w, vec, sums_two, collective_id):
    vmem = pltpu.VMEM
    count = 3 + 12 + 9 + 3 + 12 + 4 + 4
    return pl.pallas_call(
        functools.partial(attend_back_kernel, live),
        out_shape=(
            sds((4, D, 576), BF),
            sds((4, 4, 48, D), BF),
            sds((4, 4, 48, FF), BF),
            sds((4, 4, 4, 48, D), BF),
            sds((TOK, D), BF),
            sds((8, D), F32),
        ),
        in_specs=[pl.BlockSpec(memory_space=HBM)] * 9 + [pl.BlockSpec(memory_space=vmem)] * 2,
        out_specs=tuple([pl.BlockSpec(memory_space=HBM)] * 4 + [pl.BlockSpec(memory_space=vmem)] * 2),
        scratch_shapes=[
            vmem((4, 4, ROWS, 576), BF),
            vmem((GROUPS, BLOCK, 128), F32),
            vmem((4, 4, ROWS, HL), BF),
            vmem((4, 4, ROWS, 576), BF),
            vmem((3, SEQ_LEN, HEAD), F32),
            vmem((3, SEQ_LEN, HEAD), F32),
            vmem((4, 4, ROWS, 576), BF),
            vmem((TOK, D), BF),
            vmem((TOK, D), F32),
            vmem((4, D, 576), BF),
            vmem((4, D, 576), BF),
            pltpu.SemaphoreType.DMA((count,)),
            pltpu.SemaphoreType.DMA((count,)),
        ],
        compiler_params=pltpu.CompilerParams(
            collective_id=collective_id, has_side_effects=True, vmem_limit_bytes=60 * 1024 * 1024
        ),
    )(grads, heads, lse, out, up, down, x, middle_grad, w, vec, sums_two)


def mlp_kernel(
    flag, x_ref, m_ref, vec_ref, ub_ref, wo_ref, wu_ref, wd_ref, res_ref, mid_ref, raised_ref, n_ref, acc_ref
):
    step = pl.program_id(0)

    @pl.when((flag[0] == 1) & (step == 0))
    def _():
        branch = dot(m_ref[0], wo_ref[0])
        for p in range(1, 4):
            branch += dot(m_ref[p], wo_ref[p])
        middle = x_ref[...].astype(F32) + (branch + vec_ref[6:7, :])
        mid_ref[...] = middle
        n, _ = normalize(middle)
        n_ref[...] = (n * vec_ref[1:2, :] + vec_ref[3:4, :]).astype(BF)
        acc_ref[...] = middle + vec_ref[7:8, :]

    @pl.when(flag[0] == 1)
    def _():
        raised = dot(n_ref[...], wu_ref[...]) + ub_ref[0]
        raised_ref[...] = raised.astype(BF)
        active = (raised * gelu_half(raised)[0]).astype(BF)
        acc_ref[...] += dot(active, wd_ref[...])

    @pl.when((flag[0] == 1) & (step == STEPS - 1))
    def _():
        res_ref[...] = acc_ref[...].astype(BF)


def mlp(flag, x, mixed, vec, ub, wo, wu, wd):
    return pl.pallas_call(
        mlp_kernel,
        grid_spec=flagged(
            (STEPS,),
            [
                whole((TOK, D)),
                whole((4, TOK, HL)),
                whole((8, D)),
                pl.BlockSpec((1, 1, CHUNK), lambda j, f: (j * f[0], 0, 0)),
                whole((4, HL, D)),
                pl.BlockSpec((D, CHUNK), lambda j, f: (0, j * f[0])),
                pl.BlockSpec((CHUNK, D), lambda j, f: (j * f[0], 0)),
            ],
            (whole((TOK, D)), whole((TOK, D)), pl.BlockSpec((TOK, CHUNK), lambda j, f: (0, j * f[0]))),
            [pltpu.VMEM((TOK, D), BF), pltpu.VMEM((TOK, D), F32)],
        ),
        out_shape=(sds((TOK, D), BF), sds((TOK, D), F32), sds((TOK, FF), BF)),
        compiler_params=BIG,
    )(flag, x, mixed, vec, ub, wo, wu, wd)


def mlp_back_kernel(
    g_ref, raised_ref, mid_ref, m_ref, vec_ref, wo_ref, wu_ref, wd_ref,
    gd_ref, gu_ref, go_ref, gm_ref, gmid_ref, sums_ref, gub_ref, n_ref, acc_ref,
):
    step = pl.program_id(0)

    @pl.when(step == 0)
    def _():
        n, _ = normalize(mid_ref[...])
        n_ref[...] = jnp.transpose(n * vec_ref[1:2, :] + vec_ref[3:4, :]).astype(BF)
        acc_ref[...] = jnp.zeros_like(acc_ref)

    g = g_ref[...]
    u = raised_ref[...].astype(F32)
    h, cube = gelu_half(u)
    active = (u * h).astype(BF)
    gd_ref[...] = dot_tn(active, g).astype(BF)
    slope = h + (h * (1.0 - h)) * (u * (2.0 * C_ONE + 6.0 * cube))
    grad_raised = (dot_nt(g, wd_ref[...]) * slope).astype(BF)
    gub_ref[0] = jnp.sum(grad_raised.astype(F32), axis=0, keepdims=True)
    gu_ref[...] = dot(n_ref[...], grad_raised).astype(BF)
    acc_ref[...] += dot_nt(grad_raised, wu_ref[...])

    @pl.when(step == STEPS - 1)
    def _():
        n, inverse = normalize(mid_ref[...])
        back = acc_ref[...]
        g32 = g.astype(F32)
        grad_middle = g32 + norm_back(back * vec_ref[1:2, :], n, inverse)
        gmid_ref[...] = grad_middle
        branch = grad_middle.astype(BF)
        sums_ref[...] = jnp.zeros_like(sums_ref)
        sums_ref[0:1, :] = jnp.sum(back * n, axis=0, keepdims=True)
        sums_ref[1:2, :] = jnp.sum(back, axis=0, keepdims=True)
        sums_ref[2:3, :] = jnp.sum(branch.astype(F32), axis=0, keepdims=True)
        sums_ref[3:4, :] = jnp.sum(g32, axis=0, keepdims=True)
        for p in range(4):
            go_ref[p] = dot_tn(m_ref[p], branch).astype(BF)
            gm_ref[p] = dot_nt(branch, wo_ref[p]).astype(BF)


def mlp_back(g, raised, middle, mixed, vec, wo, wu, wd):
    return pl.pallas_call(
        mlp_back_kernel,
        grid=(STEPS,),
        out_shape=(
            sds((FF, D), BF),
            sds((D, FF), BF),
            sds((4, HL, D), BF),
            sds((4, TOK, HL), BF),
            sds((TOK, D), F32),
            sds((8, D), F32),
            sds((STEPS, 1, CHUNK), F32),
        ),
        in_specs=[
            whole((TOK, D)),
            pl.BlockSpec((TOK, CHUNK), lambda j: (0, j)),
            whole((TOK, D)),
            whole((4, TOK, HL)),
            whole((8, D)),
            whole((4, HL, D)),
            pl.BlockSpec((D, CHUNK), lambda j: (0, j)),
            pl.BlockSpec((CHUNK, D), lambda j: (j, 0)),
        ],
        out_specs=(
            pl.BlockSpec((CHUNK, D), lambda j: (j, 0)),
            pl.BlockSpec((D, CHUNK), lambda j: (0, j)),
            whole((4, HL, D)),
            whole((4, TOK, HL)),
            whole((TOK, D)),
            whole((8, D)),
            pl.BlockSpec((1, 1, CHUNK), lambda j: (j, 0, 0)),
        ),
        scratch_shapes=[pltpu.VMEM((D, TOK), BF), pltpu.VMEM((TOK, D), F32)],
        compiler_params=BIG,
    )(g, raised, middle, mixed, vec, wo, wu, wd)


def tile(rows):
    pads = [(0, 0)] * (rows.ndim - 2) + [(0, 8 - rows.shape[-2]), (0, 128 - rows.shape[-1])]
    return jnp.pad(rows, pads)


def open_weights(raw):
    qkv, out, up, down, vec, ub = raw
    return (
        qkv.reshape(4, D, 576),
        out.reshape(4, HL, D),
        up.reshape(D, FF),
        down.reshape(FF, D),
        vec,
        ub,
    )


def forward(live, flag, x, weights, previous, base_id):
    qkv, wo, wu, wd, vec, ub = weights
    projected = project(flag, x, vec, qkv)
    kept = attend(live, projected.reshape(4, 4, ROWS, 576), previous, base_id)
    mixed = kept[2].reshape(4, TOK, HL)
    result, middle, raised = mlp(flag, x, mixed, vec, ub, wo, wu, wd)
    return result, (mixed, middle, raised), kept


def backward(live, g, x, weights, saved, kept, base_id):
    qkv, wo, wu, wd, vec, ub = weights
    mixed, middle, raised = saved
    g_down, g_up, g_out, g_mixed, g_middle, sums_two, g_ub = mlp_back(
        g, raised, middle, mixed, vec, wo, wu, wd
    )
    g_out = g_out.reshape(4, 4, 48, D)
    g_up = g_up.reshape(4, 4, 48, FF)
    g_down = g_down.reshape(4, 4, 4, 48, D)
    g_qkv, out_got, up_got, down_got, g_x, sums = attend_back(
        live, g_mixed.reshape(4, 4, ROWS, HL), kept[0], kept[1], g_out, g_up, g_down, x, g_middle, qkv, vec, sums_two, base_id
    )
    small = jnp.stack(
        [tile(sums.reshape(8, 64, 12).transpose(1, 0, 2)), tile(g_ub.reshape(64, 1, 48))], axis=1
    )
    grads = (
        g_qkv.reshape(4, 4, 4, 48, 576),
        g_out,
        g_up,
        g_down,
        small.reshape(4, 4, 4, 2, 8, 128),
        out_got,
        up_got,
        down_got,
    )
    return g_x, grads


def per_device(ends, w_qkv, w_out, w_up, w_down, norm_gains, biases, up_bias):
    section = lax.axis_index("section")
    own = ends.reshape(TOK, D)
    qkv = w_qkv[0].reshape(12, 3, 4, HL).transpose(2, 0, 1, 3).reshape(4, 12, 576)
    small = jnp.stack([tile(jnp.concatenate([norm_gains[0], biases[0]])), tile(up_bias)]).astype(F32)
    weights = open_weights(gather(qkv, w_out[0], w_up[0], w_down[0], small))
    flag = (section == 0).astype(jnp.int32).reshape(1)
    result, _, kept = forward(0, flag, own, weights, None, 3)
    arriving = lax.ppermute(result, "section", [(0, 1)])
    x = jnp.where(section == 0, own, arriving)
    result, saved, kept = forward(1, jnp.ones((1,), jnp.int32), x, weights, kept, 4)

    g_x, grads = backward(1, own, x, weights, saved, kept, 5)
    arriving = lax.ppermute(g_x, "section", [(1, 0)])
    grads, arriving = lax.optimization_barrier((grads, arriving))
    total_one = reduce_grads(1, *grads, 7)
    total_one, arriving = lax.optimization_barrier((total_one, arriving))
    g = jnp.where(section == 1, own, arriving)
    g_x, grads = backward(0, g, x, weights, saved, kept, 6)
    total_zero = reduce_grads(0, *grads, 8)
    q, o, u, d, s = (
        jnp.where(section == 0, zero, one) for zero, one in zip(total_zero, total_one)
    )
    boundary = jnp.where(section == 0, g_x, result)
    return (
        boundary.reshape(1, 1, GROUPS, ROWS, D),
        q[None],
        o[None],
        u[None],
        d[None],
        s[0:1, 0:2, :12],
        s[0:1, 2:8, :12],
        s[1:2, 0, :48],
    )


def solution(mesh):
    rows = P("section", ("seq", "shard"), None)
    columns = P("section", None, ("seq", "shard"))
    ends = P("section", "shard", None, "seq", None)
    hidden = P("section", ("seq", "shard"))
    placed = (ends, rows, rows, rows, rows, columns, columns, hidden)
    return jax.shard_map(per_device, mesh=mesh, in_specs=placed, out_specs=placed, check_vma=False)
```
